256 devices in a mesh: graph: 32 (over z, y), feat: 8 (over x, core).
Axes of the slice: x: 4, y: 4, z: 8, core: 2. Of those that a mesh axis runs over, the one named last changes fastest.
Arguments:
- features: bfloat16 [65536, 1024], P('graph', 'feat'), may hold values from -6 to 6
- w_self: bfloat16 [1024, 1024], replicated, may hold values from -0.1875 to 0.1875
- w_neigh: bfloat16 [1024, 1024], replicated, may hold values from -0.1875 to 0.1875
- adjacency: bfloat16 [4096, 128, 128], P('graph'), may hold values from 0 to 1.5, as said below
- block_source: int32 [4096], P('graph'), may hold values from 0 to 15
- block_to_slot: int32 [4096], P('graph'), may hold values from 0 to 63
- send_rows: int32 [32, 32, 256], P('graph'), may hold values from 0 to 2047
- send_counts: int32 [32, 32], P('graph'), may hold values from 64 to 256, as said below
- degree: int32 [65536], P('graph'), may hold values from 8 to 32
- cotangent: bfloat16 [65536, 1024], P('graph', 'feat'), may hold values from -6 to 6
Outputs:
- hidden_out: bfloat16 [65536, 1024], P('graph', 'feat')
- grad_features: bfloat16 [65536, 1024], P('graph', 'feat')
- grad_self: float32 [1024, 1024], P('feat')
- grad_neigh: float32 [1024, 1024], P('feat')
The draws below stay inside these ranges and needn't reach their ends.
Inputs may be any that keep to these rules, and one draw needn't show every extreme that they name: Slots 0 to send_counts[p, q] - 1 from p to q are live; in every draw some partition receives 256 live slots from every partition. `adjacency`: edge weights; a block is mostly zeros.
All inputs are finite; a program needn't handle non-finite values.
Results may differ from the reference program's by a relative error of at most 0.0066.
Values may be sent and summed in bfloat16 or wider, within the bound.
No kernel may reach another device: no remote copies, remote signals or barrier semaphores. Data moves between devices by JAX's collectives and lax.ppermute only.
A program may use at most 128 MiB of HBM per device.

```python
import jax
import jax.numpy as jnp
from jax import lax

D = 1024
NODE_DEV = 2048
BLK = 128
PARTITIONS = 32
NODES = 65536
CAP = 256
SLOT_BLOCK_COUNT = 64
NBLK = 128
ADJACENCY_BLOCKS = 4096


def draw_adjacency(key, part):
    key_mask = jax.random.fold_in(key, 11)
    key_value = jax.random.fold_in(key, 12)
    shape = (ADJACENCY_BLOCKS, BLK, BLK)
    present = jax.random.bernoulli(key_mask, 0.3, shape)
    values = jax.random.uniform(key_value, shape, jnp.float32, 0.5, 1.5)
    return jnp.where(present, values, jnp.float32(0.0)).astype(jnp.bfloat16)


def draw_send_counts(key, part):
    part_count = NODES // NODE_DEV
    key_counts = jax.random.fold_in(key, 21)
    key_full = jax.random.fold_in(key, 22)
    counts = jax.random.randint(key_counts, (part_count, part_count), CAP // 4, CAP + 1, dtype=jnp.int32)
    full_owner = jax.random.randint(key_full, (), 0, part_count, dtype=jnp.int32)
    column = jnp.arange(part_count, dtype=jnp.int32)[None, :] == full_owner
    return jnp.where(column, jnp.int32(CAP), counts).astype(jnp.int32)


def with_ends(drawn, stream_key, low, high):
    spot = [jax.random.randint(jax.random.fold_in(stream_key, axis), (), 0, length) for axis, length in enumerate(drawn.shape)]
    longest = drawn.shape.index(max(drawn.shape))
    neighbour = spot[:longest] + [(spot[longest] + 1) % drawn.shape[longest]] + spot[longest + 1:]
    return drawn.at[tuple(spot)].set(low).at[tuple(neighbour)].set(high)


def level_of(rng, dims, cuts, low, top_value):
    loudness, own = 1.0, jax.random.fold_in(rng, 6)
    for axis_at, shards_of in cuts:
        heights = jnp.exp(jax.random.uniform(jax.random.fold_in(own, axis_at), (shards_of,), jnp.float32, low / len(cuts), top_value / len(cuts)))
        loudness = loudness * jnp.repeat(heights, dims[axis_at] // shards_of).reshape([-1 if axis == axis_at else 1 for axis in range(len(dims))])
    return loudness


def noise(rng, shape, deviation, bound, pieces=(), kind=jnp.bfloat16):
    result = jax.random.normal(rng, shape, jnp.float32) * deviation
    if len(pieces) > 0:
        result = level_of(rng, shape, pieces, -0.22, 0.18) * result
    return jnp.clip(result, min=-bound, max=bound).astype(kind)


def setup_inputs(seed: int = 0) -> dict:
    arg_keys = jax.random.split(jax.random.key(seed), 11)
    return {
        "features": noise(arg_keys[0], (NODES, D), 1.0, 6.0, ((0, 32), (1, 8))),
        "w_self": noise(arg_keys[1], (D, D), D ** -0.5, 0.1875),
        "w_neigh": noise(arg_keys[2], (D, D), D ** -0.5, 0.1875),
        "adjacency": draw_adjacency(jax.random.fold_in(arg_keys[10], 71), 0),
        "block_source": with_ends(jax.random.randint(arg_keys[4], (ADJACENCY_BLOCKS,), 0, NODE_DEV // BLK), jax.random.fold_in(arg_keys[4], 1), 0, (NODE_DEV // BLK) - 1).astype(jnp.int32),
        "block_to_slot": with_ends(jax.random.randint(arg_keys[5], (ADJACENCY_BLOCKS,), 0, SLOT_BLOCK_COUNT), jax.random.fold_in(arg_keys[5], 1), 0, SLOT_BLOCK_COUNT - 1).astype(jnp.int32),
        "send_rows": with_ends(jax.random.randint(arg_keys[6], (PARTITIONS, PARTITIONS, CAP), 0, NODE_DEV), jax.random.fold_in(arg_keys[6], 1), 0, NODE_DEV - 1).astype(jnp.int32),
        "send_counts": draw_send_counts(jax.random.fold_in(arg_keys[10], 71), 0),
        "degree": with_ends(jax.random.randint(arg_keys[8], (NODES,), 8, 33), jax.random.fold_in(arg_keys[8], 1), 8, 32).astype(jnp.int32),
        "cotangent": noise(arg_keys[9], (NODES, D), 1.0, 6.0, ((0, 32), (1, 8))),
    }


def silu_slope(values):
    sig = jax.nn.sigmoid(values)
    return sig * (1.0 + values * (1.0 - sig))


def reference(features, w_self, w_neigh, adjacency, block_source, block_to_slot, send_rows, send_counts, degree, cotangent):
    part_count = PARTITIONS
    source_count = NODE_DEV // BLK
    slot_total = SLOT_BLOCK_COUNT
    feat_blocks = features.reshape(part_count, source_count, BLK, D)
    adj_parts = adjacency.reshape(part_count, NBLK, BLK, BLK)
    source_parts = block_source.reshape(part_count, NBLK).astype(jnp.int32)
    slot_parts = block_to_slot.reshape(part_count, NBLK).astype(jnp.int32)
    slot_position = jnp.arange(CAP, dtype=jnp.int32)
    is_live = slot_position[None, None, :] < send_counts[:, :, None]
    owner_base = (jnp.arange(part_count, dtype=jnp.int32) * NODE_DEV)[None, :, None]
    targets = jnp.where(is_live, owner_base + send_rows.astype(jnp.int32), NODES).astype(jnp.int32)

    def forward_step(running, inputs):
        own_blocks, adj_here, source_local, slot_here, target_local, live_here = inputs
        picked = own_blocks[source_local]
        prods = jnp.einsum("kij,kjd->kid", adj_here.astype(jnp.float32), picked.astype(jnp.float32))
        slot_sums = jax.ops.segment_sum(prods, slot_here, num_segments=slot_total)
        slot_sums = slot_sums.reshape(part_count, CAP, D)
        partial_rows = jnp.where(live_here[:, :, None], slot_sums, 0.0).astype(jnp.bfloat16)
        running = running.at[target_local.reshape(-1)].add(partial_rows.reshape(-1, D).astype(jnp.float32), mode="drop")
        return running, None

    neighbor_sum, unused = lax.scan(forward_step, jnp.zeros((NODES, D), jnp.float32),
                                    (feat_blocks, adj_parts, source_parts, slot_parts, targets, is_live))
    degrees = degree.astype(jnp.float32)[:, None]
    neighbor_mean = (neighbor_sum / degrees).astype(jnp.bfloat16)
    pre_act = jnp.dot(features, w_self, preferred_element_type=jnp.float32) + jnp.dot(neighbor_mean, w_neigh, preferred_element_type=jnp.float32)
    hidden_out = jax.nn.silu(pre_act).astype(jnp.bfloat16)
    grad_pre = (cotangent.astype(jnp.float32) * silu_slope(pre_act)).astype(jnp.bfloat16)
    grad_self = jnp.dot(features.T, grad_pre, preferred_element_type=jnp.float32)
    grad_neigh = jnp.dot(neighbor_mean.T, grad_pre, preferred_element_type=jnp.float32)
    self_part = jnp.dot(grad_pre, w_self.T, preferred_element_type=jnp.float32)
    back_rows = (jnp.dot(grad_pre, w_neigh.T, preferred_element_type=jnp.float32) / degrees).astype(jnp.bfloat16)
    back_padded = jnp.concatenate([back_rows, jnp.zeros((1, D), jnp.bfloat16)], axis=0)

    def backward_step(inputs):
        adj_here, source_local, slot_here, target_local = inputs
        returned = back_padded[target_local].reshape(slot_total, BLK, D)
        chosen = returned[slot_here]
        contrib = jnp.einsum("kij,kid->kjd", adj_here.astype(jnp.float32), chosen.astype(jnp.float32))
        summed = jax.ops.segment_sum(contrib, source_local, num_segments=source_count)
        return summed.reshape(NODE_DEV, D)

    neigh_part = lax.map(backward_step, (adj_parts, source_parts, slot_parts, targets))
    grad_features = (self_part + neigh_part.reshape(NODES, D)).astype(jnp.bfloat16)
    return (hidden_out, grad_features, grad_self, grad_neigh)
```

```python
import functools

import jax
import jax.numpy as jnp
from jax import lax
from jax.experimental import pallas as pl
from jax.experimental.pallas import tpu as pltpu
from jax.sharding import Mesh, PartitionSpec as P

BF16 = jnp.bfloat16
F32 = jnp.float32
VMEM_BYTES = 48 * 1024 * 1024


def params(axes=0):
    return pltpu.CompilerParams(
        dimension_semantics=("arbitrary",) * axes if axes else None, vmem_limit_bytes=VMEM_BYTES
    )


def full_spec(shape):
    return pl.BlockSpec(shape, lambda *unused: (0,) * len(shape))


def forward_blocks_kernel(
    source_ref, slot_ref, count_ref, rows_ref, feat_ref, adj_ref, low_ref, high_ref, sums_ref
):
    step = pl.program_id(0)
    chunk, blk, _ = adj_ref.shape
    parts = low_ref.shape[0]
    cols = feat_ref.shape[1]

    @pl.when(step == 0)
    def _():
        sums_ref[...] = jnp.zeros(sums_ref.shape, F32)

    for item in range(chunk):
        block = step * chunk + item
        start = pl.multiple_of(source_ref[block] * blk, blk)
        product = jnp.dot(
            adj_ref[item], feat_ref[pl.ds(start, blk), :], preferred_element_type=F32
        )
        sums_ref[slot_ref[block]] += product

    @pl.when(step == pl.num_programs(0) - 1)
    def _():
        slot_row = lax.broadcasted_iota(jnp.int32, (blk, cols), 0)
        lane = lax.broadcasted_iota(jnp.int32, (1, 2 * blk), 1)
        tile_row = lax.broadcasted_iota(jnp.int32, (16, blk), 0)

        def emit(part, carry):
            count = count_ref[part]
            low = jnp.where(slot_row < count, sums_ref[2 * part], 0.0)
            high = jnp.where(slot_row + blk < count, sums_ref[2 * part + 1], 0.0)
            low_ref[part, 0:blk, :] = low.astype(BF16)
            high_ref[part] = high.astype(BF16)
            ids = rows_ref[pl.ds(part, 1), :]
            live = lane < count
            fine = jnp.where(live, ids & (blk - 1), -1).astype(F32)
            coarse = jnp.where(live, ids >> 7, -1).astype(F32)
            tile = jnp.where(tile_row == 0, fine[:, :blk], 0.0)
            tile = jnp.where(tile_row == 1, fine[:, blk:], tile)
            tile = jnp.where(tile_row == 2, coarse[:, :blk], tile)
            tile = jnp.where(tile_row == 3, coarse[:, blk:], tile)
            low_ref[part, blk : blk + 16, :] = tile.astype(BF16)
            return carry

        lax.fori_loop(0, parts, emit, 0)


def forward_blocks(block_source, block_to_slot, counts, rows, features, adjacency):
    blocks, blk, _ = adjacency.shape
    nodes, cols = features.shape
    parts, cap = rows.shape
    chunk = 16
    return pl.pallas_call(
        forward_blocks_kernel,
        grid_spec=pltpu.PrefetchScalarGridSpec(
            num_scalar_prefetch=3,
            grid=(blocks // chunk,),
            in_specs=[
                full_spec((parts, cap)),
                full_spec((nodes, cols)),
                pl.BlockSpec((chunk, blk, blk), lambda i, *unused: (i, 0, 0)),
            ],
            out_specs=[full_spec((parts, blk + 16, cols)), full_spec((parts, blk, cols))],
            scratch_shapes=[pltpu.VMEM((parts * cap // blk, blk, cols), F32)],
        ),
        out_shape=[
            jax.ShapeDtypeStruct((parts, blk + 16, cols), BF16),
            jax.ShapeDtypeStruct((parts, blk, cols), BF16),
        ],
        compiler_params=params(1),
        name="forward_blocks",
    )(block_source, block_to_slot, counts, rows, features, adjacency)


def scatter_body(half, ids_ref, rows_ref, hot_ref, acc_ref, group):
    nodes, cols = acc_ref.shape
    blk = 128
    node_row = lax.broadcasted_iota(jnp.int32, (blk, blk), 0).astype(F32)
    for part in range(group):
        tile = ids_ref[part].astype(F32)
        fine = tile[half : half + 1, :]
        coarse = tile[2 + half : 3 + half, :]
        hot = jnp.where(node_row == fine, 1.0, 0.0).astype(BF16)
        for block in range(nodes // blk):
            keep = jnp.where(coarse == float(block), 1.0, 0.0).astype(BF16)
            hot_ref[block * blk : (block + 1) * blk, part * blk : (part + 1) * blk] = hot * keep
    rows = rows_ref[...].reshape(group * blk, cols)
    acc_ref[...] += jnp.dot(hot_ref[...], rows, preferred_element_type=F32)


def scatter_low_kernel(payload_ids_ref, rows_ref, sum_ref, hot_ref):
    @pl.when(pl.program_id(0) == 0)
    def _():
        sum_ref[...] = jnp.zeros(sum_ref.shape, F32)

    scatter_body(0, payload_ids_ref, rows_ref, hot_ref, sum_ref, rows_ref.shape[0])


def scatter_high_kernel(payload_ids_ref, rows_ref, init_ref, degree_ref, mean_ref, hot_ref, acc_ref):
    @pl.when(pl.program_id(0) == 0)
    def _():
        acc_ref[...] = init_ref[...]

    scatter_body(1, payload_ids_ref, rows_ref, hot_ref, acc_ref, rows_ref.shape[0])

    @pl.when(pl.program_id(0) == pl.num_programs(0) - 1)
    def _():
        mean_ref[...] = (acc_ref[...] / degree_ref[...]).astype(BF16)


def scatter_low(low, nodes):
    parts, height, cols = low.shape
    group, blk = 8, 128
    return pl.pallas_call(
        scatter_low_kernel,
        grid=(parts // group,),
        in_specs=[
            pl.BlockSpec((group, 16, cols), lambda i: (i, blk // 16, 0)),
            pl.BlockSpec((group, blk, cols), lambda i: (i, 0, 0)),
        ],
        out_specs=full_spec((nodes, cols)),
        out_shape=jax.ShapeDtypeStruct((nodes, cols), F32),
        scratch_shapes=[pltpu.VMEM((nodes, group * blk), BF16)],
        compiler_params=params(1),
        name="scatter_low",
    )(low, low)


def scatter_high(low, high, partial_sum, degrees):
    parts, blk, cols = high.shape
    nodes = partial_sum.shape[0]
    group = 8
    return pl.pallas_call(
        scatter_high_kernel,
        grid=(parts // group,),
        in_specs=[
            pl.BlockSpec((group, 16, cols), lambda i: (i, blk // 16, 0)),
            pl.BlockSpec((group, blk, cols), lambda i: (i, 0, 0)),
            full_spec((nodes, cols)),
            full_spec((nodes, 1)),
        ],
        out_specs=full_spec((nodes, cols)),
        out_shape=jax.ShapeDtypeStruct((nodes, cols), BF16),
        scratch_shapes=[
            pltpu.VMEM((nodes, group * blk), BF16),
            pltpu.VMEM((nodes, cols), F32),
        ],
        compiler_params=params(1),
        name="scatter_high",
    )(low, high, partial_sum, degrees)


def gather_kernel(half, fine_ref, coarse_ref, back_ref, out_ref, hot_ref):
    group, blk, cols = out_ref.shape
    nodes = back_ref.shape[0]
    lane = lax.broadcasted_iota(jnp.int32, (blk, blk), 1).astype(F32)
    for part in range(group):
        fine = jnp.broadcast_to(fine_ref[0, :, part : part + 1], (blk, blk))
        coarse = jnp.broadcast_to(coarse_ref[0, :, part : part + 1], (blk, blk))
        hot = jnp.where(lane == fine, 1.0, 0.0)
        for block in range(nodes // blk):
            value = jnp.where(coarse == float(block), hot, 0.0).astype(BF16)
            hot_ref[part * blk : (part + 1) * blk, block * blk : (block + 1) * blk] = value
    picked = jnp.dot(hot_ref[...], back_ref[...], preferred_element_type=F32)
    out_ref[...] = picked.astype(BF16).reshape(group, blk, cols)


def gather_rows(half, fine, coarse, back):
    steps, blk, group = fine.shape
    nodes, cols = back.shape
    return pl.pallas_call(
        functools.partial(gather_kernel, half),
        grid=(steps,),
        in_specs=[
            pl.BlockSpec((1, blk, group), lambda i: (i, 0, 0)),
            pl.BlockSpec((1, blk, group), lambda i: (i, 0, 0)),
            full_spec((nodes, cols)),
        ],
        out_specs=pl.BlockSpec((group, blk, cols), lambda i: (i, 0, 0)),
        out_shape=jax.ShapeDtypeStruct((steps * group, blk, cols), BF16),
        scratch_shapes=[pltpu.VMEM((group * blk, nodes), BF16)],
        compiler_params=params(1),
        name="gather_rows",
    )(fine, coarse, back)


def own_term_kernel(feat_ref, weight_ref, out_ref):
    pieces = feat_ref.shape[0]
    rows = jnp.concatenate([feat_ref[piece] for piece in range(pieces)], axis=1)
    out_ref[...] = jnp.dot(rows, weight_ref[...], preferred_element_type=F32)


def own_term(feat_pieces, w_self):
    pieces, rows, cols = feat_pieces.shape
    wide = w_self.shape[1]
    tile = 256
    return pl.pallas_call(
        own_term_kernel,
        grid=(wide // tile,),
        in_specs=[
            full_spec((pieces, rows, cols)),
            pl.BlockSpec((pieces * cols, tile), lambda i: (0, i)),
        ],
        out_specs=pl.BlockSpec((rows, tile), lambda i: (0, i)),
        out_shape=jax.ShapeDtypeStruct((rows, wide), F32),
        compiler_params=params(1),
        name="own_term",
    )(feat_pieces, w_self)


def dense_kernel(mean_ref, own_ref, cot_ref, weight_ref, degree_ref, back_ref, hidden_ref, grad_ref, acc_ref):
    step = pl.program_id(0)
    pieces, rows, cols = mean_ref.shape
    tile = weight_ref.shape[1]
    mean = jnp.concatenate([mean_ref[piece] for piece in range(pieces)], axis=1)
    pre_act = own_ref[...] + jnp.dot(mean, weight_ref[...], preferred_element_type=F32)
    sig = jax.nn.sigmoid(pre_act)
    cot = jnp.concatenate([cot_ref[piece] for piece in range(cot_ref.shape[0])], axis=1)
    slope = sig * (1.0 + pre_act * (1.0 - sig))
    grad = (cot.astype(F32) * slope).astype(BF16)
    hidden = (pre_act * sig).astype(BF16)
    grad_ref[...] = grad
    for piece in range(tile // cols):
        hidden_ref[piece] = hidden[:, piece * cols : (piece + 1) * cols]
    update = lax.dot_general(
        grad, weight_ref[...], (((1,), (1,)), ((), ())), preferred_element_type=F32
    )

    @pl.when(step == 0)
    def _():
        acc_ref[...] = update

    @pl.when(step > 0)
    def _():
        acc_ref[...] += update

    @pl.when(step == pl.num_programs(0) - 1)
    def _():
        back = (acc_ref[...] / degree_ref[...]).astype(BF16)
        for piece in range(pieces):
            back_ref[piece] = back[:, piece * cols : (piece + 1) * cols]


def dense(mean_pieces, own, cot_pieces, w_neigh, degree_rows):
    pieces, rows, cols = mean_pieces.shape
    wide = w_neigh.shape[1]
    tile = 256
    per = tile // cols
    return pl.pallas_call(
        dense_kernel,
        grid=(wide // tile,),
        in_specs=[
            full_spec((pieces, rows, cols)),
            pl.BlockSpec((rows, tile), lambda i: (0, i)),
            pl.BlockSpec((per, rows, cols), lambda i: (i, 0, 0)),
            pl.BlockSpec((pieces * cols, tile), lambda i: (0, i)),
            full_spec((rows, 1)),
        ],
        out_specs=[
            full_spec((pieces, rows, cols)),
            pl.BlockSpec((per, rows, cols), lambda i: (i, 0, 0)),
            pl.BlockSpec((rows, tile), lambda i: (0, i)),
        ],
        out_shape=[
            jax.ShapeDtypeStruct((pieces, rows, cols), BF16),
            jax.ShapeDtypeStruct((pieces, rows, cols), BF16),
            jax.ShapeDtypeStruct((rows, wide), BF16),
        ],
        scratch_shapes=[pltpu.VMEM((rows, wide), F32)],
        compiler_params=params(1),
        name="dense",
    )(mean_pieces, own, cot_pieces, w_neigh, degree_rows)


def backward_blocks_kernel(
    source_ref, slot_ref, low_ref, high_ref, adj_ref, self_ref, out_ref, both_ref, acc_ref
):
    step = pl.program_id(0)
    chunk, blk, _ = adj_ref.shape
    parts = low_ref.shape[0]

    @pl.when(step == 0)
    def _():
        acc_ref[...] = self_ref[...]
        for part in range(parts):
            both_ref[2 * part] = low_ref[part]
            both_ref[2 * part + 1] = high_ref[part]

    for item in range(chunk):
        block = step * chunk + item
        start = pl.multiple_of(source_ref[block] * blk, blk)
        product = jnp.dot(
            adj_ref[item], both_ref[slot_ref[block]], preferred_element_type=F32
        )
        acc_ref[pl.ds(start, blk), :] += product

    @pl.when(step == pl.num_programs(0) - 1)
    def _():
        out_ref[...] = acc_ref[...].astype(BF16)


def backward_blocks(block_source, block_to_slot, low, high, adjacency_t, self_grad):
    blocks, blk, _ = adjacency_t.shape
    nodes, cols = self_grad.shape
    parts = low.shape[0]
    chunk = 16
    return pl.pallas_call(
        backward_blocks_kernel,
        grid_spec=pltpu.PrefetchScalarGridSpec(
            num_scalar_prefetch=2,
            grid=(blocks // chunk,),
            in_specs=[
                full_spec((parts, blk, cols)),
                full_spec((parts, blk, cols)),
                pl.BlockSpec((chunk, blk, blk), lambda i, *unused: (i, 0, 0)),
                full_spec((nodes, cols)),
            ],
            out_specs=full_spec((nodes, cols)),
            scratch_shapes=[
                pltpu.VMEM((2 * parts, blk, cols), BF16),
                pltpu.VMEM((nodes, cols), F32),
            ],
        ),
        out_shape=jax.ShapeDtypeStruct((nodes, cols), BF16),
        compiler_params=params(1),
        name="backward_blocks",
    )(block_source, block_to_slot, low, high, adjacency_t, self_grad)


def swap(value, axis):
    return lax.all_to_all(value, axis, split_axis=0, concat_axis=0, tiled=True)


def after(value, *others):
    return lax.optimization_barrier((value, *others))[0]


def reduce_over_graph(partial):
    rows, wide = partial.shape
    over_y, over_z = lax.axis_size("y"), lax.axis_size("z")
    chunk = rows // over_y
    part = swap(partial.reshape(over_y, chunk, wide), "y").astype(F32).sum(0).astype(BF16)
    part = swap(part.reshape(over_z, chunk // over_z, wide), "z").astype(F32).sum(0).astype(BF16)
    part = swap(jnp.broadcast_to(part[None], (over_z, *part.shape)), "z").reshape(chunk, wide)
    part = swap(jnp.broadcast_to(part[None], (over_y, *part.shape)), "y").reshape(rows, wide)
    return part.astype(F32)


def on_device(
    features,
    w_self,
    w_neigh,
    adjacency,
    block_source,
    block_to_slot,
    send_rows,
    send_counts,
    degree,
    cotangent,
):
    node_rows, feat_cols = features.shape
    feat_size = lax.axis_size("feat")
    feat_at = lax.axis_index("feat")
    share = node_rows // feat_size
    graph = ("z", "y")
    low, high = forward_blocks(
        block_source, block_to_slot, send_counts[0], send_rows[0], features, adjacency
    )
    low_in = swap(low, graph)
    high_in = swap(high, graph)
    pieces = jnp.stack(
        [features.reshape(feat_size, share, feat_cols), cotangent.reshape(feat_size, share, feat_cols)],
        axis=1,
    )
    pieces = swap(after(pieces, low_in), "feat")
    degrees = degree.astype(F32)[:, None]
    degree_rows = lax.dynamic_slice_in_dim(degrees, feat_at * share, share, 0)
    adjacency_t = after(adjacency, low_in).swapaxes(1, 2)
    self_rows = lax.dynamic_slice_in_dim(w_self, feat_at * feat_cols, feat_cols, 0)

    partial_sum = scatter_low(low_in, node_rows)
    blk = adjacency.shape[1]
    parts = low.shape[0]
    ids = low_in[:, blk : blk + 4, :].astype(F32).reshape(parts // 8, 8, 4, blk).transpose(2, 0, 3, 1)
    own = own_term(pieces[:, 0], w_self)
    neighbor_mean = scatter_high(low_in, high_in, partial_sum, degrees)
    mean_pieces = swap(neighbor_mean.reshape(feat_size, share, feat_cols), "feat")
    back_pieces, hidden_pieces, grad_pre = dense(
        mean_pieces, own, pieces[:, 1], w_neigh, degree_rows
    )
    back_rows = swap(back_pieces, "feat").reshape(node_rows, feat_cols)
    grad_full = lax.all_gather(grad_pre, "feat", axis=0, tiled=True)
    back_low = swap(gather_rows(0, ids[0], ids[2], back_rows), graph)
    back_high = swap(gather_rows(1, ids[1], ids[3], back_rows), graph)
    hidden_out = swap(hidden_pieces, "feat").reshape(node_rows, feat_cols)

    both = jnp.concatenate([features, neighbor_mean], axis=1)
    weight_part = lax.dot_general(
        both, grad_full, (((0,), (0,)), ((), ())), preferred_element_type=F32
    ).astype(BF16)
    weight_grads = reduce_over_graph(weight_part)
    self_grad = lax.dot_general(
        grad_full, self_rows, (((1,), (1,)), ((), ())), preferred_element_type=F32
    )
    grad_features = backward_blocks(
        block_source, block_to_slot, back_low, back_high, adjacency_t, self_grad
    )
    return hidden_out, grad_features, weight_grads[:feat_cols], weight_grads[feat_cols:]


def solution(mesh):
    split = Mesh(mesh.devices.reshape(8, 4, 8), ("z", "y", "feat"))
    graph = ("z", "y")
    placed = (
        P(graph, "feat"),
        P(),
        P(),
        P(graph, None, None),
        P(graph),
        P(graph),
        P(graph, None, None),
        P(graph, None),
        P(graph),
        P(graph, "feat"),
    )
    return jax.shard_map(
        on_device,
        mesh=split,
        in_specs=placed,
        out_specs=(P(graph, "feat"), P(graph, "feat"), P("feat", None), P("feat", None)),
        check_vma=False,
    )
```

```python
import functools

import jax
import jax.numpy as jnp
from jax import lax
from jax.experimental import pallas as pl
from jax.experimental.pallas import tpu as pltpu
from jax.sharding import Mesh, PartitionSpec as P

BF16 = jnp.bfloat16
F32 = jnp.float32
VMEM_BYTES = 48 * 1024 * 1024


def params(axes=0):
    return pltpu.CompilerParams(
        dimension_semantics=("arbitrary",) * axes if axes else None, vmem_limit_bytes=VMEM_BYTES
    )


def full_spec(shape):
    return pl.BlockSpec(shape, lambda *unused: (0,) * len(shape))


def forward_blocks_kernel(
    source_ref, slot_ref, count_ref, rows_ref, feat_ref, adj_ref, low_ref, high_ref, sums_ref
):
    step = pl.program_id(0)
    chunk, blk, _ = adj_ref.shape
    parts = low_ref.shape[0]
    cols = feat_ref.shape[1]

    @pl.when(step == 0)
    def _():
        sums_ref[...] = jnp.zeros(sums_ref.shape, F32)

    for item in range(chunk):
        block = step * chunk + item
        start = pl.multiple_of(source_ref[block] * blk, blk)
        product = jnp.dot(
            adj_ref[item], feat_ref[pl.ds(start, blk), :], preferred_element_type=F32
        )
        sums_ref[slot_ref[block]] += product

    @pl.when(step == pl.num_programs(0) - 1)
    def _():
        slot_row = lax.broadcasted_iota(jnp.int32, (blk, cols), 0)
        lane = lax.broadcasted_iota(jnp.int32, (1, 2 * blk), 1)
        tile_row = lax.broadcasted_iota(jnp.int32, (16, blk), 0)

        def emit(part, carry):
            count = count_ref[part]
            low = jnp.where(slot_row < count, sums_ref[2 * part], 0.0)
            high = jnp.where(slot_row + blk < count, sums_ref[2 * part + 1], 0.0)
            low_ref[part, 0:blk, :] = low.astype(BF16)
            high_ref[part] = high.astype(BF16)
            ids = rows_ref[pl.ds(part, 1), :]
            live = lane < count
            fine = jnp.where(live, ids & (blk - 1), -1).astype(F32)
            coarse = jnp.where(live, ids >> 7, -1).astype(F32)
            tile = jnp.where(tile_row == 0, fine[:, :blk], 0.0)
            tile = jnp.where(tile_row == 1, fine[:, blk:], tile)
            tile = jnp.where(tile_row == 2, coarse[:, :blk], tile)
            tile = jnp.where(tile_row == 3, coarse[:, blk:], tile)
            low_ref[part, blk : blk + 16, :] = tile.astype(BF16)
            return carry

        lax.fori_loop(0, parts, emit, 0)


def forward_blocks(block_source, block_to_slot, counts, rows, features, adjacency):
    blocks, blk, _ = adjacency.shape
    nodes, cols = features.shape
    parts, cap = rows.shape
    chunk = 16
    return pl.pallas_call(
        forward_blocks_kernel,
        grid_spec=pltpu.PrefetchScalarGridSpec(
            num_scalar_prefetch=3,
            grid=(blocks // chunk,),
            in_specs=[
                full_spec((parts, cap)),
                full_spec((nodes, cols)),
                pl.BlockSpec((chunk, blk, blk), lambda i, *unused: (i, 0, 0)),
            ],
            out_specs=[full_spec((parts, blk + 16, cols)), full_spec((parts, blk, cols))],
            scratch_shapes=[pltpu.VMEM((parts * cap // blk, blk, cols), F32)],
        ),
        out_shape=[
            jax.ShapeDtypeStruct((parts, blk + 16, cols), BF16),
            jax.ShapeDtypeStruct((parts, blk, cols), BF16),
        ],
        compiler_params=params(1),
        name="forward_blocks",
    )(block_source, block_to_slot, counts, rows, features, adjacency)


def scatter_body(half, ids_ref, rows_ref, hot_ref, acc_ref, group):
    nodes, cols = acc_ref.shape
    blk = 128
    node_row = lax.broadcasted_iota(jnp.int32, (blk, blk), 0).astype(F32)
    for part in range(group):
        tile = ids_ref[part].astype(F32)
        fine = tile[half : half + 1, :]
        coarse = tile[2 + half : 3 + half, :]
        hot = jnp.where(node_row == fine, 1.0, 0.0).astype(BF16)
        for block in range(nodes // blk):
            keep = jnp.where(coarse == float(block), 1.0, 0.0).astype(BF16)
            hot_ref[block * blk : (block + 1) * blk, part * blk : (part + 1) * blk] = hot * keep
    rows = rows_ref[...].reshape(group * blk, cols)
    acc_ref[...] += jnp.dot(hot_ref[...], rows, preferred_element_type=F32)


def scatter_low_kernel(payload_ids_ref, rows_ref, sum_ref, hot_ref):
    @pl.when(pl.program_id(0) == 0)
    def _():
        sum_ref[...] = jnp.zeros(sum_ref.shape, F32)

    scatter_body(0, payload_ids_ref, rows_ref, hot_ref, sum_ref, rows_ref.shape[0])


def scatter_high_kernel(payload_ids_ref, rows_ref, init_ref, degree_ref, mean_ref, hot_ref, acc_ref):
    @pl.when(pl.program_id(0) == 0)
    def _():
        acc_ref[...] = init_ref[...]

    scatter_body(1, payload_ids_ref, rows_ref, hot_ref, acc_ref, rows_ref.shape[0])

    @pl.when(pl.program_id(0) == pl.num_programs(0) - 1)
    def _():
        mean_ref[...] = (acc_ref[...] / degree_ref[...]).astype(BF16)


def scatter_low(low, nodes):
    parts, height, cols = low.shape
    group, blk = 8, 128
    return pl.pallas_call(
        scatter_low_kernel,
        grid=(parts // group,),
        in_specs=[
            pl.BlockSpec((group, 16, cols), lambda i: (i, blk // 16, 0)),
            pl.BlockSpec((group, blk, cols), lambda i: (i, 0, 0)),
        ],
        out_specs=full_spec((nodes, cols)),
        out_shape=jax.ShapeDtypeStruct((nodes, cols), F32),
        scratch_shapes=[pltpu.VMEM((nodes, group * blk), BF16)],
        compiler_params=params(1),
        name="scatter_low",
    )(low, low)


def scatter_high(low, high, partial_sum, degrees):
    parts, blk, cols = high.shape
    nodes = partial_sum.shape[0]
    group = 8
    return pl.pallas_call(
        scatter_high_kernel,
        grid=(parts // group,),
        in_specs=[
            pl.BlockSpec((group, 16, cols), lambda i: (i, blk // 16, 0)),
            pl.BlockSpec((group, blk, cols), lambda i: (i, 0, 0)),
            full_spec((nodes, cols)),
            full_spec((nodes, 1)),
        ],
        out_specs=full_spec((nodes, cols)),
        out_shape=jax.ShapeDtypeStruct((nodes, cols), BF16),
        scratch_shapes=[
            pltpu.VMEM((nodes, group * blk), BF16),
            pltpu.VMEM((nodes, cols), F32),
        ],
        compiler_params=params(1),
        name="scatter_high",
    )(low, high, partial_sum, degrees)


def gather_kernel(half, fine_ref, coarse_ref, back_ref, out_ref, hot_ref):
    group, blk, cols = out_ref.shape
    nodes = back_ref.shape[0]
    lane = lax.broadcasted_iota(jnp.int32, (blk, blk), 1).astype(F32)
    for part in range(group):
        fine = jnp.broadcast_to(fine_ref[0, :, part : part + 1], (blk, blk))
        coarse = jnp.broadcast_to(coarse_ref[0, :, part : part + 1], (blk, blk))
        hot = jnp.where(lane == fine, 1.0, 0.0)
        for block in range(nodes // blk):
            value = jnp.where(coarse == float(block), hot, 0.0).astype(BF16)
            hot_ref[part * blk : (part + 1) * blk, block * blk : (block + 1) * blk] = value
    picked = jnp.dot(hot_ref[...], back_ref[...], preferred_element_type=F32)
    out_ref[...] = picked.astype(BF16).reshape(group, blk, cols)


def gather_rows(half, fine, coarse, back):
    steps, blk, group = fine.shape
    nodes, cols = back.shape
    return pl.pallas_call(
        functools.partial(gather_kernel, half),
        grid=(steps,),
        in_specs=[
            pl.BlockSpec((1, blk, group), lambda i: (i, 0, 0)),
            pl.BlockSpec((1, blk, group), lambda i: (i, 0, 0)),
            full_spec((nodes, cols)),
        ],
        out_specs=pl.BlockSpec((group, blk, cols), lambda i: (i, 0, 0)),
        out_shape=jax.ShapeDtypeStruct((steps * group, blk, cols), BF16),
        scratch_shapes=[pltpu.VMEM((group * blk, nodes), BF16)],
        compiler_params=params(1),
        name="gather_rows",
    )(fine, coarse, back)


def own_term_kernel(at_ref, feat_ref, weight_ref, out_ref):
    pieces = feat_ref.shape[0]
    rows = jnp.concatenate([feat_ref[piece] for piece in range(pieces)], axis=1)
    out_ref[...] = jnp.dot(rows, weight_ref[...], preferred_element_type=F32)


def own_term(at, feat_all, w_self, share):
    pieces, _, cols = feat_all.shape
    wide = w_self.shape[1]
    tile = 256
    return pl.pallas_call(
        own_term_kernel,
        grid_spec=pltpu.PrefetchScalarGridSpec(
            num_scalar_prefetch=1,
            grid=(wide // tile,),
            in_specs=[
                pl.BlockSpec((pieces, share, cols), lambda i, at: (0, at[0], 0)),
                pl.BlockSpec((pieces * cols, tile), lambda i, at: (0, i)),
            ],
            out_specs=pl.BlockSpec((share, tile), lambda i, at: (0, i)),
        ),
        out_shape=jax.ShapeDtypeStruct((share, wide), F32),
        compiler_params=params(1),
        name="own_term",
    )(at, feat_all, w_self)


def dense_kernel(
    at_ref, mean_ref, own_ref, cot_ref, weight_ref, degree_ref, back_ref, hidden_ref, grad_ref, acc_ref
):
    step = pl.program_id(0)
    pieces, rows, cols = mean_ref.shape
    tile = weight_ref.shape[1]
    mean = jnp.concatenate([mean_ref[piece] for piece in range(pieces)], axis=1)
    pre_act = own_ref[...] + jnp.dot(mean, weight_ref[...], preferred_element_type=F32)
    sig = jax.nn.sigmoid(pre_act)
    cot = jnp.concatenate([cot_ref[piece] for piece in range(cot_ref.shape[0])], axis=1)
    slope = sig * (1.0 + pre_act * (1.0 - sig))
    grad = (cot.astype(F32) * slope).astype(BF16)
    hidden = (pre_act * sig).astype(BF16)
    grad_ref[...] = grad
    for piece in range(tile // cols):
        hidden_ref[piece] = hidden[:, piece * cols : (piece + 1) * cols]
    update = lax.dot_general(
        grad, weight_ref[...], (((1,), (1,)), ((), ())), preferred_element_type=F32
    )

    @pl.when(step == 0)
    def _():
        acc_ref[...] = update

    @pl.when(step > 0)
    def _():
        acc_ref[...] += update

    @pl.when(step == pl.num_programs(0) - 1)
    def _():
        back = (acc_ref[...] / degree_ref[...]).astype(BF16)
        for piece in range(pieces):
            back_ref[piece] = back[:, piece * cols : (piece + 1) * cols]


def dense(at, mean_pieces, own, cot_all, w_neigh, degrees):
    pieces, rows, cols = mean_pieces.shape
    wide = w_neigh.shape[1]
    tile = 256
    per = tile // cols
    return pl.pallas_call(
        dense_kernel,
        grid_spec=pltpu.PrefetchScalarGridSpec(
            num_scalar_prefetch=1,
            grid=(wide // tile,),
            in_specs=[
                full_spec((pieces, rows, cols)),
                pl.BlockSpec((rows, tile), lambda i, at: (0, i)),
                pl.BlockSpec((per, rows, cols), lambda i, at: (i, at[0], 0)),
                pl.BlockSpec((pieces * cols, tile), lambda i, at: (0, i)),
                pl.BlockSpec((rows, 1), lambda i, at: (at[0], 0)),
            ],
            out_specs=[
                full_spec((pieces, rows, cols)),
                pl.BlockSpec((per, rows, cols), lambda i, at: (i, 0, 0)),
                pl.BlockSpec((rows, tile), lambda i, at: (0, i)),
            ],
            scratch_shapes=[pltpu.VMEM((rows, wide), F32)],
        ),
        out_shape=[
            jax.ShapeDtypeStruct((pieces, rows, cols), BF16),
            jax.ShapeDtypeStruct((pieces, rows, cols), BF16),
            jax.ShapeDtypeStruct((rows, wide), BF16),
        ],
        compiler_params=params(1),
        name="dense",
    )(at, mean_pieces, own, cot_all, w_neigh, degrees)


def backward_blocks_kernel(
    source_ref, slot_ref, low_ref, high_ref, adj_ref, self_ref, out_ref, both_ref, acc_ref
):
    step = pl.program_id(0)
    chunk, blk, _ = adj_ref.shape
    parts = low_ref.shape[0]

    @pl.when(step == 0)
    def _():
        acc_ref[...] = self_ref[...]
        for part in range(parts):
            both_ref[2 * part] = low_ref[part]
            both_ref[2 * part + 1] = high_ref[part]

    for item in range(chunk):
        block = step * chunk + item
        start = pl.multiple_of(source_ref[block] * blk, blk)
        product = jnp.dot(
            adj_ref[item], both_ref[slot_ref[block]], preferred_element_type=F32
        )
        acc_ref[pl.ds(start, blk), :] += product

    @pl.when(step == pl.num_programs(0) - 1)
    def _():
        out_ref[...] = acc_ref[...].astype(BF16)


def backward_blocks(block_source, block_to_slot, low, high, adjacency_t, self_grad):
    blocks, blk, _ = adjacency_t.shape
    nodes, cols = self_grad.shape
    parts = low.shape[0]
    chunk = 16
    return pl.pallas_call(
        backward_blocks_kernel,
        grid_spec=pltpu.PrefetchScalarGridSpec(
            num_scalar_prefetch=2,
            grid=(blocks // chunk,),
            in_specs=[
                full_spec((parts, blk, cols)),
                full_spec((parts, blk, cols)),
                pl.BlockSpec((chunk, blk, blk), lambda i, *unused: (i, 0, 0)),
                full_spec((nodes, cols)),
            ],
            out_specs=full_spec((nodes, cols)),
            scratch_shapes=[
                pltpu.VMEM((2 * parts, blk, cols), BF16),
                pltpu.VMEM((nodes, cols), F32),
            ],
        ),
        out_shape=jax.ShapeDtypeStruct((nodes, cols), BF16),
        compiler_params=params(1),
        name="backward_blocks",
    )(block_source, block_to_slot, low, high, adjacency_t, self_grad)


def swap(value, axis):
    return lax.all_to_all(value, axis, split_axis=0, concat_axis=0, tiled=True)


def after(value, *others):
    return lax.optimization_barrier((value, *others))[0]


def rotate(value, axis, distance):
    size = lax.axis_size(axis)
    return lax.ppermute(value, axis, [(i, (i + distance) % size) for i in range(size)])


def scatter_sum(pieces, axis):
    size, at = lax.axis_size(axis), lax.axis_index(axis)
    take = functools.partial(lax.dynamic_index_in_dim, pieces, axis=0, keepdims=False)
    total = take(at).astype(F32)
    came = [rotate(take((at + d) % size), axis, d) for d in range(1, size)]
    for piece in came:
        total = total + piece.astype(F32)
    return total.astype(BF16)


def around(piece, axis):
    size = lax.axis_size(axis)
    return [piece] + [rotate(piece, axis, size - i) for i in range(1, size)]


def unroll_pieces(pieces, axis):
    size, at = lax.axis_size(axis), lax.axis_index(axis)
    doubled = jnp.stack(pieces + pieces)
    return lax.dynamic_slice_in_dim(doubled, (size - at) % size, size, 0)


def assemble_kernel(at_ref, *refs):
    *piece_refs, first_ref, second_ref = refs
    size = len(piece_refs)
    half = size // 2
    for i, piece_ref in enumerate(piece_refs):
        place = (at_ref[0] + i) % size
        value = piece_ref[...].astype(F32)

        @pl.when(place < half)
        def _():
            first_ref[place] = value

        @pl.when(place >= half)
        def _():
            second_ref[place - half] = value


def assemble(at, pieces):
    rows, wide = pieces[0].shape
    half = len(pieces) // 2
    first, second = pl.pallas_call(
        assemble_kernel,
        grid_spec=pltpu.PrefetchScalarGridSpec(
            num_scalar_prefetch=1,
            grid=(1,),
            in_specs=[full_spec((rows, wide))] * len(pieces),
            out_specs=[full_spec((half, rows, wide))] * 2,
        ),
        out_shape=[jax.ShapeDtypeStruct((half, rows, wide), F32)] * 2,
        compiler_params=params(1),
        name="assemble",
    )(at, *pieces)
    return first.reshape(half * rows, wide), second.reshape(half * rows, wide)


def reduce_over_graph(partial):
    rows, wide = partial.shape
    over_y, over_z = lax.axis_size("y"), lax.axis_size("z")
    chunk = rows // over_y
    part = scatter_sum(partial.reshape(over_y, chunk, wide), "y")
    part = scatter_sum(part.reshape(over_z, chunk // over_z, wide), "z")
    part = unroll_pieces(around(part, "z"), "z").reshape(chunk, wide)
    at = jnp.full((1,), lax.axis_index("y"), jnp.int32)
    return assemble(at, around(part, "y"))


def on_device(
    features,
    w_self,
    w_neigh,
    adjacency,
    block_source,
    block_to_slot,
    send_rows,
    send_counts,
    degree,
    cotangent,
):
    node_rows, feat_cols = features.shape
    feat_size = lax.axis_size("feat")
    feat_at = lax.axis_index("feat")
    at = jnp.full((1,), feat_at, jnp.int32)
    share = node_rows // feat_size
    graph = ("z", "y")
    low, high = forward_blocks(
        block_source, block_to_slot, send_counts[0], send_rows[0], features, adjacency
    )
    low_in = swap(low, graph)
    high_in = swap(high, graph)
    feat_all = lax.all_gather(features, "feat", axis=0)
    cot_all = lax.all_gather(cotangent, "feat", axis=0)
    degrees = degree.astype(F32)[:, None]
    adjacency_t = after(adjacency, low_in).swapaxes(1, 2)
    self_rows = lax.dynamic_slice_in_dim(w_self, feat_at * feat_cols, feat_cols, 0)

    partial_sum = scatter_low(low_in, node_rows)
    blk = adjacency.shape[1]
    parts = low.shape[0]
    ids = low_in[:, blk : blk + 4, :].astype(F32).reshape(parts // 8, 8, 4, blk).transpose(2, 0, 3, 1)
    own = own_term(at, feat_all, w_self, share)
    partial_sum, adjacency_t, ids, own = lax.optimization_barrier(
        (partial_sum, adjacency_t, ids, own)
    )
    neighbor_mean = scatter_high(low_in, high_in, partial_sum, degrees)
    mean_pieces = swap(neighbor_mean.reshape(feat_size, share, feat_cols), "feat")
    back_pieces, hidden_pieces, grad_pre = dense(at, mean_pieces, own, cot_all, w_neigh, degrees)
    back_rows = swap(back_pieces, "feat").reshape(node_rows, feat_cols)
    back_rows, grad_pre, hidden_pieces = lax.optimization_barrier(
        (back_rows, grad_pre, hidden_pieces)
    )
    rows_low = gather_rows(0, ids[0], ids[2], back_rows)
    rows_high = gather_rows(1, ids[1], ids[3], back_rows)
    back_low = swap(rows_low, graph)
    back_high = swap(rows_high, graph)
    grad_full = lax.all_gather(grad_pre, "feat", axis=0, tiled=True)
    grad_full = after(grad_full, rows_low, rows_high)

    both = jnp.concatenate([features, neighbor_mean], axis=1)
    weight_part = lax.dot_general(
        both, grad_full, (((0,), (0,)), ((), ())), preferred_element_type=F32
    ).astype(BF16)
    hidden_all = lax.all_gather(after(hidden_pieces, weight_part), "feat", axis=0)
    hidden_out = lax.dynamic_index_in_dim(hidden_all, feat_at, 1, keepdims=False)
    hidden_out = hidden_out.reshape(node_rows, feat_cols)
    grad_self, grad_neigh = reduce_over_graph(weight_part)
    self_grad = lax.dot_general(
        grad_full, self_rows, (((1,), (1,)), ((), ())), preferred_element_type=F32
    )
    grad_features = backward_blocks(
        block_source, block_to_slot, back_low, back_high, adjacency_t, self_grad
    )
    return hidden_out, grad_features, grad_self, grad_neigh


def solution(mesh):
    split = Mesh(mesh.devices.reshape(8, 4, 8), ("z", "y", "feat"))
    graph = ("z", "y")
    placed = (
        P(graph, "feat"),
        P(),
        P(),
        P(graph, None, None),
        P(graph),
        P(graph),
        P(graph, None, None),
        P(graph, None),
        P(graph),
        P(graph, "feat"),
    )
    return jax.shard_map(
        on_device,
        mesh=split,
        in_specs=placed,
        out_specs=(P(graph, "feat"), P(graph, "feat"), P("feat", None), P("feat", None)),
        check_vma=False,
    )
```

```python
import functools

import jax
import jax.numpy as jnp
from jax import lax
from jax.experimental import pallas as pl
from jax.experimental.pallas import tpu as pltpu
from jax.sharding import Mesh, PartitionSpec as P

BF16 = jnp.bfloat16
F32 = jnp.float32
VMEM_BYTES = 48 * 1024 * 1024


def params(axes=0):
    return pltpu.CompilerParams(
        dimension_semantics=("arbitrary",) * axes if axes else None, vmem_limit_bytes=VMEM_BYTES
    )


def full_spec(shape):
    return pl.BlockSpec(shape, lambda *unused: (0,) * len(shape))


def forward_blocks_kernel(
    source_ref, slot_ref, count_ref, rows_ref, feat_ref, adj_ref, low_ref, high_ref, sums_ref
):
    step = pl.program_id(0)
    chunk, blk, _ = adj_ref.shape
    parts = low_ref.shape[0]
    cols = feat_ref.shape[1]

    @pl.when(step == 0)
    def _():
        sums_ref[...] = jnp.zeros(sums_ref.shape, F32)

    for item in range(chunk):
        block = step * chunk + item
        start = pl.multiple_of(source_ref[block] * blk, blk)
        product = jnp.dot(
            adj_ref[item], feat_ref[pl.ds(start, blk), :], preferred_element_type=F32
        )
        sums_ref[slot_ref[block]] += product

    @pl.when(step == pl.num_programs(0) - 1)
    def _():
        slot_row = lax.broadcasted_iota(jnp.int32, (blk, cols), 0)
        lane = lax.broadcasted_iota(jnp.int32, (1, 2 * blk), 1)
        tile_row = lax.broadcasted_iota(jnp.int32, (16, blk), 0)

        def emit(part, carry):
            count = count_ref[part]
            low = jnp.where(slot_row < count, sums_ref[2 * part], 0.0)
            high = jnp.where(slot_row + blk < count, sums_ref[2 * part + 1], 0.0)
            low_ref[part, 0:blk, :] = low.astype(BF16)
            high_ref[part] = high.astype(BF16)
            ids = rows_ref[pl.ds(part, 1), :]
            live = lane < count
            fine = jnp.where(live, ids & (blk - 1), -1).astype(F32)
            coarse = jnp.where(live, ids >> 7, -1).astype(F32)
            tile = jnp.where(tile_row == 0, fine[:, :blk], 0.0)
            tile = jnp.where(tile_row == 1, fine[:, blk:], tile)
            tile = jnp.where(tile_row == 2, coarse[:, :blk], tile)
            tile = jnp.where(tile_row == 3, coarse[:, blk:], tile)
            low_ref[part, blk : blk + 16, :] = tile.astype(BF16)
            return carry

        lax.fori_loop(0, parts, emit, 0)


def forward_blocks(block_source, block_to_slot, counts, rows, features, adjacency):
    blocks, blk, _ = adjacency.shape
    nodes, cols = features.shape
    parts, cap = rows.shape
    chunk = 16
    return pl.pallas_call(
        forward_blocks_kernel,
        grid_spec=pltpu.PrefetchScalarGridSpec(
            num_scalar_prefetch=3,
            grid=(blocks // chunk,),
            in_specs=[
                full_spec((parts, cap)),
                full_spec((nodes, cols)),
                pl.BlockSpec((chunk, blk, blk), lambda i, *unused: (i, 0, 0)),
            ],
            out_specs=[full_spec((parts, blk + 16, cols)), full_spec((parts, blk, cols))],
            scratch_shapes=[pltpu.VMEM((parts * cap // blk, blk, cols), F32)],
        ),
        out_shape=[
            jax.ShapeDtypeStruct((parts, blk + 16, cols), BF16),
            jax.ShapeDtypeStruct((parts, blk, cols), BF16),
        ],
        compiler_params=params(1),
        name="forward_blocks",
    )(block_source, block_to_slot, counts, rows, features, adjacency)


def scatter_body(half, ids_ref, rows_ref, hot_ref, acc_ref, group):
    nodes, cols = acc_ref.shape
    blk = 128
    node_row = lax.broadcasted_iota(jnp.int32, (blk, blk), 0).astype(F32)
    for part in range(group):
        tile = ids_ref[part].astype(F32)
        fine = tile[half : half + 1, :]
        coarse = tile[2 + half : 3 + half, :]
        hot = jnp.where(node_row == fine, 1.0, 0.0).astype(BF16)
        for block in range(nodes // blk):
            keep = jnp.where(coarse == float(block), 1.0, 0.0).astype(BF16)
            hot_ref[block * blk : (block + 1) * blk, part * blk : (part + 1) * blk] = hot * keep
    rows = rows_ref[...].reshape(group * blk, cols)
    acc_ref[...] += jnp.dot(hot_ref[...], rows, preferred_element_type=F32)


def scatter_low_kernel(payload_ids_ref, rows_ref, sum_ref, hot_ref):
    @pl.when(pl.program_id(0) == 0)
    def _():
        sum_ref[...] = jnp.zeros(sum_ref.shape, F32)

    scatter_body(0, payload_ids_ref, rows_ref, hot_ref, sum_ref, rows_ref.shape[0])


def scatter_high_kernel(payload_ids_ref, rows_ref, init_ref, degree_ref, mean_ref, hot_ref, acc_ref):
    @pl.when(pl.program_id(0) == 0)
    def _():
        acc_ref[...] = init_ref[...]

    scatter_body(1, payload_ids_ref, rows_ref, hot_ref, acc_ref, rows_ref.shape[0])

    @pl.when(pl.program_id(0) == pl.num_programs(0) - 1)
    def _():
        mean_ref[...] = (acc_ref[...] / degree_ref[...]).astype(BF16)


def scatter_low(low, nodes):
    parts, height, cols = low.shape
    group, blk = 8, 128
    return pl.pallas_call(
        scatter_low_kernel,
        grid=(parts // group,),
        in_specs=[
            pl.BlockSpec((group, 16, cols), lambda i: (i, blk // 16, 0)),
            pl.BlockSpec((group, blk, cols), lambda i: (i, 0, 0)),
        ],
        out_specs=full_spec((nodes, cols)),
        out_shape=jax.ShapeDtypeStruct((nodes, cols), F32),
        scratch_shapes=[pltpu.VMEM((nodes, group * blk), BF16)],
        compiler_params=params(1),
        name="scatter_low",
    )(low, low)


def scatter_high(low, high, partial_sum, degrees):
    parts, blk, cols = high.shape
    nodes = partial_sum.shape[0]
    group = 8
    return pl.pallas_call(
        scatter_high_kernel,
        grid=(parts // group,),
        in_specs=[
            pl.BlockSpec((group, 16, cols), lambda i: (i, blk // 16, 0)),
            pl.BlockSpec((group, blk, cols), lambda i: (i, 0, 0)),
            full_spec((nodes, cols)),
            full_spec((nodes, 1)),
        ],
        out_specs=full_spec((nodes, cols)),
        out_shape=jax.ShapeDtypeStruct((nodes, cols), BF16),
        scratch_shapes=[
            pltpu.VMEM((nodes, group * blk), BF16),
            pltpu.VMEM((nodes, cols), F32),
        ],
        compiler_params=params(1),
        name="scatter_high",
    )(low, high, partial_sum, degrees)


def gather_kernel(half, fine_ref, coarse_ref, back_ref, out_ref, hot_ref):
    group, blk, cols = out_ref.shape
    nodes = back_ref.shape[0]
    lane = lax.broadcasted_iota(jnp.int32, (blk, blk), 1).astype(F32)
    for part in range(group):
        fine = jnp.broadcast_to(fine_ref[0, :, part : part + 1], (blk, blk))
        coarse = jnp.broadcast_to(coarse_ref[0, :, part : part + 1], (blk, blk))
        hot = jnp.where(lane == fine, 1.0, 0.0)
        for block in range(nodes // blk):
            value = jnp.where(coarse == float(block), hot, 0.0).astype(BF16)
            hot_ref[part * blk : (part + 1) * blk, block * blk : (block + 1) * blk] = value
    picked = jnp.dot(hot_ref[...], back_ref[...], preferred_element_type=F32)
    out_ref[...] = picked.astype(BF16).reshape(group, blk, cols)


def gather_rows(half, fine, coarse, back):
    steps, blk, group = fine.shape
    nodes, cols = back.shape
    return pl.pallas_call(
        functools.partial(gather_kernel, half),
        grid=(steps,),
        in_specs=[
            pl.BlockSpec((1, blk, group), lambda i: (i, 0, 0)),
            pl.BlockSpec((1, blk, group), lambda i: (i, 0, 0)),
            full_spec((nodes, cols)),
        ],
        out_specs=pl.BlockSpec((group, blk, cols), lambda i: (i, 0, 0)),
        out_shape=jax.ShapeDtypeStruct((steps * group, blk, cols), BF16),
        scratch_shapes=[pltpu.VMEM((group * blk, nodes), BF16)],
        compiler_params=params(1),
        name="gather_rows",
    )(fine, coarse, back)


def own_term_kernel(at_ref, feat_ref, weight_ref, out_ref):
    pieces = feat_ref.shape[0]
    rows = jnp.concatenate([feat_ref[piece] for piece in range(pieces)], axis=1)
    out_ref[...] = jnp.dot(rows, weight_ref[...], preferred_element_type=F32)


def own_term(at, feat_all, w_self, share):
    pieces, _, cols = feat_all.shape
    wide = w_self.shape[1]
    tile = 256
    return pl.pallas_call(
        own_term_kernel,
        grid_spec=pltpu.PrefetchScalarGridSpec(
            num_scalar_prefetch=1,
            grid=(wide // tile,),
            in_specs=[
                pl.BlockSpec((pieces, share, cols), lambda i, at: (0, at[0], 0)),
                pl.BlockSpec((pieces * cols, tile), lambda i, at: (0, i)),
            ],
            out_specs=pl.BlockSpec((share, tile), lambda i, at: (0, i)),
        ),
        out_shape=jax.ShapeDtypeStruct((share, wide), F32),
        compiler_params=params(1),
        name="own_term",
    )(at, feat_all, w_self)


def dense_kernel(
    at_ref, mean_ref, own_ref, cot_ref, weight_ref, degree_ref, back_ref, hidden_ref, grad_ref, acc_ref
):
    step = pl.program_id(0)
    pieces, rows, cols = mean_ref.shape
    tile = weight_ref.shape[1]
    mean = jnp.concatenate([mean_ref[piece] for piece in range(pieces)], axis=1)
    pre_act = own_ref[...] + jnp.dot(mean, weight_ref[...], preferred_element_type=F32)
    sig = jax.nn.sigmoid(pre_act)
    cot = jnp.concatenate([cot_ref[piece] for piece in range(cot_ref.shape[0])], axis=1)
    slope = sig * (1.0 + pre_act * (1.0 - sig))
    grad = (cot.astype(F32) * slope).astype(BF16)
    hidden = (pre_act * sig).astype(BF16)
    grad_ref[...] = grad
    for piece in range(tile // cols):
        hidden_ref[piece] = hidden[:, piece * cols : (piece + 1) * cols]
    update = lax.dot_general(
        grad, weight_ref[...], (((1,), (1,)), ((), ())), preferred_element_type=F32
    )

    @pl.when(step == 0)
    def _():
        acc_ref[...] = update

    @pl.when(step > 0)
    def _():
        acc_ref[...] += update

    @pl.when(step == pl.num_programs(0) - 1)
    def _():
        back = (acc_ref[...] / degree_ref[...]).astype(BF16)
        for piece in range(pieces):
            back_ref[piece] = back[:, piece * cols : (piece + 1) * cols]


def dense(at, mean_pieces, own, cot_all, w_neigh, degrees):
    pieces, rows, cols = mean_pieces.shape
    wide = w_neigh.shape[1]
    tile = 256
    per = tile // cols
    return pl.pallas_call(
        dense_kernel,
        grid_spec=pltpu.PrefetchScalarGridSpec(
            num_scalar_prefetch=1,
            grid=(wide // tile,),
            in_specs=[
                full_spec((pieces, rows, cols)),
                pl.BlockSpec((rows, tile), lambda i, at: (0, i)),
                pl.BlockSpec((per, rows, cols), lambda i, at: (i, at[0], 0)),
                pl.BlockSpec((pieces * cols, tile), lambda i, at: (0, i)),
                pl.BlockSpec((rows, 1), lambda i, at: (at[0], 0)),
            ],
            out_specs=[
                full_spec((pieces, rows, cols)),
                pl.BlockSpec((per, rows, cols), lambda i, at: (i, 0, 0)),
                pl.BlockSpec((rows, tile), lambda i, at: (0, i)),
            ],
            scratch_shapes=[pltpu.VMEM((rows, wide), F32)],
        ),
        out_shape=[
            jax.ShapeDtypeStruct((pieces, rows, cols), BF16),
            jax.ShapeDtypeStruct((pieces, rows, cols), BF16),
            jax.ShapeDtypeStruct((rows, wide), BF16),
        ],
        compiler_params=params(1),
        name="dense",
    )(at, mean_pieces, own, cot_all, w_neigh, degrees)


def backward_blocks_kernel(
    source_ref, slot_ref, low_ref, high_ref, adj_ref, self_ref, out_ref, both_ref, acc_ref
):
    step = pl.program_id(0)
    chunk, blk, _ = adj_ref.shape
    parts = low_ref.shape[0]

    @pl.when(step == 0)
    def _():
        acc_ref[...] = self_ref[...]
        for part in range(parts):
            both_ref[2 * part] = low_ref[part]
            both_ref[2 * part + 1] = high_ref[part]

    for item in range(chunk):
        block = step * chunk + item
        start = pl.multiple_of(source_ref[block] * blk, blk)
        product = jnp.dot(
            adj_ref[item], both_ref[slot_ref[block]], preferred_element_type=F32
        )
        acc_ref[pl.ds(start, blk), :] += product

    @pl.when(step == pl.num_programs(0) - 1)
    def _():
        out_ref[...] = acc_ref[...].astype(BF16)


def backward_blocks(block_source, block_to_slot, low, high, adjacency_t, self_grad):
    blocks, blk, _ = adjacency_t.shape
    nodes, cols = self_grad.shape
    parts = low.shape[0]
    chunk = 16
    return pl.pallas_call(
        backward_blocks_kernel,
        grid_spec=pltpu.PrefetchScalarGridSpec(
            num_scalar_prefetch=2,
            grid=(blocks // chunk,),
            in_specs=[
                full_spec((parts, blk, cols)),
                full_spec((parts, blk, cols)),
                pl.BlockSpec((chunk, blk, blk), lambda i, *unused: (i, 0, 0)),
                full_spec((nodes, cols)),
            ],
            out_specs=full_spec((nodes, cols)),
            scratch_shapes=[
                pltpu.VMEM((2 * parts, blk, cols), BF16),
                pltpu.VMEM((nodes, cols), F32),
            ],
        ),
        out_shape=jax.ShapeDtypeStruct((nodes, cols), BF16),
        compiler_params=params(1),
        name="backward_blocks",
    )(block_source, block_to_slot, low, high, adjacency_t, self_grad)


def swap(value, axis):
    return lax.all_to_all(value, axis, split_axis=0, concat_axis=0, tiled=True)


def after(value, *others):
    return lax.optimization_barrier((value, *others))[0]


def rotate(value, axis, distance):
    size = lax.axis_size(axis)
    return lax.ppermute(value, axis, [(i, (i + distance) % size) for i in range(size)])


def scatter_sum(pieces, axis):
    size, at = lax.axis_size(axis), lax.axis_index(axis)
    take = functools.partial(lax.dynamic_index_in_dim, pieces, axis=0, keepdims=False)
    total = take(at).astype(F32)
    came = [rotate(take((at + d) % size), axis, d) for d in range(1, size)]
    for piece in came:
        total = total + piece.astype(F32)
    return total.astype(BF16)


def around(piece, axis):
    size = lax.axis_size(axis)
    return [piece] + [rotate(piece, axis, size - i) for i in range(1, size)]


def exchange_sum(value, axis):
    size, distance = lax.axis_size(axis), 1
    while distance < size:
        other = lax.ppermute(value, axis, [(i, i ^ distance) for i in range(size)])
        value = (value.astype(F32) + other.astype(F32)).astype(BF16)
        distance *= 2
    return value


def assemble_kernel(at_ref, *refs):
    *piece_refs, first_ref, second_ref = refs
    size = len(piece_refs)
    half = size // 2
    for i, piece_ref in enumerate(piece_refs):
        place = (at_ref[0] + i) % size
        value = piece_ref[...].astype(F32)

        @pl.when(place < half)
        def _():
            first_ref[place] = value

        @pl.when(place >= half)
        def _():
            second_ref[place - half] = value


def assemble(at, pieces):
    rows, wide = pieces[0].shape
    half = len(pieces) // 2
    first, second = pl.pallas_call(
        assemble_kernel,
        grid_spec=pltpu.PrefetchScalarGridSpec(
            num_scalar_prefetch=1,
            grid=(1,),
            in_specs=[full_spec((rows, wide))] * len(pieces),
            out_specs=[full_spec((half, rows, wide))] * 2,
        ),
        out_shape=[jax.ShapeDtypeStruct((half, rows, wide), F32)] * 2,
        compiler_params=params(1),
        name="assemble",
    )(at, *pieces)
    return first.reshape(half * rows, wide), second.reshape(half * rows, wide)


def reduce_over_graph(partial):
    rows, wide = partial.shape
    over_y = lax.axis_size("y")
    part = scatter_sum(partial.reshape(over_y, rows // over_y, wide), "y")
    part = exchange_sum(part, "z")
    at = jnp.full((1,), lax.axis_index("y"), jnp.int32)
    return assemble(at, around(part, "y"))


def on_device(
    features,
    w_self,
    w_neigh,
    adjacency,
    block_source,
    block_to_slot,
    send_rows,
    send_counts,
    degree,
    cotangent,
):
    node_rows, feat_cols = features.shape
    feat_size = lax.axis_size("feat")
    feat_at = lax.axis_index("feat")
    at = jnp.full((1,), feat_at, jnp.int32)
    share = node_rows // feat_size
    graph = ("z", "y")
    low, high = forward_blocks(
        block_source, block_to_slot, send_counts[0], send_rows[0], features, adjacency
    )
    low_in = swap(low, graph)
    high_in = swap(high, graph)
    feat_all = lax.all_gather(features, "feat", axis=0)
    cot_all = lax.all_gather(cotangent, "feat", axis=0)
    degrees = degree.astype(F32)[:, None]
    adjacency_t = after(adjacency, low_in).swapaxes(1, 2)
    self_rows = lax.dynamic_slice_in_dim(w_self, feat_at * feat_cols, feat_cols, 0)

    partial_sum = scatter_low(low_in, node_rows)
    blk = adjacency.shape[1]
    parts = low.shape[0]
    ids = low_in[:, blk : blk + 4, :].astype(F32).reshape(parts // 8, 8, 4, blk).transpose(2, 0, 3, 1)
    own = own_term(at, feat_all, w_self, share)
    partial_sum, adjacency_t, ids, own = lax.optimization_barrier(
        (partial_sum, adjacency_t, ids, own)
    )
    neighbor_mean = scatter_high(low_in, high_in, partial_sum, degrees)
    mean_pieces = swap(neighbor_mean.reshape(feat_size, share, feat_cols), "feat")
    back_pieces, hidden_pieces, grad_pre = dense(at, mean_pieces, own, cot_all, w_neigh, degrees)
    back_rows = swap(back_pieces, "feat").reshape(node_rows, feat_cols)
    back_rows, grad_pre, hidden_pieces = lax.optimization_barrier(
        (back_rows, grad_pre, hidden_pieces)
    )
    rows_low = gather_rows(0, ids[0], ids[2], back_rows)
    rows_high = gather_rows(1, ids[1], ids[3], back_rows)
    back_low = swap(rows_low, graph)
    back_high = swap(rows_high, graph)
    grad_full = lax.all_gather(grad_pre, "feat", axis=0, tiled=True)
    grad_full = after(grad_full, rows_high, back_low)

    both = jnp.concatenate([features, neighbor_mean], axis=1)
    weight_part = lax.dot_general(
        both, grad_full, (((0,), (0,)), ((), ())), preferred_element_type=F32
    ).astype(BF16)
    hidden_all = lax.all_gather(after(hidden_pieces, weight_part), "feat", axis=0)
    hidden_out = lax.dynamic_index_in_dim(hidden_all, feat_at, 1, keepdims=False)
    hidden_out = hidden_out.reshape(node_rows, feat_cols)
    grad_self, grad_neigh = reduce_over_graph(weight_part)
    self_grad = lax.dot_general(
        grad_full, self_rows, (((1,), (1,)), ((), ())), preferred_element_type=F32
    )
    grad_features = backward_blocks(
        block_source, block_to_slot, back_low, back_high, adjacency_t, self_grad
    )
    return hidden_out, grad_features, grad_self, grad_neigh


def solution(mesh):
    split = Mesh(mesh.devices.reshape(8, 4, 8), ("z", "y", "feat"))
    graph = ("z", "y")
    placed = (
        P(graph, "feat"),
        P(),
        P(),
        P(graph, None, None),
        P(graph),
        P(graph),
        P(graph, None, None),
        P(graph, None),
        P(graph),
        P(graph, "feat"),
    )
    return jax.shard_map(
        on_device,
        mesh=split,
        in_specs=placed,
        out_specs=(P(graph, "feat"), P(graph, "feat"), P("feat", None), P("feat", None)),
        check_vma=False,
    )
```

```python
import functools

import jax
import jax.numpy as jnp
from jax import lax
from jax.experimental import pallas as pl
from jax.experimental.pallas import tpu as pltpu
from jax.sharding import Mesh, PartitionSpec as P

BF16 = jnp.bfloat16
F32 = jnp.float32
VMEM_BYTES = 48 * 1024 * 1024
ID_ROWS = 8


def params(axes=0):
    return pltpu.CompilerParams(
        dimension_semantics=("arbitrary",) * axes if axes else None, vmem_limit_bytes=VMEM_BYTES
    )


def full_spec(shape):
    return pl.BlockSpec(shape, lambda *unused: (0,) * len(shape))


def forward_blocks_kernel(
    source_ref, slot_ref, count_ref, rows_ref, feat_ref, adj_ref, low_ref, high_ref, sums_ref
):
    step = pl.program_id(0)
    chunk, blk, _ = adj_ref.shape
    parts = low_ref.shape[0]
    cols = feat_ref.shape[1]

    @pl.when(step == 0)
    def _():
        sums_ref[...] = jnp.zeros(sums_ref.shape, F32)

    for item in range(chunk):
        block = step * chunk + item
        start = pl.multiple_of(source_ref[block] * blk, blk)
        product = jnp.dot(
            adj_ref[item], feat_ref[pl.ds(start, blk), :], preferred_element_type=F32
        )
        sums_ref[slot_ref[block]] += product

    @pl.when(step == pl.num_programs(0) - 1)
    def _():
        slot_row = lax.broadcasted_iota(jnp.int32, (blk, cols), 0)
        lane = lax.broadcasted_iota(jnp.int32, (1, 2 * blk), 1)
        tile_row = lax.broadcasted_iota(jnp.int32, (ID_ROWS, blk), 0)

        def emit(part, carry):
            count = count_ref[part]
            low = jnp.where(slot_row < count, sums_ref[2 * part], 0.0)
            high = jnp.where(slot_row + blk < count, sums_ref[2 * part + 1], 0.0)
            low_ref[part, 0:blk, :] = low.astype(BF16)
            high_ref[part] = high.astype(BF16)
            ids = rows_ref[pl.ds(part, 1), :]
            live = lane < count
            fine = jnp.where(live, ids & (blk - 1), -1).astype(F32)
            coarse = jnp.where(live, ids >> 7, -1).astype(F32)
            tile = jnp.where(tile_row == 0, fine[:, :blk], 0.0)
            tile = jnp.where(tile_row == 1, fine[:, blk:], tile)
            tile = jnp.where(tile_row == 2, coarse[:, :blk], tile)
            tile = jnp.where(tile_row == 3, coarse[:, blk:], tile)
            low_ref[part, blk : blk + ID_ROWS, :] = tile.astype(BF16)
            return carry

        lax.fori_loop(0, parts, emit, 0)


def forward_blocks(block_source, block_to_slot, counts, rows, features, adjacency):
    blocks, blk, _ = adjacency.shape
    nodes, cols = features.shape
    parts, cap = rows.shape
    chunk = 16
    return pl.pallas_call(
        forward_blocks_kernel,
        grid_spec=pltpu.PrefetchScalarGridSpec(
            num_scalar_prefetch=3,
            grid=(blocks // chunk,),
            in_specs=[
                full_spec((parts, cap)),
                full_spec((nodes, cols)),
                pl.BlockSpec((chunk, blk, blk), lambda i, *unused: (i, 0, 0)),
            ],
            out_specs=[full_spec((parts, blk + ID_ROWS, cols)), full_spec((parts, blk, cols))],
            scratch_shapes=[pltpu.VMEM((parts * cap // blk, blk, cols), F32)],
        ),
        out_shape=[
            jax.ShapeDtypeStruct((parts, blk + ID_ROWS, cols), BF16),
            jax.ShapeDtypeStruct((parts, blk, cols), BF16),
        ],
        compiler_params=params(1),
        name="forward_blocks",
    )(block_source, block_to_slot, counts, rows, features, adjacency)


def scatter_body(half, ids_ref, rows_ref, hot_ref, acc_ref, group):
    nodes, cols = acc_ref.shape
    blk = 128
    node_row = lax.broadcasted_iota(jnp.int32, (blk, blk), 0).astype(F32)
    for part in range(group):
        tile = ids_ref[part].astype(F32)
        fine = tile[half : half + 1, :]
        coarse = tile[2 + half : 3 + half, :]
        hot = jnp.where(node_row == fine, 1.0, 0.0).astype(BF16)
        for block in range(nodes // blk):
            keep = jnp.where(coarse == float(block), 1.0, 0.0).astype(BF16)
            hot_ref[block * blk : (block + 1) * blk, part * blk : (part + 1) * blk] = hot * keep
    rows = rows_ref[...].reshape(group * blk, cols)
    acc_ref[...] += jnp.dot(hot_ref[...], rows, preferred_element_type=F32)


def scatter_low_kernel(payload_ids_ref, rows_ref, sum_ref, hot_ref):
    @pl.when(pl.program_id(0) == 0)
    def _():
        sum_ref[...] = jnp.zeros(sum_ref.shape, F32)

    scatter_body(0, payload_ids_ref, rows_ref, hot_ref, sum_ref, rows_ref.shape[0])


def scatter_high_kernel(
    ids_ref, rows_ref, coarse_ref, init_ref, degree_ref, mean_ref, hot_ref, both_ref, acc_ref
):
    step = pl.program_id(0)
    group, blk, cols = rows_ref.shape
    half_nodes = acc_ref.shape[0]
    half_blocks = half_nodes // blk

    @pl.when(step == 0)
    def _():
        acc_ref[:, :cols] = init_ref[:half_nodes]
        acc_ref[:, cols:] = init_ref[half_nodes:]

    node_row = lax.broadcasted_iota(jnp.int32, (blk, blk), 0).astype(F32)
    for part in range(group):
        tile = ids_ref[part].astype(F32)
        fine = tile[1:2, :]
        coarse = tile[3:4, :]
        coarse = jnp.where(coarse >= half_blocks, coarse - half_blocks, coarse)
        hot = jnp.where(node_row == fine, 1.0, 0.0).astype(BF16)
        here = slice(part * blk, (part + 1) * blk)
        for block in range(half_blocks):
            keep = jnp.where(coarse == float(block), 1.0, 0.0).astype(BF16)
            hot_ref[block * blk : (block + 1) * blk, here] = hot * keep
        column = jnp.broadcast_to(coarse_ref[0, 0, :, part : part + 1], (blk, cols))
        upper = jnp.where(column >= half_blocks, 1.0, 0.0).astype(BF16)
        rows = rows_ref[part]
        both_ref[here, cols:] = rows * upper
        both_ref[here, :cols] = rows * (1.0 - upper)
    acc_ref[...] += jnp.dot(hot_ref[...], both_ref[...], preferred_element_type=F32)

    @pl.when(step == pl.num_programs(0) - 1)
    def _():
        mean_ref[:half_nodes] = (acc_ref[:, :cols] / degree_ref[:half_nodes]).astype(BF16)
        mean_ref[half_nodes:] = (acc_ref[:, cols:] / degree_ref[half_nodes:]).astype(BF16)


def scatter_low(low, nodes):
    parts, height, cols = low.shape
    group, blk = 8, 128
    return pl.pallas_call(
        scatter_low_kernel,
        grid=(parts // group,),
        in_specs=[
            pl.BlockSpec((group, ID_ROWS, cols), lambda i: (i, blk // ID_ROWS, 0)),
            pl.BlockSpec((group, blk, cols), lambda i: (i, 0, 0)),
        ],
        out_specs=full_spec((nodes, cols)),
        out_shape=jax.ShapeDtypeStruct((nodes, cols), F32),
        scratch_shapes=[pltpu.VMEM((nodes, group * blk), BF16)],
        compiler_params=params(1),
        name="scatter_low",
    )(low, low)


def scatter_high(low, high, columns, partial_sum, degrees):
    parts, blk, cols = high.shape
    nodes = partial_sum.shape[0]
    group = columns.shape[3]
    return pl.pallas_call(
        scatter_high_kernel,
        grid=(parts // group,),
        in_specs=[
            pl.BlockSpec((group, ID_ROWS, cols), lambda i: (i, blk // ID_ROWS, 0)),
            pl.BlockSpec((group, blk, cols), lambda i: (i, 0, 0)),
            pl.BlockSpec((1, 1, blk, group), lambda i: (3, i, 0, 0)),
            full_spec((nodes, cols)),
            full_spec((nodes, 1)),
        ],
        out_specs=full_spec((nodes, cols)),
        out_shape=jax.ShapeDtypeStruct((nodes, cols), BF16),
        scratch_shapes=[
            pltpu.VMEM((nodes // 2, group * blk), BF16),
            pltpu.VMEM((group * blk, 2 * cols), BF16),
            pltpu.VMEM((nodes // 2, 2 * cols), F32),
        ],
        compiler_params=params(1),
        name="scatter_high",
    )(low, high, columns, partial_sum, degrees)


def gather_kernel(fine_ref, coarse_ref, back_ref, out_ref, hot_ref):
    group, blk, cols = out_ref.shape
    half_nodes = back_ref.shape[0] // 2
    half_blocks = half_nodes // blk
    lane = lax.broadcasted_iota(jnp.int32, (blk, blk), 1).astype(F32)
    for part in range(group):
        fine = jnp.broadcast_to(fine_ref[0, 0, :, part : part + 1], (blk, blk))
        coarse = jnp.broadcast_to(coarse_ref[0, 0, :, part : part + 1], (blk, blk))
        coarse = jnp.where(coarse >= half_blocks, coarse - half_blocks, coarse)
        hot = jnp.where(lane == fine, 1.0, 0.0)
        for block in range(half_blocks):
            value = jnp.where(coarse == float(block), hot, 0.0).astype(BF16)
            hot_ref[part * blk : (part + 1) * blk, block * blk : (block + 1) * blk] = value
    both = jnp.concatenate([back_ref[:half_nodes], back_ref[half_nodes:]], axis=1)
    picked = jnp.dot(hot_ref[...], both, preferred_element_type=F32)
    for part in range(group):
        coarse = jnp.broadcast_to(coarse_ref[0, 0, :, part : part + 1], (blk, cols))
        here = slice(part * blk, (part + 1) * blk)
        rows = jnp.where(coarse >= half_blocks, picked[here, cols:], picked[here, :cols])
        out_ref[part] = rows.astype(BF16)


def gather_rows(half, columns, back):
    _, steps, blk, group = columns.shape
    nodes, cols = back.shape
    return pl.pallas_call(
        gather_kernel,
        grid=(steps,),
        in_specs=[
            pl.BlockSpec((1, 1, blk, group), lambda i: (half, i, 0, 0)),
            pl.BlockSpec((1, 1, blk, group), lambda i: (2 + half, i, 0, 0)),
            full_spec((nodes, cols)),
        ],
        out_specs=pl.BlockSpec((group, blk, cols), lambda i: (i, 0, 0)),
        out_shape=jax.ShapeDtypeStruct((steps * group, blk, cols), BF16),
        scratch_shapes=[pltpu.VMEM((group * blk, nodes // 2), BF16)],
        compiler_params=params(1),
        name="gather_rows",
    )(columns, columns, back)


def own_term_kernel(at_ref, feat_ref, weight_ref, out_ref):
    pieces = feat_ref.shape[0]
    rows = jnp.concatenate([feat_ref[piece] for piece in range(pieces)], axis=1)
    out_ref[...] = jnp.dot(rows, weight_ref[...], preferred_element_type=F32)


def own_term(at, feat_all, w_self, share):
    pieces, _, cols = feat_all.shape
    wide = w_self.shape[1]
    tile = 256
    return pl.pallas_call(
        own_term_kernel,
        grid_spec=pltpu.PrefetchScalarGridSpec(
            num_scalar_prefetch=1,
            grid=(wide // tile,),
            in_specs=[
                pl.BlockSpec((pieces, share, cols), lambda i, at: (0, at[0], 0)),
                pl.BlockSpec((pieces * cols, tile), lambda i, at: (0, i)),
            ],
            out_specs=pl.BlockSpec((share, tile), lambda i, at: (0, i)),
        ),
        out_shape=jax.ShapeDtypeStruct((share, wide), F32),
        compiler_params=params(1),
        name="own_term",
    )(at, feat_all, w_self)


def dense_kernel(
    at_ref, mean_ref, own_ref, cot_ref, weight_ref, degree_ref, back_ref, hidden_ref, grad_ref, acc_ref
):
    step = pl.program_id(0)
    pieces, rows, cols = mean_ref.shape
    tile = weight_ref.shape[1]
    mean = jnp.concatenate([mean_ref[piece] for piece in range(pieces)], axis=1)
    pre_act = own_ref[...] + jnp.dot(mean, weight_ref[...], preferred_element_type=F32)
    sig = jax.nn.sigmoid(pre_act)
    cot = jnp.concatenate([cot_ref[piece] for piece in range(cot_ref.shape[0])], axis=1)
    slope = sig * (1.0 + pre_act * (1.0 - sig))
    grad = (cot.astype(F32) * slope).astype(BF16)
    hidden = (pre_act * sig).astype(BF16)
    grad_ref[...] = grad
    for piece in range(tile // cols):
        hidden_ref[piece] = hidden[:, piece * cols : (piece + 1) * cols]
    update = lax.dot_general(
        grad, weight_ref[...], (((1,), (1,)), ((), ())), preferred_element_type=F32
    )

    @pl.when(step == 0)
    def _():
        acc_ref[...] = update

    @pl.when(step > 0)
    def _():
        acc_ref[...] += update

    @pl.when(step == pl.num_programs(0) - 1)
    def _():
        back = (acc_ref[...] / degree_ref[...]).astype(BF16)
        for piece in range(pieces):
            back_ref[piece] = back[:, piece * cols : (piece + 1) * cols]


def dense(at, mean_pieces, own, cot_all, w_neigh, degrees):
    pieces, rows, cols = mean_pieces.shape
    wide = w_neigh.shape[1]
    tile = 256
    per = tile // cols
    return pl.pallas_call(
        dense_kernel,
        grid_spec=pltpu.PrefetchScalarGridSpec(
            num_scalar_prefetch=1,
            grid=(wide // tile,),
            in_specs=[
                full_spec((pieces, rows, cols)),
                pl.BlockSpec((rows, tile), lambda i, at: (0, i)),
                pl.BlockSpec((per, rows, cols), lambda i, at: (i, at[0], 0)),
                pl.BlockSpec((pieces * cols, tile), lambda i, at: (0, i)),
                pl.BlockSpec((rows, 1), lambda i, at: (at[0], 0)),
            ],
            out_specs=[
                full_spec((pieces, rows, cols)),
                pl.BlockSpec((per, rows, cols), lambda i, at: (i, 0, 0)),
                pl.BlockSpec((rows, tile), lambda i, at: (0, i)),
            ],
            scratch_shapes=[pltpu.VMEM((rows, wide), F32)],
        ),
        out_shape=[
            jax.ShapeDtypeStruct((pieces, rows, cols), BF16),
            jax.ShapeDtypeStruct((pieces, rows, cols), BF16),
            jax.ShapeDtypeStruct((rows, wide), BF16),
        ],
        compiler_params=params(1),
        name="dense",
    )(at, mean_pieces, own, cot_all, w_neigh, degrees)


def backward_blocks_kernel(
    source_ref, slot_ref, low_ref, high_ref, adj_ref, self_ref, out_ref, both_ref, acc_ref
):
    step = pl.program_id(0)
    chunk, blk, _ = adj_ref.shape
    parts = low_ref.shape[0]

    @pl.when(step == 0)
    def _():
        acc_ref[...] = self_ref[...]
        for part in range(parts):
            both_ref[2 * part] = low_ref[part]
            both_ref[2 * part + 1] = high_ref[part]

    for item in range(chunk):
        block = step * chunk + item
        start = pl.multiple_of(source_ref[block] * blk, blk)
        product = jnp.dot(
            adj_ref[item], both_ref[slot_ref[block]], preferred_element_type=F32
        )
        acc_ref[pl.ds(start, blk), :] += product

    @pl.when(step == pl.num_programs(0) - 1)
    def _():
        out_ref[...] = acc_ref[...].astype(BF16)


def backward_blocks(block_source, block_to_slot, low, high, adjacency_t, self_grad):
    blocks, blk, _ = adjacency_t.shape
    nodes, cols = self_grad.shape
    parts = low.shape[0]
    chunk = 16
    return pl.pallas_call(
        backward_blocks_kernel,
        grid_spec=pltpu.PrefetchScalarGridSpec(
            num_scalar_prefetch=2,
            grid=(blocks // chunk,),
            in_specs=[
                full_spec((parts, blk, cols)),
                full_spec((parts, blk, cols)),
                pl.BlockSpec((chunk, blk, blk), lambda i, *unused: (i, 0, 0)),
                full_spec((nodes, cols)),
            ],
            out_specs=full_spec((nodes, cols)),
            scratch_shapes=[
                pltpu.VMEM((2 * parts, blk, cols), BF16),
                pltpu.VMEM((nodes, cols), F32),
            ],
        ),
        out_shape=jax.ShapeDtypeStruct((nodes, cols), BF16),
        compiler_params=params(1),
        name="backward_blocks",
    )(block_source, block_to_slot, low, high, adjacency_t, self_grad)


def swap(value, axis):
    return lax.all_to_all(value, axis, split_axis=0, concat_axis=0, tiled=True)


def after(value, *others):
    return lax.optimization_barrier((value, *others))[0]


def rotate(value, axis, distance):
    size = lax.axis_size(axis)
    return lax.ppermute(value, axis, [(i, (i + distance) % size) for i in range(size)])


def scatter_sum(pieces, axis):
    size, at = lax.axis_size(axis), lax.axis_index(axis)
    take = functools.partial(lax.dynamic_index_in_dim, pieces, axis=0, keepdims=False)
    total = take(at).astype(F32)
    came = [rotate(take((at + d) % size), axis, d) for d in range(1, size)]
    for piece in came:
        total = total + piece.astype(F32)
    return total.astype(BF16)


def around(piece, axis):
    size = lax.axis_size(axis)
    return [piece] + [rotate(piece, axis, size - i) for i in range(1, size)]


def exchange_sum(value, axis, distance, *beside):
    size = lax.axis_size(axis)
    other = lax.ppermute(value, axis, [(i, i ^ distance) for i in range(size)])
    other = after(other, *beside)
    return (value.astype(F32) + other.astype(F32)).astype(BF16)


def assemble_kernel(at_ref, *refs):
    *piece_refs, first_ref, second_ref = refs
    size = len(piece_refs)
    half = size // 2
    for i, piece_ref in enumerate(piece_refs):
        place = (at_ref[0] + i) % size
        value = piece_ref[...].astype(F32)

        @pl.when(place < half)
        def _():
            first_ref[place] = value

        @pl.when(place >= half)
        def _():
            second_ref[place - half] = value


def assemble(at, pieces):
    rows, wide = pieces[0].shape
    half = len(pieces) // 2
    first, second = pl.pallas_call(
        assemble_kernel,
        grid_spec=pltpu.PrefetchScalarGridSpec(
            num_scalar_prefetch=1,
            grid=(1,),
            in_specs=[full_spec((rows, wide))] * len(pieces),
            out_specs=[full_spec((half, rows, wide))] * 2,
        ),
        out_shape=[jax.ShapeDtypeStruct((half, rows, wide), F32)] * 2,
        compiler_params=params(1),
        name="assemble",
    )(at, *pieces)
    return first.reshape(half * rows, wide), second.reshape(half * rows, wide)


def on_device(
    features,
    w_self,
    w_neigh,
    adjacency,
    block_source,
    block_to_slot,
    send_rows,
    send_counts,
    degree,
    cotangent,
):
    node_rows, feat_cols = features.shape
    feat_size = lax.axis_size("feat")
    feat_at = lax.axis_index("feat")
    at = jnp.full((1,), feat_at, jnp.int32)
    share = node_rows // feat_size
    graph = ("z", "y")
    low, high = forward_blocks(
        block_source, block_to_slot, send_counts[0], send_rows[0], features, adjacency
    )
    low_in = swap(low, graph)
    high_in = swap(high, graph)
    feat_all = lax.all_gather(features, "feat", axis=0)
    cot_all = lax.all_gather(cotangent, "feat", axis=0)
    degrees = degree.astype(F32)[:, None]
    adjacency_t = after(adjacency, low_in).swapaxes(1, 2)
    self_rows = lax.dynamic_slice_in_dim(w_self, feat_at * feat_cols, feat_cols, 0)

    partial_sum = scatter_low(low_in, node_rows)
    blk = adjacency.shape[1]
    parts = low.shape[0]
    ids = low_in[:, blk : blk + 4, :].astype(F32).reshape(parts // 8, 8, 4, blk).transpose(2, 0, 3, 1)
    own = own_term(at, feat_all, w_self, share)
    partial_sum, adjacency_t, ids, own = lax.optimization_barrier(
        (partial_sum, adjacency_t, ids, own)
    )
    neighbor_mean = scatter_high(low_in, high_in, ids, partial_sum, degrees)
    mean_pieces = swap(neighbor_mean.reshape(feat_size, share, feat_cols), "feat")
    back_pieces, hidden_pieces, grad_pre = dense(at, mean_pieces, own, cot_all, w_neigh, degrees)
    back_rows = swap(back_pieces, "feat").reshape(node_rows, feat_cols)
    back_rows, grad_pre, hidden_pieces = lax.optimization_barrier(
        (back_rows, grad_pre, hidden_pieces)
    )
    rows_low = gather_rows(0, ids, back_rows)
    rows_high = gather_rows(1, ids, back_rows)
    back_low = swap(rows_low, graph)
    back_high = swap(rows_high, graph)
    grad_full = lax.all_gather(grad_pre, "feat", axis=0, tiled=True)
    grad_full = after(grad_full, rows_high, back_low)

    both = jnp.concatenate([features, neighbor_mean], axis=1)
    weight_part = lax.dot_general(
        both, grad_full, (((0,), (0,)), ((), ())), preferred_element_type=F32
    ).astype(BF16)
    hidden_all = lax.all_gather(after(hidden_pieces, weight_part), "feat", axis=0)
    hidden_out = lax.dynamic_index_in_dim(hidden_all, feat_at, 1, keepdims=False)
    hidden_out = hidden_out.reshape(node_rows, feat_cols)
    self_grad = lax.dot_general(
        grad_full, self_rows, (((1,), (1,)), ((), ())), preferred_element_type=F32
    )
    over_y = lax.axis_size("y")
    part = weight_part.reshape(over_y, 2 * feat_cols // over_y, weight_part.shape[1])
    part = after(scatter_sum(part, "y"), self_grad)
    part = exchange_sum(part, "z", 4)
    part = exchange_sum(part, "z", 2)
    part = after(part, back_high)
    part = exchange_sum(part, "z", 1, hidden_out)
    grad_features = backward_blocks(
        block_source, block_to_slot, back_low, back_high, adjacency_t, self_grad
    )
    grad_self, grad_neigh = assemble(
        jnp.full((1,), lax.axis_index("y"), jnp.int32), around(part, "y")
    )
    return hidden_out, grad_features, grad_self, grad_neigh


def solution(mesh):
    split = Mesh(mesh.devices.reshape(8, 4, 8), ("z", "y", "feat"))
    graph = ("z", "y")
    placed = (
        P(graph, "feat"),
        P(),
        P(),
        P(graph, None, None),
        P(graph),
        P(graph),
        P(graph, None, None),
        P(graph, None),
        P(graph),
        P(graph, "feat"),
    )
    return jax.shard_map(
        on_device,
        mesh=split,
        in_specs=placed,
        out_specs=(P(graph, "feat"), P(graph, "feat"), P("feat", None), P("feat", None)),
        check_vma=False,
    )
```

```python
import functools

import jax
import jax.numpy as jnp
from jax import lax
from jax.experimental import pallas as pl
from jax.experimental.pallas import tpu as pltpu
from jax.sharding import Mesh, PartitionSpec as P

BF16 = jnp.bfloat16
F32 = jnp.float32
VMEM_BYTES = 20 * 1024 * 1024
ID_ROWS = 8


def params(axes=0):
    return pltpu.CompilerParams(
        dimension_semantics=("arbitrary",) * axes if axes else None, vmem_limit_bytes=VMEM_BYTES
    )


def full_spec(shape):
    return pl.BlockSpec(shape, lambda *unused: (0,) * len(shape))


def forward_blocks_kernel(
    source_ref, slot_ref, count_ref, rows_ref, feat_ref, adj_ref, low_ref, high_ref, sums_ref
):
    step = pl.program_id(0)
    chunk, blk, _ = adj_ref.shape
    parts = low_ref.shape[0]
    cols = feat_ref.shape[1]

    @pl.when(step == 0)
    def _():
        sums_ref[...] = jnp.zeros(sums_ref.shape, F32)

    for item in range(chunk):
        block = step * chunk + item
        start = pl.multiple_of(source_ref[block] * blk, blk)
        product = jnp.dot(
            adj_ref[item], feat_ref[pl.ds(start, blk), :], preferred_element_type=F32
        )
        sums_ref[slot_ref[block]] += product

    @pl.when(step == pl.num_programs(0) - 1)
    def _():
        slot_row = lax.broadcasted_iota(jnp.int32, (blk, cols), 0)
        lane = lax.broadcasted_iota(jnp.int32, (1, 2 * blk), 1)
        tile_row = lax.broadcasted_iota(jnp.int32, (ID_ROWS, blk), 0)

        def emit(part, carry):
            count = count_ref[part]
            low = jnp.where(slot_row < count, sums_ref[2 * part], 0.0)
            high = jnp.where(slot_row + blk < count, sums_ref[2 * part + 1], 0.0)
            low_ref[part, 0:blk, :] = low.astype(BF16)
            high_ref[part] = high.astype(BF16)
            ids = rows_ref[pl.ds(part, 1), :]
            live = lane < count
            fine = jnp.where(live, ids & (blk - 1), -1).astype(F32)
            coarse = jnp.where(live, ids >> 7, -1).astype(F32)
            tile = jnp.where(tile_row == 0, fine[:, :blk], 0.0)
            tile = jnp.where(tile_row == 1, fine[:, blk:], tile)
            tile = jnp.where(tile_row == 2, coarse[:, :blk], tile)
            tile = jnp.where(tile_row == 3, coarse[:, blk:], tile)
            low_ref[part, blk : blk + ID_ROWS, :] = tile.astype(BF16)
            return carry

        lax.fori_loop(0, parts, emit, 0)


def forward_blocks(block_source, block_to_slot, counts, rows, features, adjacency):
    blocks, blk, _ = adjacency.shape
    nodes, cols = features.shape
    parts, cap = rows.shape
    chunk = 16
    return pl.pallas_call(
        forward_blocks_kernel,
        grid_spec=pltpu.PrefetchScalarGridSpec(
            num_scalar_prefetch=3,
            grid=(blocks // chunk,),
            in_specs=[
                full_spec((parts, cap)),
                full_spec((nodes, cols)),
                pl.BlockSpec((chunk, blk, blk), lambda i, *unused: (i, 0, 0)),
            ],
            out_specs=[full_spec((parts, blk + ID_ROWS, cols)), full_spec((parts, blk, cols))],
            scratch_shapes=[pltpu.VMEM((parts * cap // blk, blk, cols), F32)],
        ),
        out_shape=[
            jax.ShapeDtypeStruct((parts, blk + ID_ROWS, cols), BF16),
            jax.ShapeDtypeStruct((parts, blk, cols), BF16),
        ],
        compiler_params=params(1),
        name="forward_blocks",
    )(block_source, block_to_slot, counts, rows, features, adjacency)


def scatter_body(half, ids_ref, rows_ref, hot_ref, acc_ref, group):
    nodes, cols = acc_ref.shape
    blk = 128
    node_row = lax.broadcasted_iota(jnp.int32, (blk, blk), 0).astype(F32)
    for part in range(group):
        tile = ids_ref[part].astype(F32)
        fine = tile[half : half + 1, :]
        coarse = tile[2 + half : 3 + half, :]
        hot = jnp.where(node_row == fine, 1.0, 0.0).astype(BF16)
        for block in range(nodes // blk):
            keep = jnp.where(coarse == float(block), 1.0, 0.0).astype(BF16)
            hot_ref[block * blk : (block + 1) * blk, part * blk : (part + 1) * blk] = hot * keep
    rows = rows_ref[...].reshape(group * blk, cols)
    acc_ref[...] += jnp.dot(hot_ref[...], rows, preferred_element_type=F32)


def scatter_low_kernel(payload_ids_ref, rows_ref, sum_ref, hot_ref):
    @pl.when(pl.program_id(0) == 0)
    def _():
        sum_ref[...] = jnp.zeros(sum_ref.shape, F32)

    scatter_body(0, payload_ids_ref, rows_ref, hot_ref, sum_ref, rows_ref.shape[0])


def scatter_high_kernel(
    ids_ref, rows_ref, coarse_ref, init_ref, degree_ref, mean_ref, hot_ref, both_ref, acc_ref
):
    step = pl.program_id(0)
    group, blk, cols = rows_ref.shape
    half_nodes = acc_ref.shape[0]
    half_blocks = half_nodes // blk

    @pl.when(step == 0)
    def _():
        acc_ref[:, :cols] = init_ref[:half_nodes]
        acc_ref[:, cols:] = init_ref[half_nodes:]

    node_row = lax.broadcasted_iota(jnp.int32, (blk, blk), 0).astype(F32)
    for part in range(group):
        tile = ids_ref[part].astype(F32)
        fine = tile[1:2, :]
        coarse = tile[3:4, :]
        coarse = jnp.where(coarse >= half_blocks, coarse - half_blocks, coarse)
        hot = jnp.where(node_row == fine, 1.0, 0.0).astype(BF16)
        here = slice(part * blk, (part + 1) * blk)
        for block in range(half_blocks):
            keep = jnp.where(coarse == float(block), 1.0, 0.0).astype(BF16)
            hot_ref[block * blk : (block + 1) * blk, here] = hot * keep
        column = jnp.broadcast_to(coarse_ref[0, 0, :, part : part + 1], (blk, cols))
        upper = jnp.where(column >= half_blocks, 1.0, 0.0).astype(BF16)
        rows = rows_ref[part]
        both_ref[here, cols:] = rows * upper
        both_ref[here, :cols] = rows * (1.0 - upper)
    acc_ref[...] += jnp.dot(hot_ref[...], both_ref[...], preferred_element_type=F32)

    @pl.when(step == pl.num_programs(0) - 1)
    def _():
        mean_ref[:half_nodes] = (acc_ref[:, :cols] / degree_ref[:half_nodes]).astype(BF16)
        mean_ref[half_nodes:] = (acc_ref[:, cols:] / degree_ref[half_nodes:]).astype(BF16)


def scatter_low(low, nodes):
    parts, height, cols = low.shape
    group, blk = 8, 128
    return pl.pallas_call(
        scatter_low_kernel,
        grid=(parts // group,),
        in_specs=[
            pl.BlockSpec((group, ID_ROWS, cols), lambda i: (i, blk // ID_ROWS, 0)),
            pl.BlockSpec((group, blk, cols), lambda i: (i, 0, 0)),
        ],
        out_specs=full_spec((nodes, cols)),
        out_shape=jax.ShapeDtypeStruct((nodes, cols), F32),
        scratch_shapes=[pltpu.VMEM((nodes, group * blk), BF16)],
        compiler_params=params(1),
        name="scatter_low",
    )(low, low)


def scatter_high(low, high, columns, partial_sum, degrees):
    parts, blk, cols = high.shape
    nodes = partial_sum.shape[0]
    group = columns.shape[3]
    return pl.pallas_call(
        scatter_high_kernel,
        grid=(parts // group,),
        in_specs=[
            pl.BlockSpec((group, ID_ROWS, cols), lambda i: (i, blk // ID_ROWS, 0)),
            pl.BlockSpec((group, blk, cols), lambda i: (i, 0, 0)),
            pl.BlockSpec((1, 1, blk, group), lambda i: (3, i, 0, 0)),
            full_spec((nodes, cols)),
            full_spec((nodes, 1)),
        ],
        out_specs=full_spec((nodes, cols)),
        out_shape=pltpu.HBM((nodes, cols), BF16),
        scratch_shapes=[
            pltpu.VMEM((nodes // 2, group * blk), BF16),
            pltpu.VMEM((group * blk, 2 * cols), BF16),
            pltpu.VMEM((nodes // 2, 2 * cols), F32),
        ],
        compiler_params=params(1),
        name="scatter_high",
    )(low, high, columns, partial_sum, degrees)


def gather_kernel(fine_ref, coarse_ref, back_ref, out_ref, hot_ref):
    group, blk, cols = out_ref.shape
    half_nodes = back_ref.shape[0] // 2
    half_blocks = half_nodes // blk
    lane = lax.broadcasted_iota(jnp.int32, (blk, blk), 1).astype(F32)
    for part in range(group):
        fine = jnp.broadcast_to(fine_ref[0, 0, :, part : part + 1], (blk, blk))
        coarse = jnp.broadcast_to(coarse_ref[0, 0, :, part : part + 1], (blk, blk))
        coarse = jnp.where(coarse >= half_blocks, coarse - half_blocks, coarse)
        hot = jnp.where(lane == fine, 1.0, 0.0)
        for block in range(half_blocks):
            value = jnp.where(coarse == float(block), hot, 0.0).astype(BF16)
            hot_ref[part * blk : (part + 1) * blk, block * blk : (block + 1) * blk] = value
    both = jnp.concatenate([back_ref[:half_nodes], back_ref[half_nodes:]], axis=1)
    picked = jnp.dot(hot_ref[...], both, preferred_element_type=F32)
    for part in range(group):
        coarse = jnp.broadcast_to(coarse_ref[0, 0, :, part : part + 1], (blk, cols))
        here = slice(part * blk, (part + 1) * blk)
        rows = jnp.where(coarse >= half_blocks, picked[here, cols:], picked[here, :cols])
        out_ref[part] = rows.astype(BF16)


def gather_rows(half, columns, back):
    _, steps, blk, group = columns.shape
    nodes, cols = back.shape
    return pl.pallas_call(
        gather_kernel,
        grid=(steps,),
        in_specs=[
            pl.BlockSpec((1, 1, blk, group), lambda i: (half, i, 0, 0)),
            pl.BlockSpec((1, 1, blk, group), lambda i: (2 + half, i, 0, 0)),
            full_spec((nodes, cols)),
        ],
        out_specs=pl.BlockSpec((group, blk, cols), lambda i: (i, 0, 0)),
        out_shape=pltpu.HBM((steps * group, blk, cols), BF16),
        scratch_shapes=[pltpu.VMEM((group * blk, nodes // 2), BF16)],
        compiler_params=params(1),
        name="gather_rows",
    )(columns, columns, back)


def own_term_kernel(at_ref, feat_ref, weight_ref, out_ref):
    pieces = feat_ref.shape[0]
    rows = jnp.concatenate([feat_ref[piece] for piece in range(pieces)], axis=1)
    out_ref[...] = jnp.dot(rows, weight_ref[...], preferred_element_type=F32)


def own_term(at, feat_all, w_self, share):
    pieces, _, cols = feat_all.shape
    wide = w_self.shape[1]
    tile = 256
    return pl.pallas_call(
        own_term_kernel,
        grid_spec=pltpu.PrefetchScalarGridSpec(
            num_scalar_prefetch=1,
            grid=(wide // tile,),
            in_specs=[
                pl.BlockSpec((pieces, share, cols), lambda i, at: (0, at[0], 0)),
                pl.BlockSpec((pieces * cols, tile), lambda i, at: (0, i)),
            ],
            out_specs=pl.BlockSpec((share, tile), lambda i, at: (0, i)),
        ),
        out_shape=jax.ShapeDtypeStruct((share, wide), F32),
        compiler_params=params(1),
        name="own_term",
    )(at, feat_all, w_self)


def dense_kernel(
    at_ref, mean_ref, own_ref, cot_ref, weight_ref, degree_ref, back_ref, hidden_ref, grad_ref, acc_ref
):
    step = pl.program_id(0)
    pieces, rows, cols = mean_ref.shape
    tile = weight_ref.shape[1]
    mean = jnp.concatenate([mean_ref[piece] for piece in range(pieces)], axis=1)
    pre_act = own_ref[...] + jnp.dot(mean, weight_ref[...], preferred_element_type=F32)
    sig = jax.nn.sigmoid(pre_act)
    cot = jnp.concatenate([cot_ref[piece] for piece in range(cot_ref.shape[0])], axis=1)
    slope = sig * (1.0 + pre_act * (1.0 - sig))
    grad = (cot.astype(F32) * slope).astype(BF16)
    hidden = (pre_act * sig).astype(BF16)
    grad_ref[...] = grad
    for piece in range(tile // cols):
        hidden_ref[piece] = hidden[:, piece * cols : (piece + 1) * cols]
    update = lax.dot_general(
        grad, weight_ref[...], (((1,), (1,)), ((), ())), preferred_element_type=F32
    )

    @pl.when(step == 0)
    def _():
        acc_ref[...] = update

    @pl.when(step > 0)
    def _():
        acc_ref[...] += update

    @pl.when(step == pl.num_programs(0) - 1)
    def _():
        back = (acc_ref[...] / degree_ref[...]).astype(BF16)
        for piece in range(pieces):
            back_ref[piece] = back[:, piece * cols : (piece + 1) * cols]


def dense(at, mean_pieces, own, cot_all, w_neigh, degrees):
    pieces, rows, cols = mean_pieces.shape
    wide = w_neigh.shape[1]
    tile = 256
    per = tile // cols
    return pl.pallas_call(
        dense_kernel,
        grid_spec=pltpu.PrefetchScalarGridSpec(
            num_scalar_prefetch=1,
            grid=(wide // tile,),
            in_specs=[
                full_spec((pieces, rows, cols)),
                pl.BlockSpec((rows, tile), lambda i, at: (0, i)),
                pl.BlockSpec((per, rows, cols), lambda i, at: (i, at[0], 0)),
                pl.BlockSpec((pieces * cols, tile), lambda i, at: (0, i)),
                pl.BlockSpec((rows, 1), lambda i, at: (at[0], 0)),
            ],
            out_specs=[
                full_spec((pieces, rows, cols)),
                pl.BlockSpec((per, rows, cols), lambda i, at: (i, 0, 0)),
                pl.BlockSpec((rows, tile), lambda i, at: (0, i)),
            ],
            scratch_shapes=[pltpu.VMEM((rows, wide), F32)],
        ),
        out_shape=[
            jax.ShapeDtypeStruct((pieces, rows, cols), BF16),
            jax.ShapeDtypeStruct((pieces, rows, cols), BF16),
            jax.ShapeDtypeStruct((rows, wide), BF16),
        ],
        compiler_params=params(1),
        name="dense",
    )(at, mean_pieces, own, cot_all, w_neigh, degrees)


def backward_blocks_kernel(
    source_ref, slot_ref, low_ref, high_ref, adj_ref, self_ref, out_ref, both_ref, acc_ref
):
    step = pl.program_id(0)
    chunk, blk, _ = adj_ref.shape
    parts = low_ref.shape[0]

    @pl.when(step == 0)
    def _():
        acc_ref[...] = self_ref[...]
        for part in range(parts):
            both_ref[2 * part] = low_ref[part]
            both_ref[2 * part + 1] = high_ref[part]

    for item in range(chunk):
        block = step * chunk + item
        start = pl.multiple_of(source_ref[block] * blk, blk)
        product = jnp.dot(
            adj_ref[item], both_ref[slot_ref[block]], preferred_element_type=F32
        )
        acc_ref[pl.ds(start, blk), :] += product

    @pl.when(step == pl.num_programs(0) - 1)
    def _():
        out_ref[...] = acc_ref[...].astype(BF16)


def backward_blocks(block_source, block_to_slot, low, high, adjacency_t, self_grad):
    blocks, blk, _ = adjacency_t.shape
    nodes, cols = self_grad.shape
    parts = low.shape[0]
    chunk = 16
    return pl.pallas_call(
        backward_blocks_kernel,
        grid_spec=pltpu.PrefetchScalarGridSpec(
            num_scalar_prefetch=2,
            grid=(blocks // chunk,),
            in_specs=[
                full_spec((parts, blk, cols)),
                full_spec((parts, blk, cols)),
                pl.BlockSpec((chunk, blk, blk), lambda i, *unused: (i, 0, 0)),
                full_spec((nodes, cols)),
            ],
            out_specs=full_spec((nodes, cols)),
            scratch_shapes=[
                pltpu.VMEM((2 * parts, blk, cols), BF16),
                pltpu.VMEM((nodes, cols), F32),
            ],
        ),
        out_shape=jax.ShapeDtypeStruct((nodes, cols), BF16),
        compiler_params=params(1),
        name="backward_blocks",
    )(block_source, block_to_slot, low, high, adjacency_t, self_grad)


def in_hbm(value):
    return pltpu.with_memory_space_constraint(value, pltpu.HBM)


def swap(value, axis):
    return lax.all_to_all(value, axis, split_axis=0, concat_axis=0, tiled=True)


def after(value, *others):
    return lax.optimization_barrier((value, *others))[0]


def rotate(value, axis, distance):
    size = lax.axis_size(axis)
    return lax.ppermute(value, axis, [(i, (i + distance) % size) for i in range(size)])


def scatter_sum(pieces, axis):
    size, at = lax.axis_size(axis), lax.axis_index(axis)
    take = functools.partial(lax.dynamic_index_in_dim, pieces, axis=0, keepdims=False)
    total = take(at).astype(F32)
    came = [rotate(take((at + d) % size), axis, d) for d in range(1, size)]
    for piece in came:
        total = total + piece.astype(F32)
    return total.astype(BF16)


def around(piece, axis):
    size = lax.axis_size(axis)
    return [piece] + [rotate(piece, axis, size - i) for i in range(1, size)]


def exchange_sum(value, axis, distance, *beside):
    size = lax.axis_size(axis)
    other = lax.ppermute(value, axis, [(i, i ^ distance) for i in range(size)])
    other = after(other, *beside)
    return (value.astype(F32) + other.astype(F32)).astype(BF16)


def assemble_kernel(at_ref, *refs):
    *piece_refs, first_ref, second_ref = refs
    size = len(piece_refs)
    half = size // 2
    for i, piece_ref in enumerate(piece_refs):
        place = (at_ref[0] + i) % size
        value = piece_ref[...].astype(F32)

        @pl.when(place < half)
        def _():
            first_ref[place] = value

        @pl.when(place >= half)
        def _():
            second_ref[place - half] = value


def assemble(at, pieces):
    rows, wide = pieces[0].shape
    half = len(pieces) // 2
    first, second = pl.pallas_call(
        assemble_kernel,
        grid_spec=pltpu.PrefetchScalarGridSpec(
            num_scalar_prefetch=1,
            grid=(1,),
            in_specs=[full_spec((rows, wide))] * len(pieces),
            out_specs=[full_spec((half, rows, wide))] * 2,
        ),
        out_shape=[jax.ShapeDtypeStruct((half, rows, wide), F32)] * 2,
        compiler_params=params(1),
        name="assemble",
    )(at, *pieces)
    return first.reshape(half * rows, wide), second.reshape(half * rows, wide)


def on_device(
    features,
    w_self,
    w_neigh,
    adjacency,
    block_source,
    block_to_slot,
    send_rows,
    send_counts,
    degree,
    cotangent,
):
    node_rows, feat_cols = features.shape
    feat_size = lax.axis_size("feat")
    feat_at = lax.axis_index("feat")
    at = jnp.full((1,), feat_at, jnp.int32)
    share = node_rows // feat_size
    graph = ("z", "y")
    low, high = forward_blocks(
        block_source,
        block_to_slot,
        send_counts[0],
        in_hbm(send_rows[0]),
        in_hbm(features),
        in_hbm(adjacency),
    )
    low_in = swap(low, graph)
    high_in = swap(high, graph)
    feat_all = lax.all_gather(features, "feat", axis=0)
    cot_all = lax.all_gather(cotangent, "feat", axis=0)
    degrees = degree.astype(F32)[:, None]
    adjacency_t = in_hbm(after(adjacency, low_in).swapaxes(1, 2))
    self_rows = lax.dynamic_slice_in_dim(w_self, feat_at * feat_cols, feat_cols, 0)

    partial_sum = scatter_low(low_in, node_rows)
    blk = adjacency.shape[1]
    parts = low.shape[0]
    ids = low_in[:, blk : blk + 4, :].astype(F32).reshape(parts // 8, 8, 4, blk).transpose(2, 0, 3, 1)
    own = own_term(at, in_hbm(feat_all), w_self, share)
    partial_sum, adjacency_t, ids, own = lax.optimization_barrier(
        (partial_sum, adjacency_t, ids, own)
    )
    neighbor_mean = scatter_high(low_in, high_in, ids, partial_sum, degrees)
    mean_pieces = swap(neighbor_mean.reshape(feat_size, share, feat_cols), "feat")
    back_pieces, hidden_pieces, grad_pre = dense(at, mean_pieces, own, in_hbm(cot_all), w_neigh, degrees)
    back_rows = swap(back_pieces, "feat").reshape(node_rows, feat_cols)
    back_rows, grad_pre, hidden_pieces = lax.optimization_barrier(
        (back_rows, grad_pre, hidden_pieces)
    )
    rows_low = gather_rows(0, ids, back_rows)
    rows_high = gather_rows(1, ids, back_rows)
    back_low = swap(rows_low, graph)
    grad_full = lax.all_gather(grad_pre, "feat", axis=0, tiled=True)
    grad_full = after(grad_full, rows_high)
    both = jnp.concatenate([features, neighbor_mean], axis=1)
    weight_part = lax.dot_general(
        both, grad_full, (((0,), (0,)), ((), ())), preferred_element_type=F32
    ).astype(BF16)
    over_y = lax.axis_size("y")
    part = weight_part.reshape(over_y, 2 * feat_cols // over_y, weight_part.shape[1])
    part = scatter_sum(part, "y")
    back_high = swap(after(rows_high, part, back_low), graph)

    hidden_all = lax.all_gather(after(hidden_pieces, rows_low), "feat", axis=0)
    hidden_out = lax.dynamic_index_in_dim(hidden_all, feat_at, 1, keepdims=False)
    hidden_out = hidden_out.reshape(node_rows, feat_cols)
    self_grad = lax.dot_general(
        grad_full, self_rows, (((1,), (1,)), ((), ())), preferred_element_type=F32
    )
    part = exchange_sum(part, "z", 4, self_grad)
    part = exchange_sum(part, "z", 2)
    part = exchange_sum(part, "z", 1, hidden_out)
    grad_features = backward_blocks(
        block_source, block_to_slot, back_low, back_high, adjacency_t, self_grad
    )
    grad_self, grad_neigh = assemble(
        jnp.full((1,), lax.axis_index("y"), jnp.int32), around(after(part, back_high), "y")
    )
    return hidden_out, grad_features, grad_self, grad_neigh


def solution(mesh):
    split = Mesh(mesh.devices.reshape(8, 4, 8), ("z", "y", "feat"))
    graph = ("z", "y")
    placed = (
        P(graph, "feat"),
        P(),
        P(),
        P(graph, None, None),
        P(graph),
        P(graph),
        P(graph, None, None),
        P(graph, None),
        P(graph),
        P(graph, "feat"),
    )
    return jax.shard_map(
        on_device,
        mesh=split,
        in_specs=placed,
        out_specs=(P(graph, "feat"), P(graph, "feat"), P("feat", None), P("feat", None)),
        check_vma=False,
    )
```

```python
import functools

import jax
import jax.numpy as jnp
from jax import lax
from jax.experimental import pallas as pl
from jax.experimental.pallas import tpu as pltpu
from jax.sharding import Mesh, PartitionSpec as P

BF16 = jnp.bfloat16
F32 = jnp.float32
VMEM_BYTES = 20 * 1024 * 1024
ID_ROWS = 8


def params(axes=0):
    return pltpu.CompilerParams(
        dimension_semantics=("arbitrary",) * axes if axes else None, vmem_limit_bytes=VMEM_BYTES
    )


def full_spec(shape):
    return pl.BlockSpec(shape, lambda *unused: (0,) * len(shape))


def forward_blocks_kernel(
    source_ref, slot_ref, count_ref, rows_ref, feat_ref, adj_ref, low_ref, high_ref, sums_ref
):
    step = pl.program_id(0)
    chunk, blk, _ = adj_ref.shape
    parts = low_ref.shape[0]
    cols = feat_ref.shape[1]

    @pl.when(step == 0)
    def _():
        sums_ref[...] = jnp.zeros(sums_ref.shape, F32)

    for item in range(chunk):
        block = step * chunk + item
        start = pl.multiple_of(source_ref[block] * blk, blk)
        product = jnp.dot(
            adj_ref[item], feat_ref[pl.ds(start, blk), :], preferred_element_type=F32
        )
        sums_ref[slot_ref[block]] += product

    @pl.when(step == pl.num_programs(0) - 1)
    def _():
        slot_row = lax.broadcasted_iota(jnp.int32, (blk, cols), 0)
        lane = lax.broadcasted_iota(jnp.int32, (1, 2 * blk), 1)
        tile_row = lax.broadcasted_iota(jnp.int32, (ID_ROWS, blk), 0)

        def emit(part, carry):
            count = count_ref[part]
            low = jnp.where(slot_row < count, sums_ref[2 * part], 0.0)
            high = jnp.where(slot_row + blk < count, sums_ref[2 * part + 1], 0.0)
            low_ref[part, 0:blk, :] = low.astype(BF16)
            high_ref[part] = high.astype(BF16)
            ids = rows_ref[pl.ds(part, 1), :]
            live = lane < count
            fine = jnp.where(live, ids & (blk - 1), -1).astype(F32)
            coarse = jnp.where(live, ids >> 7, -1).astype(F32)
            tile = jnp.where(tile_row == 0, fine[:, :blk], 0.0)
            tile = jnp.where(tile_row == 1, fine[:, blk:], tile)
            tile = jnp.where(tile_row == 2, coarse[:, :blk], tile)
            tile = jnp.where(tile_row == 3, coarse[:, blk:], tile)
            low_ref[part, blk : blk + ID_ROWS, :] = tile.astype(BF16)
            return carry

        lax.fori_loop(0, parts, emit, 0)


def forward_blocks(block_source, block_to_slot, counts, rows, features, adjacency):
    blocks, blk, _ = adjacency.shape
    nodes, cols = features.shape
    parts, cap = rows.shape
    chunk = 16
    return pl.pallas_call(
        forward_blocks_kernel,
        grid_spec=pltpu.PrefetchScalarGridSpec(
            num_scalar_prefetch=3,
            grid=(blocks // chunk,),
            in_specs=[
                full_spec((parts, cap)),
                full_spec((nodes, cols)),
                pl.BlockSpec((chunk, blk, blk), lambda i, *unused: (i, 0, 0)),
            ],
            out_specs=[full_spec((parts, blk + ID_ROWS, cols)), full_spec((parts, blk, cols))],
            scratch_shapes=[pltpu.VMEM((parts * cap // blk, blk, cols), F32)],
        ),
        out_shape=[
            jax.ShapeDtypeStruct((parts, blk + ID_ROWS, cols), BF16),
            jax.ShapeDtypeStruct((parts, blk, cols), BF16),
        ],
        compiler_params=params(1),
        name="forward_blocks",
    )(block_source, block_to_slot, counts, rows, features, adjacency)


def scatter_body(half, ids_ref, rows_ref, hot_ref, acc_ref, group):
    nodes, cols = acc_ref.shape
    blk = 128
    node_row = lax.broadcasted_iota(jnp.int32, (blk, blk), 0).astype(F32)
    for part in range(group):
        tile = ids_ref[part].astype(F32)
        fine = tile[half : half + 1, :]
        coarse = tile[2 + half : 3 + half, :]
        hot = jnp.where(node_row == fine, 1.0, 0.0).astype(BF16)
        for block in range(nodes // blk):
            keep = jnp.where(coarse == float(block), 1.0, 0.0).astype(BF16)
            hot_ref[block * blk : (block + 1) * blk, part * blk : (part + 1) * blk] = hot * keep
    rows = rows_ref[...].reshape(group * blk, cols)
    acc_ref[...] += jnp.dot(hot_ref[...], rows, preferred_element_type=F32)


def scatter_low_kernel(payload_ids_ref, rows_ref, sum_ref, hot_ref):
    @pl.when(pl.program_id(0) == 0)
    def _():
        sum_ref[...] = jnp.zeros(sum_ref.shape, F32)

    scatter_body(0, payload_ids_ref, rows_ref, hot_ref, sum_ref, rows_ref.shape[0])


def scatter_high_kernel(
    ids_ref, rows_ref, coarse_ref, init_ref, degree_ref, mean_ref, hot_ref, both_ref, acc_ref
):
    step = pl.program_id(0)
    group, blk, cols = rows_ref.shape
    half_nodes = acc_ref.shape[0]
    half_blocks = half_nodes // blk

    @pl.when(step == 0)
    def _():
        acc_ref[:, :cols] = init_ref[:half_nodes]
        acc_ref[:, cols:] = init_ref[half_nodes:]

    node_row = lax.broadcasted_iota(jnp.int32, (blk, blk), 0).astype(F32)
    for part in range(group):
        tile = ids_ref[part].astype(F32)
        fine = tile[1:2, :]
        coarse = tile[3:4, :]
        coarse = jnp.where(coarse >= half_blocks, coarse - half_blocks, coarse)
        hot = jnp.where(node_row == fine, 1.0, 0.0).astype(BF16)
        here = slice(part * blk, (part + 1) * blk)
        for block in range(half_blocks):
            keep = jnp.where(coarse == float(block), 1.0, 0.0).astype(BF16)
            hot_ref[block * blk : (block + 1) * blk, here] = hot * keep
        column = jnp.broadcast_to(coarse_ref[0, 0, :, part : part + 1], (blk, cols))
        upper = jnp.where(column >= half_blocks, 1.0, 0.0).astype(BF16)
        rows = rows_ref[part]
        both_ref[here, cols:] = rows * upper
        both_ref[here, :cols] = rows * (1.0 - upper)
    acc_ref[...] += jnp.dot(hot_ref[...], both_ref[...], preferred_element_type=F32)

    @pl.when(step == pl.num_programs(0) - 1)
    def _():
        mean_ref[:half_nodes] = (acc_ref[:, :cols] / degree_ref[:half_nodes]).astype(BF16)
        mean_ref[half_nodes:] = (acc_ref[:, cols:] / degree_ref[half_nodes:]).astype(BF16)


def scatter_low(low, nodes):
    parts, height, cols = low.shape
    group, blk = 8, 128
    return pl.pallas_call(
        scatter_low_kernel,
        grid=(parts // group,),
        in_specs=[
            pl.BlockSpec((group, ID_ROWS, cols), lambda i: (i, blk // ID_ROWS, 0)),
            pl.BlockSpec((group, blk, cols), lambda i: (i, 0, 0)),
        ],
        out_specs=full_spec((nodes, cols)),
        out_shape=pltpu.HBM((nodes, cols), F32),
        scratch_shapes=[pltpu.VMEM((nodes, group * blk), BF16)],
        compiler_params=params(1),
        name="scatter_low",
    )(low, low)


def scatter_high(low, high, columns, partial_sum, degrees):
    parts, blk, cols = high.shape
    nodes = partial_sum.shape[0]
    group = columns.shape[3]
    return pl.pallas_call(
        scatter_high_kernel,
        grid=(parts // group,),
        in_specs=[
            pl.BlockSpec((group, ID_ROWS, cols), lambda i: (i, blk // ID_ROWS, 0)),
            pl.BlockSpec((group, blk, cols), lambda i: (i, 0, 0)),
            pl.BlockSpec((1, 1, blk, group), lambda i: (3, i, 0, 0)),
            full_spec((nodes, cols)),
            full_spec((nodes, 1)),
        ],
        out_specs=full_spec((nodes, cols)),
        out_shape=pltpu.HBM((nodes, cols), BF16),
        scratch_shapes=[
            pltpu.VMEM((nodes // 2, group * blk), BF16),
            pltpu.VMEM((group * blk, 2 * cols), BF16),
            pltpu.VMEM((nodes // 2, 2 * cols), F32),
        ],
        compiler_params=params(1),
        name="scatter_high",
    )(low, high, columns, partial_sum, degrees)


def gather_kernel(fine_ref, coarse_ref, back_ref, out_ref, hot_ref):
    group, blk, cols = out_ref.shape
    half_nodes = back_ref.shape[0] // 2
    half_blocks = half_nodes // blk
    lane = lax.broadcasted_iota(jnp.int32, (blk, blk), 1).astype(F32)
    for part in range(group):
        fine = jnp.broadcast_to(fine_ref[0, 0, :, part : part + 1], (blk, blk))
        coarse = jnp.broadcast_to(coarse_ref[0, 0, :, part : part + 1], (blk, blk))
        coarse = jnp.where(coarse >= half_blocks, coarse - half_blocks, coarse)
        hot = jnp.where(lane == fine, 1.0, 0.0)
        for block in range(half_blocks):
            value = jnp.where(coarse == float(block), hot, 0.0).astype(BF16)
            hot_ref[part * blk : (part + 1) * blk, block * blk : (block + 1) * blk] = value
    both = jnp.concatenate([back_ref[:half_nodes], back_ref[half_nodes:]], axis=1)
    picked = jnp.dot(hot_ref[...], both, preferred_element_type=F32)
    for part in range(group):
        coarse = jnp.broadcast_to(coarse_ref[0, 0, :, part : part + 1], (blk, cols))
        here = slice(part * blk, (part + 1) * blk)
        rows = jnp.where(coarse >= half_blocks, picked[here, cols:], picked[here, :cols])
        out_ref[part] = rows.astype(BF16)


def gather_rows(half, columns, back):
    _, steps, blk, group = columns.shape
    nodes, cols = back.shape
    return pl.pallas_call(
        gather_kernel,
        grid=(steps,),
        in_specs=[
            pl.BlockSpec((1, 1, blk, group), lambda i: (half, i, 0, 0)),
            pl.BlockSpec((1, 1, blk, group), lambda i: (2 + half, i, 0, 0)),
            full_spec((nodes, cols)),
        ],
        out_specs=pl.BlockSpec((group, blk, cols), lambda i: (i, 0, 0)),
        out_shape=pltpu.HBM((steps * group, blk, cols), BF16),
        scratch_shapes=[pltpu.VMEM((group * blk, nodes // 2), BF16)],
        compiler_params=params(1),
        name="gather_rows",
    )(columns, columns, back)


def own_term_kernel(at_ref, feat_ref, weight_ref, out_ref):
    pieces = feat_ref.shape[0]
    rows = jnp.concatenate([feat_ref[piece] for piece in range(pieces)], axis=1)
    out_ref[...] = jnp.dot(rows, weight_ref[...], preferred_element_type=F32)


def own_term(at, feat_all, w_self, share):
    pieces, _, cols = feat_all.shape
    wide = w_self.shape[1]
    tile = 256
    return pl.pallas_call(
        own_term_kernel,
        grid_spec=pltpu.PrefetchScalarGridSpec(
            num_scalar_prefetch=1,
            grid=(wide // tile,),
            in_specs=[
                pl.BlockSpec((pieces, share, cols), lambda i, at: (0, at[0], 0)),
                pl.BlockSpec((pieces * cols, tile), lambda i, at: (0, i)),
            ],
            out_specs=pl.BlockSpec((share, tile), lambda i, at: (0, i)),
        ),
        out_shape=pltpu.HBM((share, wide), F32),
        compiler_params=params(1),
        name="own_term",
    )(at, feat_all, w_self)


def dense_kernel(
    at_ref, mean_ref, own_ref, cot_ref, weight_ref, degree_ref, back_ref, hidden_ref, grad_ref, acc_ref
):
    step = pl.program_id(0)
    pieces, rows, cols = mean_ref.shape
    tile = weight_ref.shape[1]
    mean = jnp.concatenate([mean_ref[piece] for piece in range(pieces)], axis=1)
    pre_act = own_ref[...] + jnp.dot(mean, weight_ref[...], preferred_element_type=F32)
    sig = jax.nn.sigmoid(pre_act)
    cot = jnp.concatenate([cot_ref[piece] for piece in range(cot_ref.shape[0])], axis=1)
    slope = sig * (1.0 + pre_act * (1.0 - sig))
    grad = (cot.astype(F32) * slope).astype(BF16)
    hidden = (pre_act * sig).astype(BF16)
    grad_ref[...] = grad
    for piece in range(tile // cols):
        hidden_ref[piece] = hidden[:, piece * cols : (piece + 1) * cols]
    update = lax.dot_general(
        grad, weight_ref[...], (((1,), (1,)), ((), ())), preferred_element_type=F32
    )

    @pl.when(step == 0)
    def _():
        acc_ref[...] = update

    @pl.when(step > 0)
    def _():
        acc_ref[...] += update

    @pl.when(step == pl.num_programs(0) - 1)
    def _():
        back = (acc_ref[...] / degree_ref[...]).astype(BF16)
        for piece in range(pieces):
            back_ref[piece] = back[:, piece * cols : (piece + 1) * cols]


def dense(at, mean_pieces, own, cot_all, w_neigh, degrees):
    pieces, rows, cols = mean_pieces.shape
    wide = w_neigh.shape[1]
    tile = 256
    per = tile // cols
    return pl.pallas_call(
        dense_kernel,
        grid_spec=pltpu.PrefetchScalarGridSpec(
            num_scalar_prefetch=1,
            grid=(wide // tile,),
            in_specs=[
                full_spec((pieces, rows, cols)),
                pl.BlockSpec((rows, tile), lambda i, at: (0, i)),
                pl.BlockSpec((per, rows, cols), lambda i, at: (i, at[0], 0)),
                pl.BlockSpec((pieces * cols, tile), lambda i, at: (0, i)),
                pl.BlockSpec((rows, 1), lambda i, at: (at[0], 0)),
            ],
            out_specs=[
                full_spec((pieces, rows, cols)),
                pl.BlockSpec((per, rows, cols), lambda i, at: (i, 0, 0)),
                pl.BlockSpec((rows, tile), lambda i, at: (0, i)),
            ],
            scratch_shapes=[pltpu.VMEM((rows, wide), F32)],
        ),
        out_shape=[
            jax.ShapeDtypeStruct((pieces, rows, cols), BF16),
            jax.ShapeDtypeStruct((pieces, rows, cols), BF16),
            jax.ShapeDtypeStruct((rows, wide), BF16),
        ],
        compiler_params=params(1),
        name="dense",
    )(at, mean_pieces, own, cot_all, w_neigh, degrees)


def backward_blocks_kernel(
    source_ref, slot_ref, low_ref, high_ref, adj_ref, self_ref, out_ref, both_ref, acc_ref
):
    step = pl.program_id(0)
    chunk, blk, _ = adj_ref.shape
    parts = low_ref.shape[0]

    @pl.when(step == 0)
    def _():
        acc_ref[...] = self_ref[...]
        for part in range(parts):
            both_ref[2 * part] = low_ref[part]
            both_ref[2 * part + 1] = high_ref[part]

    for item in range(chunk):
        block = step * chunk + item
        start = pl.multiple_of(source_ref[block] * blk, blk)
        product = jnp.dot(
            adj_ref[item], both_ref[slot_ref[block]], preferred_element_type=F32
        )
        acc_ref[pl.ds(start, blk), :] += product

    @pl.when(step == pl.num_programs(0) - 1)
    def _():
        out_ref[...] = acc_ref[...].astype(BF16)


def backward_blocks(block_source, block_to_slot, low, high, adjacency_t, self_grad):
    blocks, blk, _ = adjacency_t.shape
    nodes, cols = self_grad.shape
    parts = low.shape[0]
    chunk = 16
    return pl.pallas_call(
        backward_blocks_kernel,
        grid_spec=pltpu.PrefetchScalarGridSpec(
            num_scalar_prefetch=2,
            grid=(blocks // chunk,),
            in_specs=[
                full_spec((parts, blk, cols)),
                full_spec((parts, blk, cols)),
                pl.BlockSpec((chunk, blk, blk), lambda i, *unused: (i, 0, 0)),
                full_spec((nodes, cols)),
            ],
            out_specs=full_spec((nodes, cols)),
            scratch_shapes=[
                pltpu.VMEM((2 * parts, blk, cols), BF16),
                pltpu.VMEM((nodes, cols), F32),
            ],
        ),
        out_shape=jax.ShapeDtypeStruct((nodes, cols), BF16),
        compiler_params=params(1),
        name="backward_blocks",
    )(block_source, block_to_slot, low, high, adjacency_t, self_grad)


def in_hbm(value):
    return pltpu.with_memory_space_constraint(value, pltpu.HBM)


def swap(value, axis):
    return lax.all_to_all(value, axis, split_axis=0, concat_axis=0, tiled=True)


def after(value, *others):
    return lax.optimization_barrier((value, *others))[0]


def rotate(value, axis, distance):
    size = lax.axis_size(axis)
    return lax.ppermute(value, axis, [(i, (i + distance) % size) for i in range(size)])


def scatter_sum(pieces, axis):
    size, at = lax.axis_size(axis), lax.axis_index(axis)
    take = functools.partial(lax.dynamic_index_in_dim, pieces, axis=0, keepdims=False)
    total = take(at).astype(F32)
    came = [rotate(take((at + d) % size), axis, d) for d in range(1, size)]
    for piece in came:
        total = total + piece.astype(F32)
    return total.astype(BF16)


def quad_sum(value, axis):
    size = lax.axis_size(axis)
    one, two, three = (
        lax.ppermute(value, axis, [(i, i ^ d) for i in range(size)]).astype(F32)
        for d in (1, 2, 3)
    )
    return ((value.astype(F32) + one) + (two + three)).astype(BF16)


def around(piece, axis):
    size = lax.axis_size(axis)
    return [piece] + [rotate(piece, axis, size - i) for i in range(1, size)]


def exchange_sum(value, axis, distance, *beside):
    size = lax.axis_size(axis)
    other = lax.ppermute(value, axis, [(i, i ^ distance) for i in range(size)])
    other = after(other, *beside)
    return (value.astype(F32) + other.astype(F32)).astype(BF16)


def assemble_kernel(at_ref, *refs):
    *piece_refs, first_ref, second_ref = refs
    size = len(piece_refs)
    half = size // 2
    for i, piece_ref in enumerate(piece_refs):
        place = (at_ref[0] + i) % size
        value = piece_ref[...].astype(F32)

        @pl.when(place < half)
        def _():
            first_ref[place] = value

        @pl.when(place >= half)
        def _():
            second_ref[place - half] = value


def assemble(at, pieces):
    rows, wide = pieces[0].shape
    half = len(pieces) // 2
    first, second = pl.pallas_call(
        assemble_kernel,
        grid_spec=pltpu.PrefetchScalarGridSpec(
            num_scalar_prefetch=1,
            grid=(1,),
            in_specs=[full_spec((rows, wide))] * len(pieces),
            out_specs=[full_spec((half, rows, wide))] * 2,
        ),
        out_shape=[jax.ShapeDtypeStruct((half, rows, wide), F32)] * 2,
        compiler_params=params(1),
        name="assemble",
    )(at, *pieces)
    return first.reshape(half * rows, wide), second.reshape(half * rows, wide)


def on_device(
    features,
    w_self,
    w_neigh,
    adjacency,
    block_source,
    block_to_slot,
    send_rows,
    send_counts,
    degree,
    cotangent,
):
    node_rows, feat_cols = features.shape
    feat_size = lax.axis_size("feat")
    feat_at = lax.axis_index("feat")
    at = jnp.full((1,), feat_at, jnp.int32)
    share = node_rows // feat_size
    graph = ("z", "y")
    low, high = forward_blocks(
        in_hbm(block_source),
        in_hbm(block_to_slot),
        in_hbm(send_counts[0]),
        in_hbm(send_rows[0]),
        in_hbm(features),
        in_hbm(adjacency),
    )
    low_in = swap(low, graph)
    high_in = swap(high, graph)
    feat_all = lax.all_gather(features, "feat", axis=0)
    cot_all = lax.all_gather(after(cotangent, low_in), "feat", axis=0)
    degrees = degree.astype(F32)[:, None]
    adjacency_t = in_hbm(after(adjacency, low_in).swapaxes(1, 2))
    self_rows = lax.dynamic_slice_in_dim(w_self, feat_at * feat_cols, feat_cols, 0)

    partial_sum = scatter_low(low_in, node_rows)
    blk = adjacency.shape[1]
    parts = low.shape[0]
    ids = low_in[:, blk : blk + 4, :].astype(F32).reshape(parts // 8, 8, 4, blk).transpose(2, 0, 3, 1)
    own = own_term(at, in_hbm(feat_all), w_self, share)
    partial_sum, adjacency_t, ids, own = lax.optimization_barrier(
        (partial_sum, adjacency_t, ids, own)
    )
    neighbor_mean = scatter_high(low_in, high_in, ids, in_hbm(partial_sum), degrees)
    mean_pieces = swap(neighbor_mean.reshape(feat_size, share, feat_cols), "feat")
    back_pieces, hidden_pieces, grad_pre = dense(
        at, mean_pieces, in_hbm(own), in_hbm(cot_all), in_hbm(w_neigh), degrees
    )
    back_rows = swap(back_pieces, "feat").reshape(node_rows, feat_cols)
    back_rows, grad_pre, hidden_pieces = lax.optimization_barrier(
        (back_rows, grad_pre, hidden_pieces)
    )
    rows_low = gather_rows(0, ids, back_rows)
    rows_high = gather_rows(1, ids, back_rows)
    back_low = swap(rows_low, graph)
    grad_full = lax.all_gather(grad_pre, "feat", axis=0, tiled=True)
    grad_full = after(grad_full, rows_high)
    both = jnp.concatenate([features, neighbor_mean], axis=1)
    weight_part = lax.dot_general(
        both, grad_full, (((0,), (0,)), ((), ())), preferred_element_type=F32
    ).astype(BF16)
    over_y = lax.axis_size("y")
    part = weight_part.reshape(over_y, 2 * feat_cols // over_y, weight_part.shape[1])
    part = scatter_sum(part, "y")
    back_high = swap(after(rows_high, weight_part, back_low), graph)

    hidden_all = lax.all_gather(after(hidden_pieces, rows_low), "feat", axis=0)
    hidden_out = lax.dynamic_index_in_dim(hidden_all, feat_at, 1, keepdims=False)
    hidden_out = hidden_out.reshape(node_rows, feat_cols)
    self_grad = lax.dot_general(
        grad_full, self_rows, (((1,), (1,)), ((), ())), preferred_element_type=F32
    )
    part = after(quad_sum(part, "z"), self_grad)
    part = exchange_sum(part, "z", 4, hidden_out)
    grad_features = backward_blocks(
        in_hbm(block_source),
        in_hbm(block_to_slot),
        back_low,
        back_high,
        adjacency_t,
        self_grad,
    )
    grad_self, grad_neigh = assemble(
        jnp.full((1,), lax.axis_index("y"), jnp.int32), around(after(part, back_high), "y")
    )
    return hidden_out, grad_features, grad_self, grad_neigh


def solution(mesh):
    split = Mesh(mesh.devices.reshape(8, 4, 8), ("z", "y", "feat"))
    graph = ("z", "y")
    placed = (
        P(graph, "feat"),
        P(),
        P(),
        P(graph, None, None),
        P(graph),
        P(graph),
        P(graph, None, None),
        P(graph, None),
        P(graph),
        P(graph, "feat"),
    )
    return jax.shard_map(
        on_device,
        mesh=split,
        in_specs=placed,
        out_specs=(P(graph, "feat"), P(graph, "feat"), P("feat", None), P("feat", None)),
        check_vma=False,
    )
```

```python
import functools

import jax
import jax.numpy as jnp
from jax import lax
from jax.experimental import pallas as pl
from jax.experimental.pallas import tpu as pltpu
from jax.sharding import Mesh, PartitionSpec as P

BF16 = jnp.bfloat16
F32 = jnp.float32
VMEM_BYTES = 20 * 1024 * 1024
ID_ROWS = 8


def params(axes=0):
    return pltpu.CompilerParams(
        dimension_semantics=("arbitrary",) * axes if axes else None, vmem_limit_bytes=VMEM_BYTES
    )


def full_spec(shape):
    return pl.BlockSpec(shape, lambda *unused: (0,) * len(shape))


def forward_blocks_kernel(
    source_ref, slot_ref, count_ref, rows_ref, feat_ref, adj_ref, low_ref, high_ref, sums_ref
):
    step = pl.program_id(0)
    chunk, blk, _ = adj_ref.shape
    parts = low_ref.shape[0]
    cols = feat_ref.shape[1]

    @pl.when(step == 0)
    def _():
        sums_ref[...] = jnp.zeros(sums_ref.shape, F32)

    for item in range(chunk):
        block = step * chunk + item
        start = pl.multiple_of(source_ref[block] * blk, blk)
        product = jnp.dot(
            adj_ref[item], feat_ref[pl.ds(start, blk), :], preferred_element_type=F32
        )
        sums_ref[slot_ref[block]] += product

    @pl.when(step == pl.num_programs(0) - 1)
    def _():
        slot_row = lax.broadcasted_iota(jnp.int32, (blk, cols), 0)
        lane = lax.broadcasted_iota(jnp.int32, (1, 2 * blk), 1)
        tile_row = lax.broadcasted_iota(jnp.int32, (ID_ROWS, blk), 0)

        def emit(part, carry):
            count = count_ref[part]
            low = jnp.where(slot_row < count, sums_ref[2 * part], 0.0)
            high = jnp.where(slot_row + blk < count, sums_ref[2 * part + 1], 0.0)
            low_ref[part, 0:blk, :] = low.astype(BF16)
            high_ref[part] = high.astype(BF16)
            ids = rows_ref[pl.ds(part, 1), :]
            live = lane < count
            fine = jnp.where(live, ids & (blk - 1), -1).astype(F32)
            coarse = jnp.where(live, ids >> 7, -1).astype(F32)
            tile = jnp.where(tile_row == 0, fine[:, :blk], 0.0)
            tile = jnp.where(tile_row == 1, fine[:, blk:], tile)
            tile = jnp.where(tile_row == 2, coarse[:, :blk], tile)
            tile = jnp.where(tile_row == 3, coarse[:, blk:], tile)
            low_ref[part, blk : blk + ID_ROWS, :] = tile.astype(BF16)
            return carry

        lax.fori_loop(0, parts, emit, 0, unroll=4)


def forward_blocks(block_source, block_to_slot, counts, rows, features, adjacency):
    blocks, blk, _ = adjacency.shape
    nodes, cols = features.shape
    parts, cap = rows.shape
    chunk = 32
    return pl.pallas_call(
        forward_blocks_kernel,
        grid_spec=pltpu.PrefetchScalarGridSpec(
            num_scalar_prefetch=3,
            grid=(blocks // chunk,),
            in_specs=[
                full_spec((parts, cap)),
                full_spec((nodes, cols)),
                pl.BlockSpec((chunk, blk, blk), lambda i, *unused: (i, 0, 0)),
            ],
            out_specs=[full_spec((parts, blk + ID_ROWS, cols)), full_spec((parts, blk, cols))],
            scratch_shapes=[pltpu.VMEM((parts * cap // blk, blk, cols), F32)],
        ),
        out_shape=[
            jax.ShapeDtypeStruct((parts, blk + ID_ROWS, cols), BF16),
            jax.ShapeDtypeStruct((parts, blk, cols), BF16),
        ],
        compiler_params=params(1),
        name="forward_blocks",
    )(block_source, block_to_slot, counts, rows, features, adjacency)


def scatter_body(half, ids_ref, rows_ref, hot_ref, acc_ref, group):
    nodes, cols = acc_ref.shape
    blk = 128
    node_row = lax.broadcasted_iota(jnp.int32, (blk, blk), 0).astype(F32)
    for part in range(group):
        tile = ids_ref[part].astype(F32)
        fine = tile[half : half + 1, :]
        coarse = tile[2 + half : 3 + half, :]
        hot = jnp.where(node_row == fine, 1.0, 0.0).astype(BF16)
        for block in range(nodes // blk):
            keep = jnp.where(coarse == float(block), 1.0, 0.0).astype(BF16)
            hot_ref[block * blk : (block + 1) * blk, part * blk : (part + 1) * blk] = hot * keep
    rows = rows_ref[...].reshape(group * blk, cols)
    acc_ref[...] += jnp.dot(hot_ref[...], rows, preferred_element_type=F32)


def scatter_low_kernel(payload_ids_ref, rows_ref, sum_ref, hot_ref):
    @pl.when(pl.program_id(0) == 0)
    def _():
        sum_ref[...] = jnp.zeros(sum_ref.shape, F32)

    scatter_body(0, payload_ids_ref, rows_ref, hot_ref, sum_ref, rows_ref.shape[0])


def scatter_high_kernel(
    ids_ref, rows_ref, coarse_ref, init_ref, degree_ref, mean_ref, hot_ref, both_ref, acc_ref
):
    step = pl.program_id(0)
    group, blk, cols = rows_ref.shape
    half_nodes = acc_ref.shape[0]
    half_blocks = half_nodes // blk

    @pl.when(step == 0)
    def _():
        acc_ref[:, :cols] = init_ref[:half_nodes]
        acc_ref[:, cols:] = init_ref[half_nodes:]

    node_row = lax.broadcasted_iota(jnp.int32, (blk, blk), 0).astype(F32)
    for part in range(group):
        tile = ids_ref[part].astype(F32)
        fine = tile[1:2, :]
        coarse = tile[3:4, :]
        coarse = jnp.where(coarse >= half_blocks, coarse - half_blocks, coarse)
        hot = jnp.where(node_row == fine, 1.0, 0.0).astype(BF16)
        here = slice(part * blk, (part + 1) * blk)
        for block in range(half_blocks):
            keep = jnp.where(coarse == float(block), 1.0, 0.0).astype(BF16)
            hot_ref[block * blk : (block + 1) * blk, here] = hot * keep
        column = jnp.broadcast_to(coarse_ref[0, 0, :, part : part + 1], (blk, cols))
        upper = jnp.where(column >= half_blocks, 1.0, 0.0).astype(BF16)
        rows = rows_ref[part]
        both_ref[here, cols:] = rows * upper
        both_ref[here, :cols] = rows * (1.0 - upper)
    acc_ref[...] += jnp.dot(hot_ref[...], both_ref[...], preferred_element_type=F32)

    @pl.when(step == pl.num_programs(0) - 1)
    def _():
        mean_ref[:half_nodes] = (acc_ref[:, :cols] / degree_ref[:half_nodes]).astype(BF16)
        mean_ref[half_nodes:] = (acc_ref[:, cols:] / degree_ref[half_nodes:]).astype(BF16)


def scatter_low(low, nodes):
    parts, height, cols = low.shape
    group, blk = 8, 128
    return pl.pallas_call(
        scatter_low_kernel,
        grid=(parts // group,),
        in_specs=[
            pl.BlockSpec((group, ID_ROWS, cols), lambda i: (i, blk // ID_ROWS, 0)),
            pl.BlockSpec((group, blk, cols), lambda i: (i, 0, 0)),
        ],
        out_specs=full_spec((nodes, cols)),
        out_shape=pltpu.HBM((nodes, cols), F32),
        scratch_shapes=[pltpu.VMEM((nodes, group * blk), BF16)],
        compiler_params=params(1),
        name="scatter_low",
    )(low, low)


def scatter_high(low, high, columns, partial_sum, degrees):
    parts, blk, cols = high.shape
    nodes = partial_sum.shape[0]
    group = columns.shape[3]
    return pl.pallas_call(
        scatter_high_kernel,
        grid=(parts // group,),
        in_specs=[
            pl.BlockSpec((group, ID_ROWS, cols), lambda i: (i, blk // ID_ROWS, 0)),
            pl.BlockSpec((group, blk, cols), lambda i: (i, 0, 0)),
            pl.BlockSpec((1, 1, blk, group), lambda i: (3, i, 0, 0)),
            full_spec((nodes, cols)),
            full_spec((nodes, 1)),
        ],
        out_specs=full_spec((nodes, cols)),
        out_shape=pltpu.HBM((nodes, cols), BF16),
        scratch_shapes=[
            pltpu.VMEM((nodes // 2, group * blk), BF16),
            pltpu.VMEM((group * blk, 2 * cols), BF16),
            pltpu.VMEM((nodes // 2, 2 * cols), F32),
        ],
        compiler_params=params(1),
        name="scatter_high",
    )(low, high, columns, partial_sum, degrees)


def gather_kernel(fine_ref, coarse_ref, back_ref, out_ref, hot_ref):
    group, blk, cols = out_ref.shape
    half_nodes = back_ref.shape[0] // 2
    half_blocks = half_nodes // blk
    lane = lax.broadcasted_iota(jnp.int32, (blk, blk), 1).astype(F32)
    for part in range(group):
        fine = jnp.broadcast_to(fine_ref[0, 0, :, part : part + 1], (blk, blk))
        coarse = jnp.broadcast_to(coarse_ref[0, 0, :, part : part + 1], (blk, blk))
        coarse = jnp.where(coarse >= half_blocks, coarse - half_blocks, coarse)
        hot = jnp.where(lane == fine, 1.0, 0.0).astype(BF16)
        coarse = coarse.astype(BF16)
        for block in range(half_blocks):
            value = jnp.where(coarse == BF16(block), hot, BF16(0))
            hot_ref[part * blk : (part + 1) * blk, block * blk : (block + 1) * blk] = value
    both = jnp.concatenate([back_ref[:half_nodes], back_ref[half_nodes:]], axis=1)
    picked = jnp.dot(hot_ref[...], both, preferred_element_type=F32)
    for part in range(group):
        coarse = jnp.broadcast_to(coarse_ref[0, 0, :, part : part + 1], (blk, cols))
        here = slice(part * blk, (part + 1) * blk)
        rows = jnp.where(coarse >= half_blocks, picked[here, cols:], picked[here, :cols])
        out_ref[part] = rows.astype(BF16)


def gather_rows(half, columns, back):
    _, steps, blk, group = columns.shape
    nodes, cols = back.shape
    return pl.pallas_call(
        gather_kernel,
        grid=(steps,),
        in_specs=[
            pl.BlockSpec((1, 1, blk, group), lambda i: (half, i, 0, 0)),
            pl.BlockSpec((1, 1, blk, group), lambda i: (2 + half, i, 0, 0)),
            full_spec((nodes, cols)),
        ],
        out_specs=pl.BlockSpec((group, blk, cols), lambda i: (i, 0, 0)),
        out_shape=pltpu.HBM((steps * group, blk, cols), BF16),
        scratch_shapes=[pltpu.VMEM((group * blk, nodes // 2), BF16)],
        compiler_params=params(1),
        name="gather_rows",
    )(columns, columns, back)


def own_term_kernel(at_ref, feat_ref, weight_ref, out_ref):
    pieces = feat_ref.shape[0]
    rows = jnp.concatenate([feat_ref[piece] for piece in range(pieces)], axis=1)
    out_ref[...] = jnp.dot(rows, weight_ref[...], preferred_element_type=F32)


def own_term(at, feat_all, w_self, share):
    pieces, _, cols = feat_all.shape
    wide = w_self.shape[1]
    tile = 256
    return pl.pallas_call(
        own_term_kernel,
        grid_spec=pltpu.PrefetchScalarGridSpec(
            num_scalar_prefetch=1,
            grid=(wide // tile,),
            in_specs=[
                pl.BlockSpec((pieces, share, cols), lambda i, at: (0, at[0], 0)),
                pl.BlockSpec((pieces * cols, tile), lambda i, at: (0, i)),
            ],
            out_specs=pl.BlockSpec((share, tile), lambda i, at: (0, i)),
        ),
        out_shape=pltpu.HBM((share, wide), F32),
        compiler_params=params(1),
        name="own_term",
    )(at, feat_all, w_self)


def dense_kernel(
    at_ref, mean_ref, own_ref, cot_ref, weight_ref, degree_ref, back_ref, hidden_ref, grad_ref, acc_ref
):
    step = pl.program_id(0)
    pieces, rows, cols = mean_ref.shape
    tile = weight_ref.shape[1]
    mean = jnp.concatenate([mean_ref[piece] for piece in range(pieces)], axis=1)
    pre_act = own_ref[...] + jnp.dot(mean, weight_ref[...], preferred_element_type=F32)
    sig = jax.nn.sigmoid(pre_act)
    cot = jnp.concatenate([cot_ref[piece] for piece in range(cot_ref.shape[0])], axis=1)
    slope = sig * (1.0 + pre_act * (1.0 - sig))
    grad = (cot.astype(F32) * slope).astype(BF16)
    hidden = (pre_act * sig).astype(BF16)
    grad_ref[...] = grad
    for piece in range(tile // cols):
        hidden_ref[piece] = hidden[:, piece * cols : (piece + 1) * cols]
    update = lax.dot_general(
        grad, weight_ref[...], (((1,), (1,)), ((), ())), preferred_element_type=F32
    )

    @pl.when(step == 0)
    def _():
        acc_ref[...] = update

    @pl.when(step > 0)
    def _():
        acc_ref[...] += update

    @pl.when(step == pl.num_programs(0) - 1)
    def _():
        back = (acc_ref[...] / degree_ref[...]).astype(BF16)
        for piece in range(pieces):
            back_ref[piece] = back[:, piece * cols : (piece + 1) * cols]


def dense(at, mean_pieces, own, cot_all, w_neigh, degrees):
    pieces, rows, cols = mean_pieces.shape
    wide = w_neigh.shape[1]
    tile = 256
    per = tile // cols
    return pl.pallas_call(
        dense_kernel,
        grid_spec=pltpu.PrefetchScalarGridSpec(
            num_scalar_prefetch=1,
            grid=(wide // tile,),
            in_specs=[
                full_spec((pieces, rows, cols)),
                pl.BlockSpec((rows, tile), lambda i, at: (0, i)),
                pl.BlockSpec((per, rows, cols), lambda i, at: (i, at[0], 0)),
                pl.BlockSpec((pieces * cols, tile), lambda i, at: (0, i)),
                pl.BlockSpec((rows, 1), lambda i, at: (at[0], 0)),
            ],
            out_specs=[
                full_spec((pieces, rows, cols)),
                pl.BlockSpec((per, rows, cols), lambda i, at: (i, 0, 0)),
                pl.BlockSpec((rows, tile), lambda i, at: (0, i)),
            ],
            scratch_shapes=[pltpu.VMEM((rows, wide), F32)],
        ),
        out_shape=[
            jax.ShapeDtypeStruct((pieces, rows, cols), BF16),
            jax.ShapeDtypeStruct((pieces, rows, cols), BF16),
            jax.ShapeDtypeStruct((rows, wide), BF16),
        ],
        compiler_params=params(1),
        name="dense",
    )(at, mean_pieces, own, cot_all, w_neigh, degrees)


def backward_blocks_kernel(
    source_ref, slot_ref, low_ref, high_ref, adj_ref, self_ref, out_ref, both_ref, acc_ref
):
    step = pl.program_id(0)
    chunk, blk, _ = adj_ref.shape
    parts = low_ref.shape[0]

    @pl.when(step == 0)
    def _():
        acc_ref[...] = self_ref[...]
        for part in range(parts):
            both_ref[2 * part] = low_ref[part]
            both_ref[2 * part + 1] = high_ref[part]

    for item in range(chunk):
        block = step * chunk + item
        start = pl.multiple_of(source_ref[block] * blk, blk)
        product = jnp.dot(
            adj_ref[item], both_ref[slot_ref[block]], preferred_element_type=F32
        )
        acc_ref[pl.ds(start, blk), :] += product

    @pl.when(step == pl.num_programs(0) - 1)
    def _():
        out_ref[...] = acc_ref[...].astype(BF16)


def backward_blocks(block_source, block_to_slot, low, high, adjacency_t, self_grad):
    blocks, blk, _ = adjacency_t.shape
    nodes, cols = self_grad.shape
    parts = low.shape[0]
    chunk = 32
    return pl.pallas_call(
        backward_blocks_kernel,
        grid_spec=pltpu.PrefetchScalarGridSpec(
            num_scalar_prefetch=2,
            grid=(blocks // chunk,),
            in_specs=[
                full_spec((parts, blk, cols)),
                full_spec((parts, blk, cols)),
                pl.BlockSpec((chunk, blk, blk), lambda i, *unused: (i, 0, 0)),
                full_spec((nodes, cols)),
            ],
            out_specs=full_spec((nodes, cols)),
            scratch_shapes=[
                pltpu.VMEM((2 * parts, blk, cols), BF16),
                pltpu.VMEM((nodes, cols), F32),
            ],
        ),
        out_shape=jax.ShapeDtypeStruct((nodes, cols), BF16),
        compiler_params=params(1),
        name="backward_blocks",
    )(block_source, block_to_slot, low, high, adjacency_t, self_grad)


def in_hbm(value):
    return pltpu.with_memory_space_constraint(value, pltpu.HBM)


def swap(value, axis):
    return lax.all_to_all(value, axis, split_axis=0, concat_axis=0, tiled=True)


def after(value, *others):
    return lax.optimization_barrier((value, *others))[0]


def rotate(value, axis, distance):
    size = lax.axis_size(axis)
    return lax.ppermute(value, axis, [(i, (i + distance) % size) for i in range(size)])


def scatter_sum(pieces, axis):
    size, at = lax.axis_size(axis), lax.axis_index(axis)
    take = functools.partial(lax.dynamic_index_in_dim, pieces, axis=0, keepdims=False)
    total = take(at).astype(F32)
    came = [rotate(take((at + d) % size), axis, d) for d in range(1, size)]
    for piece in came:
        total = total + piece.astype(F32)
    return total.astype(BF16)


def quad_sum(value, axis):
    size = lax.axis_size(axis)
    one, two, three = (
        lax.ppermute(value, axis, [(i, i ^ d) for i in range(size)]).astype(F32)
        for d in (1, 2, 3)
    )
    return ((value.astype(F32) + one) + (two + three)).astype(BF16)


def around(piece, axis):
    size = lax.axis_size(axis)
    return [piece] + [rotate(piece, axis, size - i) for i in range(1, size)]


def exchange_sum(value, axis, distance, *beside):
    size = lax.axis_size(axis)
    other = lax.ppermute(value, axis, [(i, i ^ distance) for i in range(size)])
    other = after(other, *beside)
    return (value.astype(F32) + other.astype(F32)).astype(BF16)


def assemble_kernel(at_ref, *refs):
    *piece_refs, first_ref, second_ref = refs
    size = len(piece_refs)
    half = size // 2
    for i, piece_ref in enumerate(piece_refs):
        place = (at_ref[0] + i) % size
        value = piece_ref[...].astype(F32)

        @pl.when(place < half)
        def _():
            first_ref[place] = value

        @pl.when(place >= half)
        def _():
            second_ref[place - half] = value


def assemble(at, pieces):
    rows, wide = pieces[0].shape
    half = len(pieces) // 2
    first, second = pl.pallas_call(
        assemble_kernel,
        grid_spec=pltpu.PrefetchScalarGridSpec(
            num_scalar_prefetch=1,
            grid=(1,),
            in_specs=[full_spec((rows, wide))] * len(pieces),
            out_specs=[full_spec((half, rows, wide))] * 2,
        ),
        out_shape=[jax.ShapeDtypeStruct((half, rows, wide), F32)] * 2,
        compiler_params=params(1),
        name="assemble",
    )(at, *pieces)
    return first.reshape(half * rows, wide), second.reshape(half * rows, wide)


def on_device(
    features,
    w_self,
    w_neigh,
    adjacency,
    block_source,
    block_to_slot,
    send_rows,
    send_counts,
    degree,
    cotangent,
):
    node_rows, feat_cols = features.shape
    feat_size = lax.axis_size("feat")
    feat_at = lax.axis_index("feat")
    at = jnp.full((1,), feat_at, jnp.int32)
    share = node_rows // feat_size
    graph = ("z", "y")
    low, high = forward_blocks(
        in_hbm(block_source),
        in_hbm(block_to_slot),
        in_hbm(send_counts[0]),
        in_hbm(send_rows[0]),
        in_hbm(features),
        in_hbm(adjacency),
    )
    low_in = swap(low, graph)
    high_in = swap(high, graph)
    feat_all = lax.all_gather(features, "feat", axis=0)
    cot_all = lax.all_gather(after(cotangent, low_in), "feat", axis=0)
    degrees = degree.astype(F32)[:, None]
    adjacency_t = in_hbm(after(adjacency, low_in).swapaxes(1, 2))
    self_rows = lax.dynamic_slice_in_dim(w_self, feat_at * feat_cols, feat_cols, 0)

    partial_sum = scatter_low(low_in, node_rows)
    blk = adjacency.shape[1]
    parts = low.shape[0]
    ids = low_in[:, blk : blk + 4, :].astype(F32).reshape(parts // 8, 8, 4, blk).transpose(2, 0, 3, 1)
    own = own_term(at, in_hbm(feat_all), w_self, share)
    partial_sum, adjacency_t, ids, own = lax.optimization_barrier(
        (partial_sum, adjacency_t, ids, own)
    )
    neighbor_mean = scatter_high(low_in, high_in, ids, in_hbm(partial_sum), degrees)
    mean_pieces = swap(neighbor_mean.reshape(feat_size, share, feat_cols), "feat")
    back_pieces, hidden_pieces, grad_pre = dense(
        at, mean_pieces, in_hbm(own), in_hbm(cot_all), in_hbm(w_neigh), degrees
    )
    back_rows = swap(back_pieces, "feat").reshape(node_rows, feat_cols)
    back_rows, grad_pre, hidden_pieces = lax.optimization_barrier(
        (back_rows, grad_pre, hidden_pieces)
    )
    rows_low = gather_rows(0, ids, back_rows)
    rows_high = gather_rows(1, ids, back_rows)
    back_low = swap(rows_low, graph)
    grad_full = lax.all_gather(grad_pre, "feat", axis=0, tiled=True)
    grad_full = after(grad_full, rows_high)
    both = jnp.concatenate([features, neighbor_mean], axis=1)
    weight_part = lax.dot_general(
        both, grad_full, (((0,), (0,)), ((), ())), preferred_element_type=F32
    ).astype(BF16)
    over_y = lax.axis_size("y")
    part = weight_part.reshape(over_y, 2 * feat_cols // over_y, weight_part.shape[1])
    part = scatter_sum(part, "y")
    back_high = swap(after(rows_high, weight_part, back_low), graph)

    hidden_all = lax.all_gather(after(hidden_pieces, rows_low), "feat", axis=0)
    hidden_out = lax.dynamic_index_in_dim(hidden_all, feat_at, 1, keepdims=False)
    hidden_out = hidden_out.reshape(node_rows, feat_cols)
    self_grad = lax.dot_general(
        grad_full, self_rows, (((1,), (1,)), ((), ())), preferred_element_type=F32
    )
    part = after(quad_sum(part, "z"), self_grad)
    grad_features = backward_blocks(
        in_hbm(block_source),
        in_hbm(block_to_slot),
        back_low,
        back_high,
        adjacency_t,
        self_grad,
    )
    part = exchange_sum(part, "z", 4, grad_features)
    at = after(jnp.full((1,), lax.axis_index("y"), jnp.int32), hidden_out)
    grad_self, grad_neigh = assemble(at, around(part, "y"))
    return hidden_out, grad_features, grad_self, grad_neigh


def solution(mesh):
    split = Mesh(mesh.devices.reshape(8, 4, 8), ("z", "y", "feat"))
    graph = ("z", "y")
    placed = (
        P(graph, "feat"),
        P(),
        P(),
        P(graph, None, None),
        P(graph),
        P(graph),
        P(graph, None, None),
        P(graph, None),
        P(graph),
        P(graph, "feat"),
    )
    return jax.shard_map(
        on_device,
        mesh=split,
        in_specs=placed,
        out_specs=(P(graph, "feat"), P(graph, "feat"), P("feat", None), P("feat", None)),
        check_vma=False,
    )
```

```python
import functools

import jax
import jax.numpy as jnp
from jax import lax
from jax.experimental import pallas as pl
from jax.experimental.pallas import tpu as pltpu
from jax.sharding import Mesh, PartitionSpec as P

BF16 = jnp.bfloat16
F32 = jnp.float32
VMEM_BYTES = 20 * 1024 * 1024
ID_ROWS = 8


def params(axes=0):
    return pltpu.CompilerParams(
        dimension_semantics=("arbitrary",) * axes if axes else None, vmem_limit_bytes=VMEM_BYTES
    )


def full_spec(shape):
    return pl.BlockSpec(shape, lambda *unused: (0,) * len(shape))


def forward_blocks_kernel(
    source_ref, slot_ref, count_ref, rows_ref, feat_ref, adj_ref, low_ref, high_ref, sums_ref
):
    step = pl.program_id(0)
    chunk, blk, _ = adj_ref.shape
    parts = low_ref.shape[0]
    cols = feat_ref.shape[1]

    @pl.when(step == 0)
    def _():
        sums_ref[...] = jnp.zeros(sums_ref.shape, F32)

    for item in range(chunk):
        block = step * chunk + item
        start = pl.multiple_of(source_ref[block] * blk, blk)
        product = jnp.dot(
            adj_ref[item], feat_ref[pl.ds(start, blk), :], preferred_element_type=F32
        )
        sums_ref[slot_ref[block]] += product

    @pl.when(step == pl.num_programs(0) - 1)
    def _():
        slot_row = lax.broadcasted_iota(jnp.int32, (blk, cols), 0)
        lane = lax.broadcasted_iota(jnp.int32, (1, 2 * blk), 1)
        tile_row = lax.broadcasted_iota(jnp.int32, (ID_ROWS, blk), 0)

        def emit(part, carry):
            count = count_ref[part]
            low = jnp.where(slot_row < count, sums_ref[2 * part], 0.0)
            high = jnp.where(slot_row + blk < count, sums_ref[2 * part + 1], 0.0)
            low_ref[part, 0:blk, :] = low.astype(BF16)
            high_ref[part] = high.astype(BF16)
            ids = rows_ref[pl.ds(part, 1), :]
            live = lane < count
            fine = jnp.where(live, ids & (blk - 1), -1).astype(F32)
            coarse = jnp.where(live, ids >> 7, -1).astype(F32)
            tile = jnp.where(tile_row == 0, fine[:, :blk], 0.0)
            tile = jnp.where(tile_row == 1, fine[:, blk:], tile)
            tile = jnp.where(tile_row == 2, coarse[:, :blk], tile)
            tile = jnp.where(tile_row == 3, coarse[:, blk:], tile)
            low_ref[part, blk : blk + ID_ROWS, :] = tile.astype(BF16)
            return carry

        lax.fori_loop(0, parts, emit, 0, unroll=4)


def forward_blocks(block_source, block_to_slot, counts, rows, features, adjacency):
    blocks, blk, _ = adjacency.shape
    nodes, cols = features.shape
    parts, cap = rows.shape
    chunk = 32
    return pl.pallas_call(
        forward_blocks_kernel,
        grid_spec=pltpu.PrefetchScalarGridSpec(
            num_scalar_prefetch=3,
            grid=(blocks // chunk,),
            in_specs=[
                full_spec((parts, cap)),
                full_spec((nodes, cols)),
                pl.BlockSpec((chunk, blk, blk), lambda i, *unused: (i, 0, 0)),
            ],
            out_specs=[full_spec((parts, blk + ID_ROWS, cols)), full_spec((parts, blk, cols))],
            scratch_shapes=[pltpu.VMEM((parts * cap // blk, blk, cols), F32)],
        ),
        out_shape=[
            jax.ShapeDtypeStruct((parts, blk + ID_ROWS, cols), BF16),
            jax.ShapeDtypeStruct((parts, blk, cols), BF16),
        ],
        compiler_params=params(1),
        name="forward_blocks",
    )(block_source, block_to_slot, counts, rows, features, adjacency)


def scatter_body(half, ids_ref, rows_ref, hot_ref, acc_ref, group):
    nodes, cols = acc_ref.shape
    blk = 128
    node_row = lax.broadcasted_iota(jnp.int32, (blk, blk), 0).astype(F32)
    for part in range(group):
        tile = ids_ref[part].astype(F32)
        fine = tile[half : half + 1, :]
        coarse = tile[2 + half : 3 + half, :]
        hot = jnp.where(node_row == fine, 1.0, 0.0).astype(BF16)
        for block in range(nodes // blk):
            keep = jnp.where(coarse == float(block), 1.0, 0.0).astype(BF16)
            hot_ref[block * blk : (block + 1) * blk, part * blk : (part + 1) * blk] = hot * keep
    rows = rows_ref[...].reshape(group * blk, cols)
    acc_ref[...] += jnp.dot(hot_ref[...], rows, preferred_element_type=F32)


def scatter_low_kernel(payload_ids_ref, rows_ref, sum_ref, hot_ref):
    @pl.when(pl.program_id(0) == 0)
    def _():
        sum_ref[...] = jnp.zeros(sum_ref.shape, F32)

    scatter_body(0, payload_ids_ref, rows_ref, hot_ref, sum_ref, rows_ref.shape[0])


def scatter_high_kernel(
    ids_ref,
    rows_ref,
    coarse_ref,
    init_ref,
    degree_ref,
    mean_ref,
    hot_a_ref,
    hot_b_ref,
    both_a_ref,
    both_b_ref,
    acc_ref,
):
    blk, cols = rows_ref.shape[1:]
    groups, group = coarse_ref.shape[1], coarse_ref.shape[3]
    half_nodes = acc_ref.shape[0]
    half_blocks = half_nodes // blk
    acc_ref[:, :cols] = init_ref[:half_nodes]
    acc_ref[:, cols:] = init_ref[half_nodes:]
    node_row = lax.broadcasted_iota(jnp.int32, (blk, blk), 0).astype(F32)
    for at in range(groups):
        hot_ref = hot_b_ref if at % 2 else hot_a_ref
        both_ref = both_b_ref if at % 2 else both_a_ref
        for part in range(group):
            tile = ids_ref[at * group + part].astype(F32)
            fine = tile[1:2, :]
            coarse = tile[3:4, :]
            coarse = jnp.where(coarse >= half_blocks, coarse - half_blocks, coarse)
            hot = jnp.where(node_row == fine, 1.0, 0.0).astype(BF16)
            here = slice(part * blk, (part + 1) * blk)
            for block in range(half_blocks):
                keep = jnp.where(coarse == float(block), 1.0, 0.0).astype(BF16)
                hot_ref[block * blk : (block + 1) * blk, here] = hot * keep
            column = jnp.broadcast_to(coarse_ref[0, at, :, part : part + 1], (blk, cols))
            upper = jnp.where(column >= half_blocks, 1.0, 0.0).astype(BF16)
            rows = rows_ref[at * group + part]
            both_ref[here, cols:] = rows * upper
            both_ref[here, :cols] = rows * (1.0 - upper)
        acc_ref[...] += jnp.dot(hot_ref[...], both_ref[...], preferred_element_type=F32)
    mean_ref[:half_nodes] = (acc_ref[:, :cols] / degree_ref[:half_nodes]).astype(BF16)
    mean_ref[half_nodes:] = (acc_ref[:, cols:] / degree_ref[half_nodes:]).astype(BF16)


def scatter_low(low, nodes):
    parts, height, cols = low.shape
    group, blk = 8, 128
    return pl.pallas_call(
        scatter_low_kernel,
        grid=(parts // group,),
        in_specs=[
            pl.BlockSpec((group, ID_ROWS, cols), lambda i: (i, blk // ID_ROWS, 0)),
            pl.BlockSpec((group, blk, cols), lambda i: (i, 0, 0)),
        ],
        out_specs=full_spec((nodes, cols)),
        out_shape=pltpu.HBM((nodes, cols), F32),
        scratch_shapes=[pltpu.VMEM((nodes, group * blk), BF16)],
        compiler_params=params(1),
        name="scatter_low",
    )(low, low)


def scatter_high(low, high, columns, partial_sum, degrees):
    parts, blk, cols = high.shape
    nodes = partial_sum.shape[0]
    groups, group = columns.shape[1], columns.shape[3]
    return pl.pallas_call(
        scatter_high_kernel,
        grid=(1,),
        in_specs=[
            pl.BlockSpec((parts, ID_ROWS, cols), lambda i: (0, blk // ID_ROWS, 0)),
            full_spec((parts, blk, cols)),
            pl.BlockSpec((1, groups, blk, group), lambda i: (3, 0, 0, 0)),
            full_spec((nodes, cols)),
            full_spec((nodes, 1)),
        ],
        out_specs=full_spec((nodes, cols)),
        out_shape=pltpu.HBM((nodes, cols), BF16),
        scratch_shapes=[
            pltpu.VMEM((nodes // 2, group * blk), BF16),
            pltpu.VMEM((nodes // 2, group * blk), BF16),
            pltpu.VMEM((group * blk, 2 * cols), BF16),
            pltpu.VMEM((group * blk, 2 * cols), BF16),
            pltpu.VMEM((nodes // 2, 2 * cols), F32),
        ],
        compiler_params=params(1),
        name="scatter_high",
    )(low, high, columns, partial_sum, degrees)


def gather_kernel(fine_ref, coarse_ref, back_ref, out_ref, hot_a_ref, hot_b_ref):
    blk, cols = out_ref.shape[1:]
    groups, group = fine_ref.shape[1], fine_ref.shape[3]
    half_nodes = back_ref.shape[0] // 2
    half_blocks = half_nodes // blk
    lane = lax.broadcasted_iota(jnp.int32, (blk, blk), 1).astype(F32)
    both = jnp.concatenate([back_ref[:half_nodes], back_ref[half_nodes:]], axis=1)
    for at in range(groups):
        hot_ref = hot_b_ref if at % 2 else hot_a_ref
        for part in range(group):
            fine = jnp.broadcast_to(fine_ref[0, at, :, part : part + 1], (blk, blk))
            coarse = jnp.broadcast_to(coarse_ref[0, at, :, part : part + 1], (blk, blk))
            coarse = jnp.where(coarse >= half_blocks, coarse - half_blocks, coarse)
            hot = jnp.where(lane == fine, 1.0, 0.0).astype(BF16)
            coarse = coarse.astype(BF16)
            for block in range(half_blocks):
                value = jnp.where(coarse == BF16(block), hot, BF16(0))
                hot_ref[part * blk : (part + 1) * blk, block * blk : (block + 1) * blk] = value
        picked = jnp.dot(hot_ref[...], both, preferred_element_type=F32)
        for part in range(group):
            coarse = jnp.broadcast_to(coarse_ref[0, at, :, part : part + 1], (blk, cols))
            here = slice(part * blk, (part + 1) * blk)
            rows = jnp.where(coarse >= half_blocks, picked[here, cols:], picked[here, :cols])
            out_ref[at * group + part] = rows.astype(BF16)


def gather_rows(half, columns, back):
    _, groups, blk, group = columns.shape
    nodes, cols = back.shape
    return pl.pallas_call(
        gather_kernel,
        grid=(1,),
        in_specs=[
            pl.BlockSpec((1, groups, blk, group), lambda i: (half, 0, 0, 0)),
            pl.BlockSpec((1, groups, blk, group), lambda i: (2 + half, 0, 0, 0)),
            full_spec((nodes, cols)),
        ],
        out_specs=full_spec((groups * group, blk, cols)),
        out_shape=pltpu.HBM((groups * group, blk, cols), BF16),
        scratch_shapes=[
            pltpu.VMEM((group * blk, nodes // 2), BF16),
            pltpu.VMEM((group * blk, nodes // 2), BF16),
        ],
        compiler_params=params(1),
        name="gather_rows",
    )(columns, columns, back)


def own_term_kernel(at_ref, feat_ref, weight_ref, out_ref):
    pieces = feat_ref.shape[0]
    rows = jnp.concatenate([feat_ref[piece] for piece in range(pieces)], axis=1)
    out_ref[...] = jnp.dot(rows, weight_ref[...], preferred_element_type=F32)


def own_term(at, feat_all, w_self, share):
    pieces, _, cols = feat_all.shape
    wide = w_self.shape[1]
    tile = 256
    return pl.pallas_call(
        own_term_kernel,
        grid_spec=pltpu.PrefetchScalarGridSpec(
            num_scalar_prefetch=1,
            grid=(wide // tile,),
            in_specs=[
                pl.BlockSpec((pieces, share, cols), lambda i, at: (0, at[0], 0)),
                pl.BlockSpec((pieces * cols, tile), lambda i, at: (0, i)),
            ],
            out_specs=pl.BlockSpec((share, tile), lambda i, at: (0, i)),
        ),
        out_shape=pltpu.HBM((share, wide), F32),
        compiler_params=params(1),
        name="own_term",
    )(at, feat_all, w_self)


def dense_kernel(
    at_ref, mean_ref, own_ref, cot_ref, weight_ref, degree_ref, back_ref, hidden_ref, grad_ref, acc_ref
):
    step = pl.program_id(0)
    pieces, rows, cols = mean_ref.shape
    tile = weight_ref.shape[1]
    mean = jnp.concatenate([mean_ref[piece] for piece in range(pieces)], axis=1)
    pre_act = own_ref[...] + jnp.dot(mean, weight_ref[...], preferred_element_type=F32)
    sig = jax.nn.sigmoid(pre_act)
    cot = jnp.concatenate([cot_ref[piece] for piece in range(cot_ref.shape[0])], axis=1)
    slope = sig * (1.0 + pre_act * (1.0 - sig))
    grad = (cot.astype(F32) * slope).astype(BF16)
    hidden = (pre_act * sig).astype(BF16)
    grad_ref[...] = grad
    for piece in range(tile // cols):
        hidden_ref[piece] = hidden[:, piece * cols : (piece + 1) * cols]
    update = lax.dot_general(
        grad, weight_ref[...], (((1,), (1,)), ((), ())), preferred_element_type=F32
    )

    @pl.when(step == 0)
    def _():
        acc_ref[...] = update

    @pl.when(step > 0)
    def _():
        acc_ref[...] += update

    @pl.when(step == pl.num_programs(0) - 1)
    def _():
        back = (acc_ref[...] / degree_ref[...]).astype(BF16)
        for piece in range(pieces):
            back_ref[piece] = back[:, piece * cols : (piece + 1) * cols]


def dense(at, mean_pieces, own, cot_all, w_neigh, degrees):
    pieces, rows, cols = mean_pieces.shape
    wide = w_neigh.shape[1]
    tile = 256
    per = tile // cols
    return pl.pallas_call(
        dense_kernel,
        grid_spec=pltpu.PrefetchScalarGridSpec(
            num_scalar_prefetch=1,
            grid=(wide // tile,),
            in_specs=[
                full_spec((pieces, rows, cols)),
                pl.BlockSpec((rows, tile), lambda i, at: (0, i)),
                pl.BlockSpec((per, rows, cols), lambda i, at: (i, at[0], 0)),
                pl.BlockSpec((pieces * cols, tile), lambda i, at: (0, i)),
                pl.BlockSpec((rows, 1), lambda i, at: (at[0], 0)),
            ],
            out_specs=[
                full_spec((pieces, rows, cols)),
                pl.BlockSpec((per, rows, cols), lambda i, at: (i, 0, 0)),
                pl.BlockSpec((rows, tile), lambda i, at: (0, i)),
            ],
            scratch_shapes=[pltpu.VMEM((rows, wide), F32)],
        ),
        out_shape=[
            jax.ShapeDtypeStruct((pieces, rows, cols), BF16),
            jax.ShapeDtypeStruct((pieces, rows, cols), BF16),
            jax.ShapeDtypeStruct((rows, wide), BF16),
        ],
        compiler_params=params(1),
        name="dense",
    )(at, mean_pieces, own, cot_all, w_neigh, degrees)


def backward_blocks_kernel(
    source_ref, slot_ref, low_ref, high_ref, adj_ref, self_ref, out_ref, both_ref, acc_ref
):
    step = pl.program_id(0)
    chunk, blk, _ = adj_ref.shape
    parts = low_ref.shape[0]

    @pl.when(step == 0)
    def _():
        acc_ref[...] = self_ref[...]
        for part in range(parts):
            both_ref[2 * part] = low_ref[part]
            both_ref[2 * part + 1] = high_ref[part]

    for item in range(chunk):
        block = step * chunk + item
        start = pl.multiple_of(source_ref[block] * blk, blk)
        product = jnp.dot(
            adj_ref[item], both_ref[slot_ref[block]], preferred_element_type=F32
        )
        acc_ref[pl.ds(start, blk), :] += product

    @pl.when(step == pl.num_programs(0) - 1)
    def _():
        out_ref[...] = acc_ref[...].astype(BF16)


def backward_blocks(block_source, block_to_slot, low, high, adjacency_t, self_grad):
    blocks, blk, _ = adjacency_t.shape
    nodes, cols = self_grad.shape
    parts = low.shape[0]
    chunk = 32
    return pl.pallas_call(
        backward_blocks_kernel,
        grid_spec=pltpu.PrefetchScalarGridSpec(
            num_scalar_prefetch=2,
            grid=(blocks // chunk,),
            in_specs=[
                full_spec((parts, blk, cols)),
                full_spec((parts, blk, cols)),
                pl.BlockSpec((chunk, blk, blk), lambda i, *unused: (i, 0, 0)),
                full_spec((nodes, cols)),
            ],
            out_specs=full_spec((nodes, cols)),
            scratch_shapes=[
                pltpu.VMEM((2 * parts, blk, cols), BF16),
                pltpu.VMEM((nodes, cols), F32),
            ],
        ),
        out_shape=jax.ShapeDtypeStruct((nodes, cols), BF16),
        compiler_params=params(1),
        name="backward_blocks",
    )(block_source, block_to_slot, low, high, adjacency_t, self_grad)


def in_hbm(value):
    return pltpu.with_memory_space_constraint(value, pltpu.HBM)


def swap(value, axis):
    return lax.all_to_all(value, axis, split_axis=0, concat_axis=0, tiled=True)


def after(value, *others):
    return lax.optimization_barrier((value, *others))[0]


def rotate(value, axis, distance):
    size = lax.axis_size(axis)
    return lax.ppermute(value, axis, [(i, (i + distance) % size) for i in range(size)])


def scatter_sum(pieces, axis):
    size, at = lax.axis_size(axis), lax.axis_index(axis)
    take = functools.partial(lax.dynamic_index_in_dim, pieces, axis=0, keepdims=False)
    total = take(at).astype(F32)
    came = [rotate(take((at + d) % size), axis, d) for d in range(1, size)]
    for piece in came:
        total = total + piece.astype(F32)
    return total.astype(BF16)


def quad_sum(value, axis):
    size = lax.axis_size(axis)
    one, two, three = (
        lax.ppermute(value, axis, [(i, i ^ d) for i in range(size)]).astype(F32)
        for d in (1, 2, 3)
    )
    return ((value.astype(F32) + one) + (two + three)).astype(BF16)


def around(piece, axis):
    size = lax.axis_size(axis)
    return [piece] + [rotate(piece, axis, size - i) for i in range(1, size)]


def exchange_sum(value, axis, distance, *beside):
    size = lax.axis_size(axis)
    other = lax.ppermute(value, axis, [(i, i ^ distance) for i in range(size)])
    other = after(other, *beside)
    return (value.astype(F32) + other.astype(F32)).astype(BF16)


def assemble_kernel(at_ref, *refs):
    *piece_refs, first_ref, second_ref = refs
    size = len(piece_refs)
    half = size // 2
    for i, piece_ref in enumerate(piece_refs):
        place = (at_ref[0] + i) % size
        value = piece_ref[...].astype(F32)

        @pl.when(place < half)
        def _():
            first_ref[place] = value

        @pl.when(place >= half)
        def _():
            second_ref[place - half] = value


def assemble(at, pieces):
    rows, wide = pieces[0].shape
    half = len(pieces) // 2
    first, second = pl.pallas_call(
        assemble_kernel,
        grid_spec=pltpu.PrefetchScalarGridSpec(
            num_scalar_prefetch=1,
            grid=(1,),
            in_specs=[full_spec((rows, wide))] * len(pieces),
            out_specs=[full_spec((half, rows, wide))] * 2,
        ),
        out_shape=[jax.ShapeDtypeStruct((half, rows, wide), F32)] * 2,
        compiler_params=params(1),
        name="assemble",
    )(at, *pieces)
    return first.reshape(half * rows, wide), second.reshape(half * rows, wide)


def on_device(
    features,
    w_self,
    w_neigh,
    adjacency,
    block_source,
    block_to_slot,
    send_rows,
    send_counts,
    degree,
    cotangent,
):
    node_rows, feat_cols = features.shape
    feat_size = lax.axis_size("feat")
    feat_at = lax.axis_index("feat")
    at = jnp.full((1,), feat_at, jnp.int32)
    share = node_rows // feat_size
    graph = ("z", "y")
    low, high = forward_blocks(
        in_hbm(block_source),
        in_hbm(block_to_slot),
        in_hbm(send_counts[0]),
        in_hbm(send_rows[0]),
        in_hbm(features),
        in_hbm(adjacency),
    )
    low_in = swap(low, graph)
    high_in = swap(high, graph)
    feat_all = lax.all_gather(features, "feat", axis=0)
    cot_all = lax.all_gather(after(cotangent, low_in), "feat", axis=0)
    degrees = degree.astype(F32)[:, None]
    adjacency_t = in_hbm(after(adjacency, low_in).swapaxes(1, 2))
    self_rows = lax.dynamic_slice_in_dim(w_self, feat_at * feat_cols, feat_cols, 0)

    partial_sum = scatter_low(low_in, node_rows)
    blk = adjacency.shape[1]
    parts = low.shape[0]
    ids = low_in[:, blk : blk + 4, :].astype(F32).reshape(parts // 8, 8, 4, blk).transpose(2, 0, 3, 1)
    own = own_term(at, in_hbm(feat_all), w_self, share)
    partial_sum, adjacency_t, ids, own = lax.optimization_barrier(
        (partial_sum, adjacency_t, ids, own)
    )
    neighbor_mean = scatter_high(low_in, high_in, ids, in_hbm(partial_sum), degrees)
    mean_pieces = swap(neighbor_mean.reshape(feat_size, share, feat_cols), "feat")
    back_pieces, hidden_pieces, grad_pre = dense(
        at, mean_pieces, in_hbm(own), in_hbm(cot_all), in_hbm(w_neigh), degrees
    )
    back_rows = swap(back_pieces, "feat").reshape(node_rows, feat_cols)
    back_rows, grad_pre, hidden_pieces = lax.optimization_barrier(
        (back_rows, grad_pre, hidden_pieces)
    )
    rows_low = gather_rows(0, ids, back_rows)
    rows_high = gather_rows(1, ids, back_rows)
    back_low = swap(rows_low, graph)
    grad_full = lax.all_gather(grad_pre, "feat", axis=0, tiled=True)
    grad_full = after(grad_full, rows_high)
    both = jnp.concatenate([features, neighbor_mean], axis=1)
    weight_part = lax.dot_general(
        both, grad_full, (((0,), (0,)), ((), ())), preferred_element_type=F32
    ).astype(BF16)
    over_y = lax.axis_size("y")
    part = weight_part.reshape(over_y, 2 * feat_cols // over_y, weight_part.shape[1])
    part = scatter_sum(part, "y")
    back_high = swap(after(rows_high, weight_part, back_low), graph)

    hidden_all = lax.all_gather(after(hidden_pieces, rows_low), "feat", axis=0)
    hidden_out = lax.dynamic_index_in_dim(hidden_all, feat_at, 1, keepdims=False)
    hidden_out = hidden_out.reshape(node_rows, feat_cols)
    self_grad = lax.dot_general(
        grad_full, self_rows, (((1,), (1,)), ((), ())), preferred_element_type=F32
    )
    part = after(quad_sum(part, "z"), self_grad)
    grad_features = backward_blocks(
        in_hbm(block_source),
        in_hbm(block_to_slot),
        back_low,
        back_high,
        adjacency_t,
        self_grad,
    )
    part = exchange_sum(part, "z", 4, grad_features)
    at = after(jnp.full((1,), lax.axis_index("y"), jnp.int32), hidden_out)
    grad_self, grad_neigh = assemble(at, around(part, "y"))
    return hidden_out, grad_features, grad_self, grad_neigh


def solution(mesh):
    split = Mesh(mesh.devices.reshape(8, 4, 8), ("z", "y", "feat"))
    graph = ("z", "y")
    placed = (
        P(graph, "feat"),
        P(),
        P(),
        P(graph, None, None),
        P(graph),
        P(graph),
        P(graph, None, None),
        P(graph, None),
        P(graph),
        P(graph, "feat"),
    )
    return jax.shard_map(
        on_device,
        mesh=split,
        in_specs=placed,
        out_specs=(P(graph, "feat"), P(graph, "feat"), P("feat", None), P("feat", None)),
        check_vma=False,
    )
```

```python
import functools

import jax
import jax.numpy as jnp
from jax import lax
from jax.experimental import pallas as pl
from jax.experimental.pallas import tpu as pltpu
from jax.sharding import Mesh, PartitionSpec as P

BF16 = jnp.bfloat16
F32 = jnp.float32
VMEM_BYTES = 20 * 1024 * 1024
ID_ROWS = 8


def params(axes=0):
    return pltpu.CompilerParams(
        dimension_semantics=("arbitrary",) * axes if axes else None, vmem_limit_bytes=VMEM_BYTES
    )


def full_spec(shape):
    return pl.BlockSpec(shape, lambda *unused: (0,) * len(shape))


def forward_blocks_kernel(
    source_ref, slot_ref, count_ref, rows_ref, feat_ref, adj_ref, low_ref, high_ref, sums_ref
):
    step = pl.program_id(0)
    chunk, blk, _ = adj_ref.shape
    parts = low_ref.shape[0]
    cols = feat_ref.shape[1]

    @pl.when(step == 0)
    def _():
        sums_ref[...] = jnp.zeros(sums_ref.shape, F32)

    for item in range(chunk):
        block = step * chunk + item
        start = pl.multiple_of(source_ref[block] * blk, blk)
        product = jnp.dot(
            adj_ref[item], feat_ref[pl.ds(start, blk), :], preferred_element_type=F32
        )
        sums_ref[slot_ref[block]] += product

    @pl.when(step == pl.num_programs(0) - 1)
    def _():
        slot_row = lax.broadcasted_iota(jnp.int32, (blk, cols), 0)
        lane = lax.broadcasted_iota(jnp.int32, (1, 2 * blk), 1)
        tile_row = lax.broadcasted_iota(jnp.int32, (ID_ROWS, blk), 0)

        def emit(part, carry):
            count = count_ref[part]
            low = jnp.where(slot_row < count, sums_ref[2 * part], 0.0)
            high = jnp.where(slot_row + blk < count, sums_ref[2 * part + 1], 0.0)
            low_ref[part, 0:blk, :] = low.astype(BF16)
            high_ref[part] = high.astype(BF16)
            ids = rows_ref[pl.ds(part, 1), :]
            live = lane < count
            fine = jnp.where(live, ids & (blk - 1), -1).astype(F32)
            coarse = jnp.where(live, ids >> 7, -1).astype(F32)
            tile = jnp.where(tile_row == 0, fine[:, :blk], 0.0)
            tile = jnp.where(tile_row == 1, fine[:, blk:], tile)
            tile = jnp.where(tile_row == 2, coarse[:, :blk], tile)
            tile = jnp.where(tile_row == 3, coarse[:, blk:], tile)
            low_ref[part, blk : blk + ID_ROWS, :] = tile.astype(BF16)
            return carry

        lax.fori_loop(0, parts, emit, 0, unroll=4)


def forward_blocks(block_source, block_to_slot, counts, rows, features, adjacency):
    blocks, blk, _ = adjacency.shape
    nodes, cols = features.shape
    parts, cap = rows.shape
    chunk = 64
    return pl.pallas_call(
        forward_blocks_kernel,
        grid_spec=pltpu.PrefetchScalarGridSpec(
            num_scalar_prefetch=3,
            grid=(blocks // chunk,),
            in_specs=[
                full_spec((parts, cap)),
                full_spec((nodes, cols)),
                pl.BlockSpec((chunk, blk, blk), lambda i, *unused: (i, 0, 0)),
            ],
            out_specs=[full_spec((parts, blk + ID_ROWS, cols)), full_spec((parts, blk, cols))],
            scratch_shapes=[pltpu.VMEM((parts * cap // blk, blk, cols), F32)],
        ),
        out_shape=[
            jax.ShapeDtypeStruct((parts, blk + ID_ROWS, cols), BF16),
            jax.ShapeDtypeStruct((parts, blk, cols), BF16),
        ],
        compiler_params=params(1),
        name="forward_blocks",
    )(block_source, block_to_slot, counts, rows, features, adjacency)


def scatter_body(half, ids_ref, rows_ref, hot_ref, acc_ref, group):
    nodes, cols = acc_ref.shape
    blk = 128
    node_row = lax.broadcasted_iota(jnp.int32, (blk, blk), 0).astype(F32)
    for part in range(group):
        tile = ids_ref[part].astype(F32)
        fine = tile[half : half + 1, :]
        coarse = tile[2 + half : 3 + half, :]
        hot = jnp.where(node_row == fine, 1.0, 0.0).astype(BF16)
        for block in range(nodes // blk):
            keep = jnp.where(coarse == float(block), 1.0, 0.0).astype(BF16)
            hot_ref[block * blk : (block + 1) * blk, part * blk : (part + 1) * blk] = hot * keep
    rows = rows_ref[...].reshape(group * blk, cols)
    acc_ref[...] += jnp.dot(hot_ref[...], rows, preferred_element_type=F32)


def scatter_low_kernel(payload_ids_ref, rows_ref, sum_ref, hot_ref):
    @pl.when(pl.program_id(0) == 0)
    def _():
        sum_ref[...] = jnp.zeros(sum_ref.shape, F32)

    scatter_body(0, payload_ids_ref, rows_ref, hot_ref, sum_ref, rows_ref.shape[0])


def scatter_high_kernel(
    ids_ref,
    rows_ref,
    coarse_ref,
    init_ref,
    degree_ref,
    mean_ref,
    hot_a_ref,
    hot_b_ref,
    both_a_ref,
    both_b_ref,
    acc_ref,
):
    blk, cols = rows_ref.shape[1:]
    groups, group = coarse_ref.shape[1], coarse_ref.shape[3]
    half_nodes = acc_ref.shape[0]
    half_blocks = half_nodes // blk
    acc_ref[:, :cols] = init_ref[:half_nodes]
    acc_ref[:, cols:] = init_ref[half_nodes:]
    node_row = lax.broadcasted_iota(jnp.int32, (blk, blk), 0).astype(F32)
    for at in range(groups):
        hot_ref = hot_b_ref if at % 2 else hot_a_ref
        both_ref = both_b_ref if at % 2 else both_a_ref
        for part in range(group):
            tile = ids_ref[at * group + part].astype(F32)
            fine = tile[1:2, :]
            coarse = tile[3:4, :]
            coarse = jnp.where(coarse >= half_blocks, coarse - half_blocks, coarse)
            hot = jnp.where(node_row == fine, 1.0, 0.0).astype(BF16)
            here = slice(part * blk, (part + 1) * blk)
            for block in range(half_blocks):
                keep = jnp.where(coarse == float(block), 1.0, 0.0).astype(BF16)
                hot_ref[block * blk : (block + 1) * blk, here] = hot * keep
            column = jnp.broadcast_to(coarse_ref[0, at, :, part : part + 1], (blk, cols))
            upper = jnp.where(column >= half_blocks, 1.0, 0.0).astype(BF16)
            rows = rows_ref[at * group + part]
            both_ref[here, cols:] = rows * upper
            both_ref[here, :cols] = rows * (1.0 - upper)
        acc_ref[...] += jnp.dot(hot_ref[...], both_ref[...], preferred_element_type=F32)
    mean_ref[:half_nodes] = (acc_ref[:, :cols] / degree_ref[:half_nodes]).astype(BF16)
    mean_ref[half_nodes:] = (acc_ref[:, cols:] / degree_ref[half_nodes:]).astype(BF16)


def scatter_low(low, nodes):
    parts, height, cols = low.shape
    group, blk = 8, 128
    return pl.pallas_call(
        scatter_low_kernel,
        grid=(parts // group,),
        in_specs=[
            pl.BlockSpec((group, ID_ROWS, cols), lambda i: (i, blk // ID_ROWS, 0)),
            pl.BlockSpec((group, blk, cols), lambda i: (i, 0, 0)),
        ],
        out_specs=full_spec((nodes, cols)),
        out_shape=pltpu.HBM((nodes, cols), F32),
        scratch_shapes=[pltpu.VMEM((nodes, group * blk), BF16)],
        compiler_params=params(1),
        name="scatter_low",
    )(low, low)


def scatter_high(low, high, columns, partial_sum, degrees):
    parts, blk, cols = high.shape
    nodes = partial_sum.shape[0]
    groups, group = columns.shape[1], columns.shape[3]
    return pl.pallas_call(
        scatter_high_kernel,
        grid=(1,),
        in_specs=[
            pl.BlockSpec((parts, ID_ROWS, cols), lambda i: (0, blk // ID_ROWS, 0)),
            full_spec((parts, blk, cols)),
            pl.BlockSpec((1, groups, blk, group), lambda i: (3, 0, 0, 0)),
            full_spec((nodes, cols)),
            full_spec((nodes, 1)),
        ],
        out_specs=full_spec((nodes, cols)),
        out_shape=pltpu.HBM((nodes, cols), BF16),
        scratch_shapes=[
            pltpu.VMEM((nodes // 2, group * blk), BF16),
            pltpu.VMEM((nodes // 2, group * blk), BF16),
            pltpu.VMEM((group * blk, 2 * cols), BF16),
            pltpu.VMEM((group * blk, 2 * cols), BF16),
            pltpu.VMEM((nodes // 2, 2 * cols), F32),
        ],
        compiler_params=params(1),
        name="scatter_high",
    )(low, high, columns, partial_sum, degrees)


def gather_kernel(fine_ref, coarse_ref, back_ref, out_ref, hot_a_ref, hot_b_ref):
    blk, cols = out_ref.shape[1:]
    groups, group = fine_ref.shape[1], fine_ref.shape[3]
    half_nodes = back_ref.shape[0] // 2
    half_blocks = half_nodes // blk
    lane = lax.broadcasted_iota(jnp.int32, (blk, blk), 1).astype(F32)
    both = jnp.concatenate([back_ref[:half_nodes], back_ref[half_nodes:]], axis=1)
    for at in range(groups):
        hot_ref = hot_b_ref if at % 2 else hot_a_ref
        for part in range(group):
            fine = jnp.broadcast_to(fine_ref[0, at, :, part : part + 1], (blk, blk))
            coarse = jnp.broadcast_to(coarse_ref[0, at, :, part : part + 1], (blk, blk))
            coarse = jnp.where(coarse >= half_blocks, coarse - half_blocks, coarse)
            hot = jnp.where(lane == fine, 1.0, 0.0).astype(BF16)
            coarse = coarse.astype(BF16)
            for block in range(half_blocks):
                value = jnp.where(coarse == BF16(block), hot, BF16(0))
                hot_ref[part * blk : (part + 1) * blk, block * blk : (block + 1) * blk] = value
        picked = jnp.dot(hot_ref[...], both, preferred_element_type=F32)
        for part in range(group):
            coarse = jnp.broadcast_to(coarse_ref[0, at, :, part : part + 1], (blk, cols))
            here = slice(part * blk, (part + 1) * blk)
            rows = jnp.where(coarse >= half_blocks, picked[here, cols:], picked[here, :cols])
            out_ref[at * group + part] = rows.astype(BF16)


def gather_rows(half, columns, back):
    _, groups, blk, group = columns.shape
    nodes, cols = back.shape
    return pl.pallas_call(
        gather_kernel,
        grid=(1,),
        in_specs=[
            pl.BlockSpec((1, groups, blk, group), lambda i: (half, 0, 0, 0)),
            pl.BlockSpec((1, groups, blk, group), lambda i: (2 + half, 0, 0, 0)),
            full_spec((nodes, cols)),
        ],
        out_specs=full_spec((groups * group, blk, cols)),
        out_shape=pltpu.HBM((groups * group, blk, cols), BF16),
        scratch_shapes=[
            pltpu.VMEM((group * blk, nodes // 2), BF16),
            pltpu.VMEM((group * blk, nodes // 2), BF16),
        ],
        compiler_params=params(1),
        name="gather_rows",
    )(columns, columns, back)


def own_term_kernel(at_ref, feat_ref, weight_ref, out_ref):
    pieces = feat_ref.shape[0]
    rows = jnp.concatenate([feat_ref[piece] for piece in range(pieces)], axis=1)
    out_ref[...] = jnp.dot(rows, weight_ref[...], preferred_element_type=F32)


def own_term(at, feat_all, w_self, share):
    pieces, _, cols = feat_all.shape
    wide = w_self.shape[1]
    tile = 256
    return pl.pallas_call(
        own_term_kernel,
        grid_spec=pltpu.PrefetchScalarGridSpec(
            num_scalar_prefetch=1,
            grid=(wide // tile,),
            in_specs=[
                pl.BlockSpec((pieces, share, cols), lambda i, at: (0, at[0], 0)),
                pl.BlockSpec((pieces * cols, tile), lambda i, at: (0, i)),
            ],
            out_specs=pl.BlockSpec((share, tile), lambda i, at: (0, i)),
        ),
        out_shape=pltpu.HBM((share, wide), F32),
        compiler_params=params(1),
        name="own_term",
    )(at, feat_all, w_self)


def dense_kernel(
    at_ref,
    mean_ref,
    own_ref,
    cot_ref,
    weight_ref,
    turned_ref,
    degree_ref,
    back_ref,
    hidden_ref,
    grad_ref,
    acc_ref,
):
    step = pl.program_id(0)
    pieces, rows, cols = mean_ref.shape
    tile = weight_ref.shape[1]
    mean = jnp.concatenate([mean_ref[piece] for piece in range(pieces)], axis=1)
    pre_act = own_ref[...] + jnp.dot(mean, weight_ref[...], preferred_element_type=F32)
    sig = jax.nn.sigmoid(pre_act)
    cot = jnp.concatenate([cot_ref[piece] for piece in range(cot_ref.shape[0])], axis=1)
    slope = sig * (1.0 + pre_act * (1.0 - sig))
    grad = (cot.astype(F32) * slope).astype(BF16)
    hidden = (pre_act * sig).astype(BF16)
    grad_ref[...] = grad
    for piece in range(tile // cols):
        hidden_ref[piece] = hidden[:, piece * cols : (piece + 1) * cols]
    update = jnp.dot(grad, turned_ref[...], preferred_element_type=F32)

    @pl.when(step == 0)
    def _():
        acc_ref[...] = update

    @pl.when(step > 0)
    def _():
        acc_ref[...] += update

    @pl.when(step == pl.num_programs(0) - 1)
    def _():
        back = (acc_ref[...] / degree_ref[...]).astype(BF16)
        for piece in range(pieces):
            back_ref[piece] = back[:, piece * cols : (piece + 1) * cols]


def dense(at, mean_pieces, own, cot_all, w_neigh, w_neigh_t, degrees):
    pieces, rows, cols = mean_pieces.shape
    wide = w_neigh.shape[1]
    tile = 256
    per = tile // cols
    return pl.pallas_call(
        dense_kernel,
        grid_spec=pltpu.PrefetchScalarGridSpec(
            num_scalar_prefetch=1,
            grid=(wide // tile,),
            in_specs=[
                full_spec((pieces, rows, cols)),
                pl.BlockSpec((rows, tile), lambda i, at: (0, i)),
                pl.BlockSpec((per, rows, cols), lambda i, at: (i, at[0], 0)),
                pl.BlockSpec((pieces * cols, tile), lambda i, at: (0, i)),
                pl.BlockSpec((tile, pieces * cols), lambda i, at: (i, 0)),
                pl.BlockSpec((rows, 1), lambda i, at: (at[0], 0)),
            ],
            out_specs=[
                full_spec((pieces, rows, cols)),
                pl.BlockSpec((per, rows, cols), lambda i, at: (i, 0, 0)),
                pl.BlockSpec((rows, tile), lambda i, at: (0, i)),
            ],
            scratch_shapes=[pltpu.VMEM((rows, wide), F32)],
        ),
        out_shape=[
            jax.ShapeDtypeStruct((pieces, rows, cols), BF16),
            jax.ShapeDtypeStruct((pieces, rows, cols), BF16),
            jax.ShapeDtypeStruct((rows, wide), BF16),
        ],
        compiler_params=params(1),
        name="dense",
    )(at, mean_pieces, own, cot_all, w_neigh, w_neigh_t, degrees)


def backward_blocks_kernel(
    source_ref, slot_ref, low_ref, high_ref, adj_ref, self_ref, out_ref, both_ref, acc_ref
):
    step = pl.program_id(0)
    chunk, blk, _ = adj_ref.shape
    parts = low_ref.shape[0]

    @pl.when(step == 0)
    def _():
        acc_ref[...] = self_ref[...]
        for part in range(parts):
            both_ref[2 * part] = low_ref[part]
            both_ref[2 * part + 1] = high_ref[part]

    for item in range(chunk):
        block = step * chunk + item
        start = pl.multiple_of(source_ref[block] * blk, blk)
        product = jnp.dot(
            adj_ref[item], both_ref[slot_ref[block]], preferred_element_type=F32
        )
        acc_ref[pl.ds(start, blk), :] += product

    @pl.when(step == pl.num_programs(0) - 1)
    def _():
        out_ref[...] = acc_ref[...].astype(BF16)


def backward_blocks(block_source, block_to_slot, low, high, adjacency_t, self_grad):
    blocks, blk, _ = adjacency_t.shape
    nodes, cols = self_grad.shape
    parts = low.shape[0]
    chunk = 64
    return pl.pallas_call(
        backward_blocks_kernel,
        grid_spec=pltpu.PrefetchScalarGridSpec(
            num_scalar_prefetch=2,
            grid=(blocks // chunk,),
            in_specs=[
                full_spec((parts, blk, cols)),
                full_spec((parts, blk, cols)),
                pl.BlockSpec((chunk, blk, blk), lambda i, *unused: (i, 0, 0)),
                full_spec((nodes, cols)),
            ],
            out_specs=full_spec((nodes, cols)),
            scratch_shapes=[
                pltpu.VMEM((2 * parts, blk, cols), BF16),
                pltpu.VMEM((nodes, cols), F32),
            ],
        ),
        out_shape=jax.ShapeDtypeStruct((nodes, cols), BF16),
        compiler_params=params(1),
        name="backward_blocks",
    )(block_source, block_to_slot, low, high, adjacency_t, self_grad)


def in_hbm(value):
    return pltpu.with_memory_space_constraint(value, pltpu.HBM)


def swap(value, axis):
    return lax.all_to_all(value, axis, split_axis=0, concat_axis=0, tiled=True)


def after(value, *others):
    return lax.optimization_barrier((value, *others))[0]


def rotate(value, axis, distance):
    size = lax.axis_size(axis)
    return lax.ppermute(value, axis, [(i, (i + distance) % size) for i in range(size)])


def scatter_sum(pieces, axis):
    size, at = lax.axis_size(axis), lax.axis_index(axis)
    take = functools.partial(lax.dynamic_index_in_dim, pieces, axis=0, keepdims=False)
    total = take(at).astype(F32)
    came = [rotate(take((at + d) % size), axis, d) for d in range(1, size)]
    for piece in came:
        total = total + piece.astype(F32)
    return total.astype(BF16)


def quad_sum(value, axis):
    size = lax.axis_size(axis)
    one, two, three = (
        lax.ppermute(value, axis, [(i, i ^ d) for i in range(size)]).astype(F32)
        for d in (1, 2, 3)
    )
    return ((value.astype(F32) + one) + (two + three)).astype(BF16)


def around(piece, axis):
    size = lax.axis_size(axis)
    return [piece] + [rotate(piece, axis, size - i) for i in range(1, size)]


def exchange_sum(value, axis, distance, *beside):
    size = lax.axis_size(axis)
    other = lax.ppermute(value, axis, [(i, i ^ distance) for i in range(size)])
    other = after(other, *beside)
    return (value.astype(F32) + other.astype(F32)).astype(BF16)


def assemble_kernel(at_ref, *refs):
    *piece_refs, first_ref, second_ref = refs
    size = len(piece_refs)
    half = size // 2
    for i, piece_ref in enumerate(piece_refs):
        place = (at_ref[0] + i) % size
        value = piece_ref[...].astype(F32)

        @pl.when(place < half)
        def _():
            first_ref[place] = value

        @pl.when(place >= half)
        def _():
            second_ref[place - half] = value


def assemble(at, pieces):
    rows, wide = pieces[0].shape
    half = len(pieces) // 2
    first, second = pl.pallas_call(
        assemble_kernel,
        grid_spec=pltpu.PrefetchScalarGridSpec(
            num_scalar_prefetch=1,
            grid=(1,),
            in_specs=[full_spec((rows, wide))] * len(pieces),
            out_specs=[full_spec((half, rows, wide))] * 2,
        ),
        out_shape=[jax.ShapeDtypeStruct((half, rows, wide), F32)] * 2,
        compiler_params=params(1),
        name="assemble",
    )(at, *pieces)
    return first.reshape(half * rows, wide), second.reshape(half * rows, wide)


def on_device(
    features,
    w_self,
    w_neigh,
    adjacency,
    block_source,
    block_to_slot,
    send_rows,
    send_counts,
    degree,
    cotangent,
):
    node_rows, feat_cols = features.shape
    feat_size = lax.axis_size("feat")
    feat_at = lax.axis_index("feat")
    at = jnp.full((1,), feat_at, jnp.int32)
    share = node_rows // feat_size
    graph = ("z", "y")
    low, high = forward_blocks(
        in_hbm(block_source),
        in_hbm(block_to_slot),
        in_hbm(send_counts[0]),
        in_hbm(send_rows[0]),
        in_hbm(features),
        in_hbm(adjacency),
    )
    low_in = swap(low, graph)
    high_in = swap(high, graph)
    feat_all = lax.all_gather(features, "feat", axis=0)
    cot_all = lax.all_gather(after(cotangent, low_in), "feat", axis=0)
    degrees = degree.astype(F32)[:, None]
    adjacency_t = in_hbm(after(adjacency, low_in).swapaxes(1, 2))
    self_rows = lax.dynamic_slice_in_dim(w_self, feat_at * feat_cols, feat_cols, 0)

    partial_sum = scatter_low(low_in, node_rows)
    blk = adjacency.shape[1]
    parts = low.shape[0]
    ids = low_in[:, blk : blk + 4, :].astype(F32).reshape(parts // 8, 8, 4, blk).transpose(2, 0, 3, 1)
    own = own_term(at, in_hbm(feat_all), w_self, share)
    w_neigh_t = in_hbm(after(w_neigh, low_in).T)
    partial_sum, adjacency_t, ids, own, w_neigh_t = lax.optimization_barrier(
        (partial_sum, adjacency_t, ids, own, w_neigh_t)
    )
    neighbor_mean = scatter_high(low_in, high_in, ids, in_hbm(partial_sum), degrees)
    mean_pieces = swap(neighbor_mean.reshape(feat_size, share, feat_cols), "feat")
    back_pieces, hidden_pieces, grad_pre = dense(
        at, mean_pieces, in_hbm(own), in_hbm(cot_all), in_hbm(w_neigh), w_neigh_t, degrees
    )
    back_rows = swap(back_pieces, "feat").reshape(node_rows, feat_cols)
    back_rows, grad_pre, hidden_pieces = lax.optimization_barrier(
        (back_rows, grad_pre, hidden_pieces)
    )
    rows_low = gather_rows(0, ids, back_rows)
    rows_high = gather_rows(1, ids, back_rows)
    back_low = swap(rows_low, graph)
    grad_full = lax.all_gather(grad_pre, "feat", axis=0, tiled=True)
    grad_full = after(grad_full, rows_high)
    both = jnp.concatenate([features, neighbor_mean], axis=1)
    weight_part = lax.dot_general(
        both, grad_full, (((0,), (0,)), ((), ())), preferred_element_type=F32
    ).astype(BF16)
    over_y = lax.axis_size("y")
    part = weight_part.reshape(over_y, 2 * feat_cols // over_y, weight_part.shape[1])
    part = scatter_sum(part, "y")
    back_high = swap(after(rows_high, weight_part, back_low), graph)

    hidden_all = lax.all_gather(after(hidden_pieces, rows_low), "feat", axis=0)
    hidden_out = lax.dynamic_index_in_dim(hidden_all, feat_at, 1, keepdims=False)
    hidden_out = hidden_out.reshape(node_rows, feat_cols)
    self_grad = lax.dot_general(
        grad_full, self_rows, (((1,), (1,)), ((), ())), preferred_element_type=F32
    )
    part = after(quad_sum(part, "z"), self_grad)
    grad_features = backward_blocks(
        in_hbm(block_source),
        in_hbm(block_to_slot),
        back_low,
        back_high,
        adjacency_t,
        self_grad,
    )
    part = exchange_sum(part, "z", 4, grad_features)
    at = after(jnp.full((1,), lax.axis_index("y"), jnp.int32), hidden_out)
    grad_self, grad_neigh = assemble(at, around(part, "y"))
    return hidden_out, grad_features, grad_self, grad_neigh


def solution(mesh):
    split = Mesh(mesh.devices.reshape(8, 4, 8), ("z", "y", "feat"))
    graph = ("z", "y")
    placed = (
        P(graph, "feat"),
        P(),
        P(),
        P(graph, None, None),
        P(graph),
        P(graph),
        P(graph, None, None),
        P(graph, None),
        P(graph),
        P(graph, "feat"),
    )
    return jax.shard_map(
        on_device,
        mesh=split,
        in_specs=placed,
        out_specs=(P(graph, "feat"), P(graph, "feat"), P("feat", None), P("feat", None)),
        check_vma=False,
    )
```

```python
import functools

import jax
import jax.numpy as jnp
from jax import lax
from jax.experimental import pallas as pl
from jax.experimental.pallas import tpu as pltpu
from jax.sharding import Mesh, PartitionSpec as P

BF16 = jnp.bfloat16
F32 = jnp.float32
VMEM_BYTES = 20 * 1024 * 1024
ID_ROWS = 8


def params(axes=0):
    return pltpu.CompilerParams(
        dimension_semantics=("arbitrary",) * axes if axes else None, vmem_limit_bytes=VMEM_BYTES
    )


def full_spec(shape):
    return pl.BlockSpec(shape, lambda *unused: (0,) * len(shape))


def forward_blocks_kernel(
    source_ref, slot_ref, count_ref, rows_ref, feat_ref, adj_ref, low_ref, high_ref, sums_ref
):
    step = pl.program_id(0)
    chunk, blk, _ = adj_ref.shape
    parts = low_ref.shape[0]
    cols = feat_ref.shape[1]

    @pl.when(step == 0)
    def _():
        sums_ref[...] = jnp.zeros(sums_ref.shape, F32)

    for item in range(chunk):
        block = step * chunk + item
        start = pl.multiple_of(source_ref[block] * blk, blk)
        product = jnp.dot(
            adj_ref[item], feat_ref[pl.ds(start, blk), :], preferred_element_type=F32
        )
        sums_ref[slot_ref[block]] += product

    @pl.when(step == pl.num_programs(0) - 1)
    def _():
        slot_row = lax.broadcasted_iota(jnp.int32, (blk, cols), 0)
        lane = lax.broadcasted_iota(jnp.int32, (1, 2 * blk), 1)
        tile_row = lax.broadcasted_iota(jnp.int32, (ID_ROWS, blk), 0)

        def emit(part, carry):
            count = count_ref[part]
            low = jnp.where(slot_row < count, sums_ref[2 * part], 0.0)
            high = jnp.where(slot_row + blk < count, sums_ref[2 * part + 1], 0.0)
            low_ref[part, 0:blk, :] = low.astype(BF16)
            high_ref[part] = high.astype(BF16)
            ids = rows_ref[pl.ds(part, 1), :]
            live = lane < count
            fine = jnp.where(live, ids & (blk - 1), -1).astype(F32)
            coarse = jnp.where(live, ids >> 7, -1).astype(F32)
            tile = jnp.where(tile_row == 0, fine[:, :blk], 0.0)
            tile = jnp.where(tile_row == 1, fine[:, blk:], tile)
            tile = jnp.where(tile_row == 2, coarse[:, :blk], tile)
            tile = jnp.where(tile_row == 3, coarse[:, blk:], tile)
            low_ref[part, blk : blk + ID_ROWS, :] = tile.astype(BF16)
            return carry

        lax.fori_loop(0, parts, emit, 0, unroll=4)


def forward_blocks(block_source, block_to_slot, counts, rows, features, adjacency):
    blocks, blk, _ = adjacency.shape
    nodes, cols = features.shape
    parts, cap = rows.shape
    chunk = 64
    return pl.pallas_call(
        forward_blocks_kernel,
        grid_spec=pltpu.PrefetchScalarGridSpec(
            num_scalar_prefetch=3,
            grid=(blocks // chunk,),
            in_specs=[
                full_spec((parts, cap)),
                full_spec((nodes, cols)),
                pl.BlockSpec((chunk, blk, blk), lambda i, *unused: (i, 0, 0)),
            ],
            out_specs=[full_spec((parts, blk + ID_ROWS, cols)), full_spec((parts, blk, cols))],
            scratch_shapes=[pltpu.VMEM((parts * cap // blk, blk, cols), F32)],
        ),
        out_shape=[
            jax.ShapeDtypeStruct((parts, blk + ID_ROWS, cols), BF16),
            jax.ShapeDtypeStruct((parts, blk, cols), BF16),
        ],
        compiler_params=params(1),
        name="forward_blocks",
    )(block_source, block_to_slot, counts, rows, features, adjacency)


def scatter_body(half, ids_ref, rows_ref, hot_ref, acc_ref, group):
    nodes, cols = acc_ref.shape
    blk = 128
    node_row = lax.broadcasted_iota(jnp.int32, (blk, blk), 0).astype(F32)
    for part in range(group):
        tile = ids_ref[part].astype(F32)
        fine = tile[half : half + 1, :]
        coarse = tile[2 + half : 3 + half, :]
        hot = jnp.where(node_row == fine, 1.0, 0.0).astype(BF16)
        for block in range(nodes // blk):
            keep = jnp.where(coarse == float(block), 1.0, 0.0).astype(BF16)
            hot_ref[block * blk : (block + 1) * blk, part * blk : (part + 1) * blk] = hot * keep
    rows = rows_ref[...].reshape(group * blk, cols)
    acc_ref[...] += jnp.dot(hot_ref[...], rows, preferred_element_type=F32)


def scatter_low_kernel(payload_ids_ref, rows_ref, sum_ref, hot_ref):
    @pl.when(pl.program_id(0) == 0)
    def _():
        sum_ref[...] = jnp.zeros(sum_ref.shape, F32)

    scatter_body(0, payload_ids_ref, rows_ref, hot_ref, sum_ref, rows_ref.shape[0])


def scatter_high_kernel(
    ids_ref,
    rows_ref,
    coarse_ref,
    init_ref,
    degree_ref,
    mean_ref,
    hot_a_ref,
    hot_b_ref,
    both_a_ref,
    both_b_ref,
    acc_ref,
):
    blk, cols = rows_ref.shape[1:]
    groups, group = coarse_ref.shape[1], coarse_ref.shape[3]
    half_nodes = acc_ref.shape[0]
    half_blocks = half_nodes // blk
    acc_ref[:, :cols] = init_ref[:half_nodes]
    acc_ref[:, cols:] = init_ref[half_nodes:]
    node_row = lax.broadcasted_iota(jnp.int32, (blk, blk), 0).astype(F32)
    for at in range(groups):
        hot_ref = hot_b_ref if at % 2 else hot_a_ref
        both_ref = both_b_ref if at % 2 else both_a_ref
        for part in range(group):
            tile = ids_ref[at * group + part].astype(F32)
            fine = tile[1:2, :]
            coarse = tile[3:4, :]
            coarse = jnp.where(coarse >= half_blocks, coarse - half_blocks, coarse)
            hot = jnp.where(node_row == fine, 1.0, 0.0).astype(BF16)
            here = slice(part * blk, (part + 1) * blk)
            for block in range(half_blocks):
                keep = jnp.where(coarse == float(block), 1.0, 0.0).astype(BF16)
                hot_ref[block * blk : (block + 1) * blk, here] = hot * keep
            column = jnp.broadcast_to(coarse_ref[0, at, :, part : part + 1], (blk, cols))
            upper = jnp.where(column >= half_blocks, 1.0, 0.0).astype(BF16)
            rows = rows_ref[at * group + part]
            both_ref[here, cols:] = rows * upper
            both_ref[here, :cols] = rows * (1.0 - upper)
        acc_ref[...] += jnp.dot(hot_ref[...], both_ref[...], preferred_element_type=F32)
    mean_ref[:half_nodes] = (acc_ref[:, :cols] / degree_ref[:half_nodes]).astype(BF16)
    mean_ref[half_nodes:] = (acc_ref[:, cols:] / degree_ref[half_nodes:]).astype(BF16)


def scatter_low(low, nodes):
    parts, height, cols = low.shape
    group, blk = 8, 128
    return pl.pallas_call(
        scatter_low_kernel,
        grid=(parts // group,),
        in_specs=[
            pl.BlockSpec((group, ID_ROWS, cols), lambda i: (i, blk // ID_ROWS, 0)),
            pl.BlockSpec((group, blk, cols), lambda i: (i, 0, 0)),
        ],
        out_specs=full_spec((nodes, cols)),
        out_shape=pltpu.HBM((nodes, cols), F32),
        scratch_shapes=[pltpu.VMEM((nodes, group * blk), BF16)],
        compiler_params=params(1),
        name="scatter_low",
    )(low, low)


def scatter_high(low, high, columns, partial_sum, degrees):
    parts, blk, cols = high.shape
    nodes = partial_sum.shape[0]
    groups, group = columns.shape[1], columns.shape[3]
    return pl.pallas_call(
        scatter_high_kernel,
        grid=(1,),
        in_specs=[
            pl.BlockSpec((parts, ID_ROWS, cols), lambda i: (0, blk // ID_ROWS, 0)),
            full_spec((parts, blk, cols)),
            pl.BlockSpec((1, groups, blk, group), lambda i: (3, 0, 0, 0)),
            full_spec((nodes, cols)),
            full_spec((nodes, 1)),
        ],
        out_specs=full_spec((nodes, cols)),
        out_shape=pltpu.HBM((nodes, cols), BF16),
        scratch_shapes=[
            pltpu.VMEM((nodes // 2, group * blk), BF16),
            pltpu.VMEM((nodes // 2, group * blk), BF16),
            pltpu.VMEM((group * blk, 2 * cols), BF16),
            pltpu.VMEM((group * blk, 2 * cols), BF16),
            pltpu.VMEM((nodes // 2, 2 * cols), F32),
        ],
        compiler_params=params(1),
        name="scatter_high",
    )(low, high, columns, partial_sum, degrees)


def gather_kernel(fine_ref, coarse_ref, back_ref, out_ref, hot_a_ref, hot_b_ref):
    blk, cols = out_ref.shape[1:]
    groups, group = fine_ref.shape[1], fine_ref.shape[3]
    half_nodes = back_ref.shape[0] // 2
    half_blocks = half_nodes // blk
    lane = lax.broadcasted_iota(jnp.int32, (blk, blk), 1).astype(F32)
    both = jnp.concatenate([back_ref[:half_nodes], back_ref[half_nodes:]], axis=1)
    for at in range(groups):
        hot_ref = hot_b_ref if at % 2 else hot_a_ref
        for part in range(group):
            fine = jnp.broadcast_to(fine_ref[0, at, :, part : part + 1], (blk, blk))
            coarse = jnp.broadcast_to(coarse_ref[0, at, :, part : part + 1], (blk, blk))
            coarse = jnp.where(coarse >= half_blocks, coarse - half_blocks, coarse)
            hot = jnp.where(lane == fine, 1.0, 0.0).astype(BF16)
            coarse = coarse.astype(BF16)
            for block in range(half_blocks):
                value = jnp.where(coarse == BF16(block), hot, BF16(0))
                hot_ref[part * blk : (part + 1) * blk, block * blk : (block + 1) * blk] = value
        picked = jnp.dot(hot_ref[...], both, preferred_element_type=F32)
        for part in range(group):
            coarse = jnp.broadcast_to(coarse_ref[0, at, :, part : part + 1], (blk, cols))
            here = slice(part * blk, (part + 1) * blk)
            rows = jnp.where(coarse >= half_blocks, picked[here, cols:], picked[here, :cols])
            out_ref[at * group + part] = rows.astype(BF16)


def gather_rows(half, columns, back):
    _, groups, blk, group = columns.shape
    nodes, cols = back.shape
    return pl.pallas_call(
        gather_kernel,
        grid=(1,),
        in_specs=[
            pl.BlockSpec((1, groups, blk, group), lambda i: (half, 0, 0, 0)),
            pl.BlockSpec((1, groups, blk, group), lambda i: (2 + half, 0, 0, 0)),
            full_spec((nodes, cols)),
        ],
        out_specs=full_spec((groups * group, blk, cols)),
        out_shape=pltpu.HBM((groups * group, blk, cols), BF16),
        scratch_shapes=[
            pltpu.VMEM((group * blk, nodes // 2), BF16),
            pltpu.VMEM((group * blk, nodes // 2), BF16),
        ],
        compiler_params=params(1),
        name="gather_rows",
    )(columns, columns, back)


def own_term_kernel(at_ref, feat_ref, weight_ref, out_ref):
    pieces = feat_ref.shape[0]
    rows = jnp.concatenate([feat_ref[piece] for piece in range(pieces)], axis=1)
    out_ref[...] = jnp.dot(rows, weight_ref[...], preferred_element_type=F32)


def own_term(at, feat_all, w_self, share):
    pieces, _, cols = feat_all.shape
    wide = w_self.shape[1]
    tile = 256
    return pl.pallas_call(
        own_term_kernel,
        grid_spec=pltpu.PrefetchScalarGridSpec(
            num_scalar_prefetch=1,
            grid=(wide // tile,),
            in_specs=[
                pl.BlockSpec((pieces, share, cols), lambda i, at: (0, at[0], 0)),
                pl.BlockSpec((pieces * cols, tile), lambda i, at: (0, i)),
            ],
            out_specs=pl.BlockSpec((share, tile), lambda i, at: (0, i)),
        ),
        out_shape=pltpu.HBM((share, wide), F32),
        compiler_params=params(1),
        name="own_term",
    )(at, feat_all, w_self)


def dense_kernel(
    at_ref, mean_ref, own_ref, cot_ref, weight_ref, degree_ref, back_ref, hidden_ref, grad_ref, acc_ref
):
    step = pl.program_id(0)
    pieces, rows, cols = mean_ref.shape
    tile = weight_ref.shape[1]
    mean = jnp.concatenate([mean_ref[piece] for piece in range(pieces)], axis=1)
    pre_act = own_ref[...] + jnp.dot(mean, weight_ref[...], preferred_element_type=F32)
    sig = jax.nn.sigmoid(pre_act)
    cot = jnp.concatenate([cot_ref[piece] for piece in range(cot_ref.shape[0])], axis=1)
    slope = sig * (1.0 + pre_act * (1.0 - sig))
    grad = (cot.astype(F32) * slope).astype(BF16)
    hidden = (pre_act * sig).astype(BF16)
    grad_ref[...] = grad
    for piece in range(tile // cols):
        hidden_ref[piece] = hidden[:, piece * cols : (piece + 1) * cols]
    update = lax.dot_general(
        grad, weight_ref[...], (((1,), (1,)), ((), ())), preferred_element_type=F32
    )

    @pl.when(step == 0)
    def _():
        acc_ref[...] = update

    @pl.when(step > 0)
    def _():
        acc_ref[...] += update

    @pl.when(step == pl.num_programs(0) - 1)
    def _():
        back = (acc_ref[...] / degree_ref[...]).astype(BF16)
        for piece in range(pieces):
            back_ref[piece] = back[:, piece * cols : (piece + 1) * cols]


def dense(at, mean_pieces, own, cot_all, w_neigh, degrees):
    pieces, rows, cols = mean_pieces.shape
    wide = w_neigh.shape[1]
    tile = 256
    per = tile // cols
    return pl.pallas_call(
        dense_kernel,
        grid_spec=pltpu.PrefetchScalarGridSpec(
            num_scalar_prefetch=1,
            grid=(wide // tile,),
            in_specs=[
                full_spec((pieces, rows, cols)),
                pl.BlockSpec((rows, tile), lambda i, at: (0, i)),
                pl.BlockSpec((per, rows, cols), lambda i, at: (i, at[0], 0)),
                pl.BlockSpec((pieces * cols, tile), lambda i, at: (0, i)),
                pl.BlockSpec((rows, 1), lambda i, at: (at[0], 0)),
            ],
            out_specs=[
                full_spec((pieces, rows, cols)),
                pl.BlockSpec((per, rows, cols), lambda i, at: (i, 0, 0)),
                pl.BlockSpec((rows, tile), lambda i, at: (0, i)),
            ],
            scratch_shapes=[pltpu.VMEM((rows, wide), F32)],
        ),
        out_shape=[
            jax.ShapeDtypeStruct((pieces, rows, cols), BF16),
            jax.ShapeDtypeStruct((pieces, rows, cols), BF16),
            jax.ShapeDtypeStruct((rows, wide), BF16),
        ],
        compiler_params=params(1),
        name="dense",
    )(at, mean_pieces, own, cot_all, w_neigh, degrees)


def backward_blocks_kernel(
    source_ref, slot_ref, low_ref, high_ref, adj_ref, self_ref, out_ref, both_ref, acc_ref
):
    step = pl.program_id(0)
    chunk, blk, _ = adj_ref.shape
    parts = low_ref.shape[0]

    @pl.when(step == 0)
    def _():
        acc_ref[...] = self_ref[...]
        for part in range(parts):
            both_ref[2 * part] = low_ref[part]
            both_ref[2 * part + 1] = high_ref[part]

    for item in range(chunk):
        block = step * chunk + item
        start = pl.multiple_of(source_ref[block] * blk, blk)
        product = jnp.dot(
            adj_ref[item], both_ref[slot_ref[block]], preferred_element_type=F32
        )
        acc_ref[pl.ds(start, blk), :] += product

    @pl.when(step == pl.num_programs(0) - 1)
    def _():
        out_ref[...] = acc_ref[...].astype(BF16)


def backward_blocks(block_source, block_to_slot, low, high, adjacency_t, self_grad):
    blocks, blk, _ = adjacency_t.shape
    nodes, cols = self_grad.shape
    parts = low.shape[0]
    chunk = 64
    return pl.pallas_call(
        backward_blocks_kernel,
        grid_spec=pltpu.PrefetchScalarGridSpec(
            num_scalar_prefetch=2,
            grid=(blocks // chunk,),
            in_specs=[
                full_spec((parts, blk, cols)),
                full_spec((parts, blk, cols)),
                pl.BlockSpec((chunk, blk, blk), lambda i, *unused: (i, 0, 0)),
                full_spec((nodes, cols)),
            ],
            out_specs=full_spec((nodes, cols)),
            scratch_shapes=[
                pltpu.VMEM((2 * parts, blk, cols), BF16),
                pltpu.VMEM((nodes, cols), F32),
            ],
        ),
        out_shape=jax.ShapeDtypeStruct((nodes, cols), BF16),
        compiler_params=params(1),
        name="backward_blocks",
    )(block_source, block_to_slot, low, high, adjacency_t, self_grad)


def in_hbm(value):
    return pltpu.with_memory_space_constraint(value, pltpu.HBM)


def swap(value, axis):
    return lax.all_to_all(value, axis, split_axis=0, concat_axis=0, tiled=True)


def after(value, *others):
    return lax.optimization_barrier((value, *others))[0]


def rotate(value, axis, distance):
    size = lax.axis_size(axis)
    return lax.ppermute(value, axis, [(i, (i + distance) % size) for i in range(size)])


def scatter_sum(pieces, axis):
    size, at = lax.axis_size(axis), lax.axis_index(axis)
    take = functools.partial(lax.dynamic_index_in_dim, pieces, axis=0, keepdims=False)
    total = take(at).astype(F32)
    came = [rotate(take((at + d) % size), axis, d) for d in range(1, size)]
    for piece in came:
        total = total + piece.astype(F32)
    return total.astype(BF16)


def quad_sum(value, axis):
    size = lax.axis_size(axis)
    one, two, three = (
        lax.ppermute(value, axis, [(i, i ^ d) for i in range(size)]).astype(F32)
        for d in (1, 2, 3)
    )
    return ((value.astype(F32) + one) + (two + three)).astype(BF16)


def quad_sum(value, axis):
    size = lax.axis_size(axis)
    one, two, three = (
        lax.ppermute(value, axis, [(i, i ^ d) for i in range(size)]).astype(F32)
        for d in (1, 2, 3)
    )
    return ((value.astype(F32) + one) + (two + three)).astype(BF16)


def around(piece, axis):
    size = lax.axis_size(axis)
    return [piece] + [rotate(piece, axis, size - i) for i in range(1, size)]


def exchange_sum(value, axis, distance, *beside):
    size = lax.axis_size(axis)
    other = lax.ppermute(value, axis, [(i, i ^ distance) for i in range(size)])
    other = after(other, *beside)
    return (value.astype(F32) + other.astype(F32)).astype(BF16)


def on_device(
    features,
    w_self,
    w_neigh,
    adjacency,
    block_source,
    block_to_slot,
    send_rows,
    send_counts,
    degree,
    cotangent,
):
    node_rows, feat_cols = features.shape
    feat_size = lax.axis_size("feat")
    feat_at = lax.axis_index("feat")
    at = jnp.full((1,), feat_at, jnp.int32)
    share = node_rows // feat_size
    graph = ("z", "y")
    low, high = forward_blocks(
        in_hbm(block_source),
        in_hbm(block_to_slot),
        in_hbm(send_counts[0]),
        in_hbm(send_rows[0]),
        in_hbm(features),
        in_hbm(adjacency),
    )
    low_in = swap(low, graph)
    high_in = swap(high, graph)
    feat_all = lax.all_gather(features, "feat", axis=0)
    cot_all = lax.all_gather(after(cotangent, low_in), "feat", axis=0)
    degrees = degree.astype(F32)[:, None]
    adjacency_t = in_hbm(after(adjacency, low_in).swapaxes(1, 2))
    self_rows = lax.dynamic_slice_in_dim(w_self, feat_at * feat_cols, feat_cols, 0)

    partial_sum = scatter_low(low_in, node_rows)
    blk = adjacency.shape[1]
    parts = low.shape[0]
    ids = low_in[:, blk : blk + 4, :].astype(F32).reshape(parts // 8, 8, 4, blk).transpose(2, 0, 3, 1)
    own = own_term(at, in_hbm(feat_all), w_self, share)
    partial_sum, adjacency_t, ids, own = lax.optimization_barrier(
        (partial_sum, adjacency_t, ids, own)
    )
    neighbor_mean = scatter_high(low_in, high_in, ids, in_hbm(partial_sum), degrees)
    mean_pieces = swap(neighbor_mean.reshape(feat_size, share, feat_cols), "feat")
    back_pieces, hidden_pieces, grad_pre = dense(
        at, mean_pieces, in_hbm(own), in_hbm(cot_all), in_hbm(w_neigh), degrees
    )
    back_rows = swap(back_pieces, "feat").reshape(node_rows, feat_cols)
    back_rows, grad_pre, hidden_pieces = lax.optimization_barrier(
        (back_rows, grad_pre, hidden_pieces)
    )
    rows_low = gather_rows(0, ids, back_rows)
    rows_high = gather_rows(1, ids, back_rows)
    back_low = swap(rows_low, graph)
    grad_full = lax.all_gather(grad_pre, "feat", axis=0, tiled=True)
    grad_full = after(grad_full, rows_high)
    both = jnp.concatenate([features, neighbor_mean], axis=1)
    weight_part = lax.dot_general(
        both, grad_full, (((0,), (0,)), ((), ())), preferred_element_type=F32
    ).astype(BF16)
    over_y = lax.axis_size("y")
    part = weight_part.reshape(over_y, 2 * feat_cols // over_y, weight_part.shape[1])
    part = scatter_sum(part, "y")
    back_high = swap(after(rows_high, weight_part, back_low), graph)

    hidden_all = lax.all_gather(after(hidden_pieces, rows_low), "feat", axis=0)
    hidden_out = lax.dynamic_index_in_dim(hidden_all, feat_at, 1, keepdims=False)
    hidden_out = hidden_out.reshape(node_rows, feat_cols)
    self_grad = lax.dot_general(
        grad_full, self_rows, (((1,), (1,)), ((), ())), preferred_element_type=F32
    )
    part = after(quad_sum(part, "z"), self_grad)
    grad_features = backward_blocks(
        in_hbm(block_source),
        in_hbm(block_to_slot),
        back_low,
        back_high,
        adjacency_t,
        self_grad,
    )
    part = exchange_sum(part, "z", 4, grad_features)
    spread = after(swap(jnp.broadcast_to(part[None], (over_y, *part.shape)), "y"), hidden_out)
    weight_grads = spread.reshape(2 * feat_cols, part.shape[1]).astype(F32)
    grad_self, grad_neigh = weight_grads[:feat_cols], weight_grads[feat_cols:]
    return hidden_out, grad_features, grad_self, grad_neigh


def solution(mesh):
    split = Mesh(mesh.devices.reshape(8, 4, 8), ("z", "y", "feat"))
    graph = ("z", "y")
    placed = (
        P(graph, "feat"),
        P(),
        P(),
        P(graph, None, None),
        P(graph),
        P(graph),
        P(graph, None, None),
        P(graph, None),
        P(graph),
        P(graph, "feat"),
    )
    return jax.shard_map(
        on_device,
        mesh=split,
        in_specs=placed,
        out_specs=(P(graph, "feat"), P(graph, "feat"), P("feat", None), P("feat", None)),
        check_vma=False,
    )
```
